32 devices in a mesh: gx: 8 (over z, y), gy: 4 (over x, core).
Axes of the slice: x: 2, y: 2, z: 4, core: 2. Of those that a mesh axis runs over, the one named last changes fastest.
Arguments:
- source_term: float32 [256, 128, 256], P('gx', 'gy'), may hold values from -6 to 6
- mobility_x: float32 [256, 128, 256], P('gx', 'gy'), may hold values from 0.001 to 1
- mobility_y: float32 [256, 128, 256], P('gx', 'gy'), may hold values from 0.001 to 1
- mobility_z: float32 [256, 128, 256], P('gx', 'gy'), may hold values from 0.001 to 1
- bubble_fraction: float32 [256, 128, 256], P('gx', 'gy'), may hold values from 0.1 to 1
- tile_labels: int32 [256, 128, 2], P('gx', 'gy'), may hold values from 0 to 65535, as said below
- send_tiles: int32 [32, 32, 128], P(('gx', 'gy')), may hold values from 0 to 2048, as said below
- recv_rows: int32 [32, 32, 128], P(('gx', 'gy')), may hold values from 0 to 2048, as said below
- block_inverse: float32 [512, 128, 128], P(('gx', 'gy'))
- couplings: float32 [512, 2, 128, 128], P(('gx', 'gy')), may hold values from -0.05303301 to 0.05303301
- neighbours: int32 [512, 2], P(('gx', 'gy')), may hold values from 0 to 511, as said below
Outputs:
- solution_field: float32 [256, 128, 256], P('gx', 'gy')
- residual: float32 [256, 128, 256], P('gx', 'gy')
The draws below stay inside these ranges and needn't reach their ends.
Inputs may be any that keep to these rules, and one draw needn't show every extreme that they name: The tile_labels entry of a tile is o * 2048 + r exactly where its device s lists it in send_tiles[s, o, n] and recv_rows[o, s, n] = r; every tile is listed once. send_tiles[s, o, n] is a tile number of device s, or 2048 for an empty slot; the filled slots of each s and o come first; one owner receives 128 filled slots from every device. recv_rows[o, s, n] is the owned row that slot n from device s adds into, or 2048 where that slot is empty. Block q belongs to device q // 16. neighbours[q, n] is a block of another device. The entries listed by the blocks of one device name blocks of exactly 8 distinct devices, exactly 4 entries for each of them.
All inputs are finite; a program needn't handle non-finite values.
Results may differ from the reference program's by a relative error of at most 0.00012.
Values sent between devices are 32-bit elements; how exact they have to be, the bound alone decides.
A program may use at most 64 MiB of HBM per device.

```python
import math
import jax
import jax.numpy as jnp
from jax import lax

CX = 32
CY = 32
NZ = 256
TZ = 128
NB_DEV = 2048
CB = 128
NBR = 2
LINK = 4
ITERS = 2
NX = 256
NY = 128
NZT = 2
TPD = 2048
NB = 65536
BPD = 16
NBLK = 512
MEAN = 64
CAP = 128
N_GX = 8
N_GY = 4
DEVICES = 32


def owner_layout(key):
    base_key = jax.random.fold_in(key, 11)
    key_pairing, key_surplus, key_shuffle, key_rows = jax.random.split(base_key, 4)
    half_count = DEVICES // 2
    pairing = jax.random.permutation(key_pairing, DEVICES).astype(jnp.int32)
    front_owner = pairing[half_count]
    second = pairing[half_count + 1]
    swapped = front_owner == DEVICES - 1
    pairing = pairing.at[half_count].set(jnp.where(swapped, second, front_owner))
    pairing = pairing.at[half_count + 1].set(jnp.where(swapped, front_owner, second))
    surplus = jax.random.randint(key_surplus, (DEVICES, half_count), 0, MEAN + 1)
    surplus = surplus.at[:, 0].set(MEAN)
    ranked = jnp.concatenate([MEAN + surplus, MEAN - surplus], axis=1).astype(jnp.int32)
    counts = jnp.zeros((DEVICES, DEVICES), jnp.int32).at[:, pairing].set(ranked)
    run_ends = jnp.cumsum(counts, axis=1)
    starts = run_ends - counts
    places = jnp.arange(TPD, dtype=jnp.int32)
    owners = jax.vmap(lambda run_row: jnp.searchsorted(run_row, places, side='right'))(run_ends).astype(jnp.int32)
    shuffles = jax.vmap(lambda sub_key: jax.random.permutation(sub_key, TPD))(jax.random.split(key_shuffle, DEVICES)).astype(jnp.int32)
    row_ids = jax.random.randint(key_rows, (DEVICES, TPD), 0, NB_DEV)
    run_start = jnp.take_along_axis(starts, owners, axis=1) == places[None, :]
    row_ids = jnp.where(run_start, NB_DEV - 1, row_ids).astype(jnp.int32)
    sources = jnp.arange(DEVICES, dtype=jnp.int32)[:, None]
    tile_label = jnp.zeros((DEVICES, TPD), jnp.int32).at[sources, shuffles].set(owners * NB_DEV + row_ids)
    slot_ids = jnp.arange(CAP, dtype=jnp.int32)
    positions = starts[:, :, None] + slot_ids[None, None, :]
    filled = slot_ids[None, None, :] < counts[:, :, None]
    clipped = jnp.minimum(positions, TPD - 1).reshape(DEVICES, DEVICES * CAP)
    tile_ids = jnp.take_along_axis(shuffles, clipped, axis=1).reshape(DEVICES, DEVICES, CAP)
    picked = jnp.take_along_axis(row_ids, clipped, axis=1).reshape(DEVICES, DEVICES, CAP)
    send_list = jnp.where(filled, tile_ids, TPD).astype(jnp.int32)
    recv_list = jnp.transpose(jnp.where(filled, picked, NB_DEV), (1, 0, 2)).astype(jnp.int32)
    labels = tile_label.reshape(N_GX, N_GY, CX, CY, NZT).transpose(0, 2, 1, 3, 4).reshape(NX, NY, NZT)
    return (labels, send_list, recv_list)


def draw_tile_labels(key, part):
    return owner_layout(key)[0]


def draw_send_tiles(key, part):
    return owner_layout(key)[1]


def draw_recv_rows(key, part):
    return owner_layout(key)[2]


def draw_neighbours(key, part):
    key_offsets, key_order, key_local = jax.random.split(jax.random.fold_in(key, 23), 3)
    push_count = BPD * NBR
    group_count = push_count // LINK
    offset_keys = jax.random.split(key_offsets, DEVICES)
    order_keys = jax.random.split(key_order, DEVICES)
    offsets = jax.vmap(lambda sub_key: jax.random.permutation(sub_key, DEVICES - 1)[:group_count] + 1)(offset_keys).astype(jnp.int32)
    orders = jax.vmap(lambda sub_key: jax.random.permutation(sub_key, push_count))(order_keys).astype(jnp.int32)
    group_of = (orders // LINK).astype(jnp.int32)
    chosen = jnp.take_along_axis(offsets, group_of, axis=1)
    sources = jnp.arange(DEVICES, dtype=jnp.int32)[:, None]
    targets = (sources + chosen) % DEVICES
    local = jax.random.randint(key_local, (DEVICES, push_count), 0, BPD)
    blocks = targets * BPD + local
    return blocks.reshape(NBLK, NBR).astype(jnp.int32)


def draw_block_inverse(key, part):
    key_scale, key_noise = jax.random.split(jax.random.fold_in(key, 31))
    scales = jnp.exp(jax.random.uniform(key_scale, (NBLK, 1, 1), jnp.float32, math.log(0.3), 0.0))
    noise = jax.random.normal(key_noise, (NBLK, CB, CB), jnp.float32)
    mixed = (noise + jnp.swapaxes(noise, 1, 2)) * (0.25 / math.sqrt(2.0 * CB))
    return (scales * (jnp.eye(CB, dtype=jnp.float32)[None] + mixed)).astype(jnp.float32)


def steps_of(stream_key, shape, shards, smallest, largest):
    def one(position, shards_of):
        draws = jax.random.uniform(jax.random.fold_in(jax.random.fold_in(stream_key, 6), position), (shards_of,), jnp.float32, smallest / len(shards), largest / len(shards))
        return jnp.repeat(jnp.exp(draws), shape[position] // shards_of).reshape((-1,) + (1,) * (len(shape) - position - 1))

    loudness = one(*shards[0])
    for cut in shards[1:]:
        loudness = loudness * one(*cut)
    return loudness


def scatter_about(stream_key, shape, width, bound, cuts=(), held_as=jnp.bfloat16):
    loudness = steps_of(stream_key, shape, cuts, -0.22, 0.18) if cuts else 1.0
    array = jax.random.normal(stream_key, shape, jnp.float32) * width * loudness
    return jnp.minimum(jnp.maximum(array, -bound), bound).astype(held_as)


def setup_inputs(seed: int = 0) -> dict:
    seeds = jax.random.split(jax.random.key(seed), 12)
    source_term = scatter_about(seeds[0], (NX, NY, NZ), 1.0, 6.0, ((0, 8), (1, 4)), jnp.float32)
    mobility_x = jnp.clip(jnp.exp(math.log(1.0) - 6.9077552 * jax.random.uniform(seeds[1], (NX, NY, NZ), jnp.float32) ** steps_of(seeds[1], (NX, NY, NZ), ((0, 8), (1, 4)), -0.2, 0.2)), 0.001, 1.0)
    mobility_y = jnp.clip(jnp.exp(math.log(1.0) - 6.9077552 * jax.random.uniform(seeds[2], (NX, NY, NZ), jnp.float32) ** steps_of(seeds[2], (NX, NY, NZ), ((0, 8), (1, 4)), -0.2, 0.2)), 0.001, 1.0)
    mobility_z = jnp.clip(jnp.exp(math.log(1.0) - 6.9077552 * jax.random.uniform(seeds[3], (NX, NY, NZ), jnp.float32) ** steps_of(seeds[3], (NX, NY, NZ), ((0, 8), (1, 4)), -0.2, 0.2)), 0.001, 1.0)
    bubble_fraction = jnp.clip(0.1 + 0.9 * jax.random.uniform(seeds[4], (NX, NY, NZ), jnp.float32) ** steps_of(seeds[4], (NX, NY, NZ), ((0, 8), (1, 4)), -0.2, 0.2), 0.1, 1.0)
    tile_labels = draw_tile_labels(jax.random.fold_in(seeds[11], 71), 0)
    send_tiles = draw_send_tiles(jax.random.fold_in(seeds[11], 71), 0)
    recv_rows = draw_recv_rows(jax.random.fold_in(seeds[11], 71), 0)
    block_inverse = draw_block_inverse(jax.random.fold_in(seeds[11], 71), 0)
    couplings = scatter_about(seeds[9], (NBLK, NBR, CB, CB), (0.1 / CB ** 0.5), 0.05303301, ((0, 32),), jnp.float32)
    neighbours = draw_neighbours(jax.random.fold_in(seeds[11], 71), 0)
    return {"source_term": source_term, "mobility_x": mobility_x, "mobility_y": mobility_y, "mobility_z": mobility_z, "bubble_fraction": bubble_fraction, "tile_labels": tile_labels, "send_tiles": send_tiles, "recv_rows": recv_rows, "block_inverse": block_inverse, "couplings": couplings, "neighbours": neighbours}


def lower_plane(values, axis):
    zero_plane = jnp.zeros_like(lax.slice_in_dim(values, 0, 1, axis=axis))
    return jnp.concatenate([zero_plane, lax.slice_in_dim(values, 0, values.shape[axis] - 1, axis=axis)], axis=axis)


def upper_plane(values, axis):
    zero_plane = jnp.zeros_like(lax.slice_in_dim(values, 0, 1, axis=axis))
    return jnp.concatenate([lax.slice_in_dim(values, 1, values.shape[axis], axis=axis), zero_plane], axis=axis)


def apply_operator(field, mobility_x, mobility_y, mobility_z):
    total_part = None
    for axis, mobility in ((0, mobility_x), (1, mobility_y), (2, mobility_z)):
        flux = mobility * (upper_plane(field, axis) - field)
        part = flux - lower_plane(flux, axis)
        total_part = part if total_part is None else total_part + part
    return -total_part


def restrict(tile_totals, send_tiles, recv_rows):
    per_device = tile_totals.reshape(N_GX, CX, N_GY, CY, NZT).transpose(0, 2, 1, 3, 4).reshape(DEVICES, TPD)
    padded = jnp.concatenate([per_device, jnp.zeros((DEVICES, 1), jnp.float32)], axis=1)
    values = jnp.take_along_axis(padded, send_tiles.reshape(DEVICES, DEVICES * CAP), axis=1)
    row_ids = jnp.transpose(recv_rows, (1, 0, 2))
    owner_ids = jnp.arange(DEVICES, dtype=jnp.int32)[None, :, None]
    target = jnp.where(row_ids < NB_DEV, owner_ids * NB_DEV + row_ids, NB).astype(jnp.int32)
    summed = jax.ops.segment_sum(values.reshape(-1), target.reshape(-1), num_segments=NB + 1)
    return summed[:NB]


def precondition(resid, bubble_fraction, tile_labels, send_tiles, recv_rows, block_inverse, couplings, neighbours, diagonal):
    tile_totals = (bubble_fraction * resid).reshape(NX, NY, NZT, TZ).sum(axis=3)
    totals = restrict(tile_totals, send_tiles, recv_rows).reshape(NBLK, CB)
    sweep_one = jnp.einsum("qij,qj->qi", block_inverse, totals, precision=lax.Precision.HIGHEST)
    pushed = jnp.einsum("qkij,qj->qki", couplings, sweep_one, precision=lax.Precision.HIGHEST)
    coupled = jnp.zeros((NBLK, CB), jnp.float32).at[neighbours.reshape(-1)].add(pushed.reshape(-1, CB))
    sweep_two = jnp.einsum("qij,qj->qi", block_inverse, totals - coupled, precision=lax.Precision.HIGHEST)
    tile_values = sweep_two.reshape(-1)[tile_labels]
    spread = jnp.broadcast_to(tile_values[..., None], (NX, NY, NZT, TZ)).reshape(NX, NY, NZ)
    return bubble_fraction * spread + resid / diagonal


def reference(source_term, mobility_x, mobility_y, mobility_z, bubble_fraction, tile_labels, send_tiles, recv_rows, block_inverse, couplings, neighbours):
    diagonal = (mobility_x + lower_plane(mobility_x, 0)) + (mobility_y + lower_plane(mobility_y, 1)) + (mobility_z + lower_plane(mobility_z, 2))

    def apply_pre(resid):
        return precondition(resid, bubble_fraction, tile_labels, send_tiles, recv_rows, block_inverse, couplings, neighbours, diagonal)

    solution_field = jnp.zeros_like(source_term)
    residual = source_term
    precond = apply_pre(residual)
    direction = precond
    rz_now = jnp.sum(residual * precond)
    for step in range(ITERS):
        image = apply_operator(direction, mobility_x, mobility_y, mobility_z)
        alpha = rz_now / jnp.sum(direction * image)
        solution_field = solution_field + alpha * direction
        residual = residual - alpha * image
        if step + 1 < ITERS:
            precond = apply_pre(residual)
            rz_next = jnp.sum(residual * precond)
            direction = precond + (rz_next / rz_now) * direction
            rz_now = rz_next
    return solution_field, residual
```

```python
import functools

import jax
import jax.numpy as jnp
from jax import lax
from jax.experimental import pallas as pl
from jax.experimental.pallas import tpu as pltpu
from jax.sharding import PartitionSpec as P

TZ = 128
LINK = 4
SLOT = 4
F32 = jnp.float32
BF16 = jnp.bfloat16
MESH = pl.DeviceIdType.MESH
NT = (((1,), (1,)), ((), ()))
NN = (((1,), (0,)), ((), ()))
GROUP = 8


def log2(value):
    assert value & (value - 1) == 0
    return value.bit_length() - 1


def iota(shape, axis):
    return lax.broadcasted_iota(jnp.int32, shape, axis)


def split_two(value):
    first = value.astype(BF16).astype(F32)
    return first, (value - first).astype(BF16).astype(F32)


def stack_two(value, axis=0):
    return jnp.concatenate(split_two(value), axis=axis).astype(BF16)


def fold_two(value):
    half = value.shape[0] // 2
    return value[:half] + value[half:]


def fold_tiles(value):
    tiles = [
        value[y : y + 8, z : z + 128]
        for y in range(0, value.shape[0], 8)
        for z in range(0, value.shape[1], 128)
    ]
    while len(tiles) > 1:
        tiles = [a + b for a, b in zip(tiles[::2], tiles[1::2])]
    return tiles[0]


def write_one_hots(index_ref, hot_ref):
    def step(block, carry):
        for sub in range(GROUP):
            index = index_ref[pl.ds(block * GROUP + sub, 1), :]
            hot = jnp.where(iota((128, 128), 0) == (index & 127), 1.0, 0.0)
            hot_ref[block, :, sub * 128 : (sub + 1) * 128] = hot.astype(BF16)
        return carry

    lax.fori_loop(0, hot_ref.shape[0], step, 0)


def gather_rows(table, index_ref, hot_ref, out_ref):
    parts = stack_two(table)
    high_count = table.shape[0]

    def step(block, carry):
        picked = fold_two(
            lax.dot_general(parts, hot_ref[block], NN, preferred_element_type=F32)
        )
        for sub in range(GROUP):
            row = block * GROUP + sub
            hit = iota((high_count, 128), 0) == (index_ref[pl.ds(row, 1), :] >> 7)
            mine = picked[:, sub * 128 : (sub + 1) * 128]
            out_ref[row] = jnp.sum(jnp.where(hit, mine, 0.0), axis=0, keepdims=True)
        return carry

    lax.fori_loop(0, hot_ref.shape[0], step, 0)


def scatter_rows(value_ref, index_ref, hot_ref, high_count):
    def step(block, total):
        pieces = []
        for sub in range(GROUP):
            row = block * GROUP + sub
            hit = iota((high_count, 128), 0) == (index_ref[pl.ds(row, 1), :] >> 7)
            pieces.append(stack_two(jnp.where(hit, value_ref[row], 0.0)))
        return total + lax.dot_general(
            jnp.concatenate(pieces, axis=1), hot_ref[block], NT, preferred_element_type=F32
        )

    start = jnp.zeros((2 * high_count, 128), F32)
    return fold_two(lax.fori_loop(0, hot_ref.shape[0], step, start))


def block_vectors(vectors):
    first, second = split_two(vectors)
    out = []
    for q in range(vectors.shape[0]):
        mine = iota(vectors.shape, 0) == q
        top = jnp.where(mine, first, 0.0)
        low = jnp.where(mine, second, 0.0)
        upper = jnp.concatenate([top, top], axis=1)
        lower = jnp.concatenate([low, jnp.zeros_like(low)], axis=1)
        out.append(jnp.concatenate([upper, lower], axis=0).astype(BF16))
    return out


def block_products(vectors, split_ref):
    total = None
    for q, part in enumerate(block_vectors(vectors)):
        term = lax.dot_general(part, split_ref[q], NT, preferred_element_type=F32)
        total = term if total is None else total + term
    return fold_two(total)


def kernel(
    counts,
    source_hbm,
    mob_x_hbm,
    mob_y_hbm,
    mob_z_hbm,
    fraction_hbm,
    inverse_hbm,
    couplings_hbm,
    send_ref,
    recv_ref,
    near_ref,
    out_x,
    out_r,
    res,
    mob_x,
    mob_y,
    mob_z,
    fraction,
    inverse,
    couplings,
    inv_diag,
    local,
    direction,
    local_two,
    zed,
    image,
    image_two,
    inverse_split,
    couplings_split,
    send_hot,
    recv_hot,
    send_map,
    totals_table,
    values_table,
    local_table,
    stencil_table,
    table_halo,
    low_mx,
    low_my,
    edge_my,
    edge_f,
    high_fx,
    high_fy,
    edges,
    halo_x,
    halo_y,
    row_send,
    row_recv,
    link_send,
    link_recv,
    sum_send,
    sum_recv,
    load_sem,
    side_send_sem,
    side_recv_sem,
    early_send_sem,
    early_recv_sem,
    table_send_sem,
    table_recv_sem,
    row_send_sem,
    row_recv_sem,
    link_send_sem,
    link_recv_sem,
    sum_send_sem,
    sum_recv_sem,
):
    count_x, count_y = counts
    devices = count_x * count_y
    at_x, at_y = lax.axis_index("gx"), lax.axis_index("gy")
    me = at_x * count_y + at_y
    size_x, size_y, depth = res.shape
    tiles_z = depth // TZ
    group = 128 // (size_y * tiles_z)
    table_rows = size_x // group
    blocks = inverse.shape[0]
    push_count = near_ref.size

    loads = [
        pltpu.make_async_copy(src, dst, load_sem.at[n])
        for n, (src, dst) in enumerate(
            (
                (source_hbm, res),
                (fraction_hbm, fraction),
                (mob_y_hbm, mob_y),
                (mob_x_hbm, mob_x),
                (mob_z_hbm, mob_z),
                (inverse_hbm, inverse),
                (couplings_hbm, couplings),
            )
        )
    ]
    for load in loads:
        load.start()

    barrier = pltpu.get_barrier_semaphore()

    def peer(step):
        other = lax.rem(me + step, devices)
        return (other // count_y, lax.rem(other, count_y)), other

    def greet(step, carry):
        pl.semaphore_signal(barrier, inc=1, device_id=peer(step)[0], device_id_type=MESH)
        return carry

    for ref in (low_mx, low_my, high_fx, high_fy, halo_x, halo_y, table_halo):
        ref[...] = jnp.zeros_like(ref)
    lax.fori_loop(1, devices, greet, 0)

    def exchange(send, recv, send_sem, recv_sem, same=False):
        def one(step, carry):
            device, other = peer(step)
            pltpu.make_async_remote_copy(
                src_ref=send.at[0 if same else other],
                dst_ref=recv.at[me],
                send_sem=send_sem,
                recv_sem=recv_sem,
                device_id=device,
                device_id_type=MESH,
            ).start()
            return carry

        lax.fori_loop(1, devices, one, 0)
        recv[me] = send[0 if same else me]

    def arrived(recv, recv_sem):
        part = recv.at[pl.ds(0, devices - 1)]
        pltpu.make_async_copy(part, part, recv_sem).wait()

    tile = send_ref[...]
    low = tile & 127
    tile_k = low & (tiles_z - 1)
    tile_j = (low >> log2(tiles_z)) & (size_y - 1)
    tile_g = low >> log2(tiles_z * size_y)
    send_map[...] = (
        (tile - low) + tile_k * (group * size_y) + tile_g * size_y + tile_j
    )

    def tile_sums(planes):
        stacked = jnp.concatenate(
            [plane[:, k * TZ : (k + 1) * TZ] for k in range(tiles_z) for plane in planes],
            axis=0,
        )
        return jnp.sum(stacked.T, axis=0, keepdims=True)

    def row_exchange(n):
        exchange(row_send.at[n], row_recv.at[n], row_send_sem.at[n], row_recv_sem.at[n])

    write_one_hots(send_map, send_hot)
    loads[0].wait()
    loads[1].wait()

    def first_totals(row, carry):
        xs = [row * group + g for g in range(group)]
        totals_table[0, pl.ds(row, 1), :] = tile_sums([fraction[x] * res[x] for x in xs])
        return carry

    lax.fori_loop(0, table_rows, first_totals, 0)
    gather_rows(totals_table[0], send_map, send_hot, row_send.at[0])
    pl.semaphore_wait(barrier, devices - 1)
    row_exchange(0)

    def side_copy(src, dst, send_sem, recv_sem, shift_x, shift_y):
        return pltpu.make_async_remote_copy(
            src_ref=src,
            dst_ref=dst,
            send_sem=send_sem,
            recv_sem=recv_sem,
            device_id=(at_x + shift_x, at_y + shift_y),
            device_id_type=MESH,
        )

    has_low_x, has_high_x = at_x > 0, at_x < count_x - 1
    has_low_y, has_high_y = at_y > 0, at_y < count_y - 1
    sides = (
        (has_low_x, has_high_x, -1, 0),
        (has_high_x, has_low_x, 1, 0),
        (has_low_y, has_high_y, 0, -1),
        (has_high_y, has_low_y, 0, 1),
    )

    def side_group(parts, send_sem, recv_sem):
        out = []
        for n, (side, src, dst) in enumerate(parts):
            there, came, shift_x, shift_y = sides[side]
            copy = side_copy(src, dst, send_sem.at[n], recv_sem.at[n], shift_x, shift_y)
            out.append((there, came, copy))
        return out

    def start(copies):
        for there, came, copy in copies:
            pl.when(there)(copy.start)

    def came_in(copies):
        for there, came, copy in copies:
            pl.when(came)(copy.wait_recv)

    loads[2].wait()
    loads[3].wait()

    def take_edge(x, carry):
        edge_my[x] = mob_y[x, size_y - 1 : size_y, :]
        edge_f[x] = fraction[x, 0:1, :]
        return carry

    lax.fori_loop(0, size_x, take_edge, 0)
    early = side_group(
        (
            (1, mob_x.at[size_x - 1], low_mx),
            (3, edge_my, low_my),
            (0, fraction.at[0], high_fx),
            (2, edge_f, high_fy),
        ),
        early_send_sem,
        early_recv_sem,
    )
    start(early)

    near_row = jnp.concatenate([near_ref[k : k + 1] for k in range(near_ref.shape[0])], axis=1)
    target_row = near_row >> log2(blocks)
    down, across = iota((push_count, push_count), 0), iota((push_count, push_count), 1)
    target_col = jnp.sum(
        jnp.where(down == across, target_row.astype(F32), 0.0), axis=1, keepdims=True
    ).astype(jnp.int32)
    earlier = down < across
    same = jnp.where((target_row == target_col) & earlier, 1, 0)
    rank = jnp.sum(same, axis=0, keepdims=True)
    slot = target_row * SLOT + rank
    chosen = iota((devices * SLOT, push_count), 0) == slot
    local_block = (near_row & (blocks - 1)).astype(F32)
    identity = jnp.sum(jnp.where(chosen, local_block, 0.0), axis=1, keepdims=True)
    link_send[0] = jnp.broadcast_to(identity, (devices * SLOT, 128)).reshape(
        devices, SLOT, 128
    )
    spread = jnp.where(chosen, 1.0, 0.0).astype(BF16)

    def link_exchange(n):
        exchange(link_send.at[n], link_recv.at[n], link_send_sem.at[n], link_recv_sem.at[n])

    link_exchange(0)

    lane = iota((size_y, depth), 1)
    row_of = iota((size_y, depth), 0)

    def below_z(plane):
        return jnp.where(lane == 0, 0.0, pltpu.roll(plane, 1, 1))

    def above_z(plane):
        return jnp.where(lane == depth - 1, 0.0, pltpu.roll(plane, depth - 1, 1))

    def below_y(plane, edge):
        return jnp.where(row_of == 0, edge, pltpu.roll(plane, 1, 0))

    def above_y(plane, edge):
        return jnp.where(row_of == size_y - 1, edge, pltpu.roll(plane, size_y - 1, 0))

    wide = group * size_y
    slot_of = iota((table_rows, 128), 1)
    slot_y = slot_of & (size_y - 1)
    slot_g = (slot_of >> log2(size_y)) & (group - 1)
    slot_k = slot_of >> log2(wide)

    def turn(table, shift):
        return pltpu.roll(table, shift % 128, 1) if shift % 128 else table

    def next_x(table, high):
        inner = turn(table, -size_y)
        outer = turn(
            jnp.concatenate([table[1:], high[0:1]], axis=0), (group - 1) * size_y
        )
        return jnp.where(slot_g < group - 1, inner, outer)

    def last_x(table, low):
        inner = turn(table, size_y)
        outer = turn(
            jnp.concatenate([low[table_rows - 1 :], table[: table_rows - 1]], axis=0),
            -(group - 1) * size_y,
        )
        return jnp.where(slot_g > 0, inner, outer)

    def next_y(table, high):
        return jnp.where(slot_y < size_y - 1, turn(table, -1), turn(high, size_y - 1))

    def last_y(table, low):
        return jnp.where(slot_y > 0, turn(table, 1), turn(low, 1 - size_y))

    def next_z(table):
        return jnp.where(slot_k < tiles_z - 1, turn(table, -wide), 0.0)

    def last_z(table):
        return jnp.where(slot_k > 0, turn(table, wide), 0.0)

    write_one_hots(recv_ref, recv_hot)
    loads[5].wait()

    def split_inverse(q, carry):
        inverse_split[q] = stack_two(inverse[q], axis=1)
        return carry

    lax.fori_loop(0, blocks, split_inverse, 0)
    loads[6].wait()

    def split_couplings(q, carry):
        couplings_split[q] = stack_two(
            jnp.concatenate([couplings[q, k] for k in range(couplings.shape[1])], axis=0),
            axis=1,
        )
        return carry

    lax.fori_loop(0, blocks, split_couplings, 0)

    zero_tile = jnp.zeros((8, 128), F32)
    fields = (local, direction, local_two, zed)

    def keep_edges(phase, x, value):
        edges[phase, 0, x] = value[0:1]
        edges[phase, 1, x] = value[size_y - 1 : size_y]

    def halo_copies(phase):
        field = fields[phase]
        return side_group(
            (
                (0, field.at[0], halo_x.at[phase, 1]),
                (1, field.at[size_x - 1], halo_x.at[phase, 0]),
                (2, edges.at[phase, 0], halo_y.at[phase, 1]),
                (3, edges.at[phase, 1], halo_y.at[phase, 0]),
            ),
            side_send_sem.at[phase],
            side_recv_sem.at[phase],
        )

    def prepare(row, lower, above, total):
        whole, across_x, across_y, across_z = [], [], [], []
        for g in range(group):
            x = row * group + g
            mob_a, mob_b, mob_c = mob_x[x], mob_y[x], mob_z[x]
            weight, source = fraction[x], res[x]
            diagonal = (
                (mob_a + lower) + (mob_b + below_y(mob_b, low_my[x])) + (mob_c + below_z(mob_c))
            )
            inverse_here = 1.0 / diagonal
            value = source * inverse_here
            inv_diag[x] = inverse_here
            local[x] = value
            keep_edges(0, x, value)
            total = total + fold_tiles(source * value)
            up = fraction[x + 1] if g < group - 1 or above is None else above
            whole.append(diagonal * (weight * weight))
            across_x.append(mob_a * weight * up)
            across_y.append(mob_b * weight * above_y(weight, high_fy[x]))
            across_z.append(mob_c * weight * above_z(weight))
            lower = mob_a
        here = pl.ds(row, 1)
        stencil_table[1, here, :] = tile_sums(across_x)
        stencil_table[2, here, :] = tile_sums(across_y)
        turned = jnp.concatenate(
            [p[:, k * TZ : (k + 1) * TZ] for k in range(tiles_z) for p in across_z], axis=0
        ).T
        crossing = turned[TZ - 1 : TZ]
        inside = jnp.sum(turned, axis=0, keepdims=True) - crossing
        stencil_table[3, here, :] = crossing
        stencil_table[0, here, :] = tile_sums(whole) - 2.0 * inside
        return lower, total

    def table_copies(n, pairs):
        return side_group(
            [(side, src, table_halo.at[n, side]) for side, src in pairs],
            table_send_sem.at[n],
            table_recv_sem.at[n],
        )

    def apply_operator(phase, emit):
        field = fields[phase]

        def group_step(row, here, flux_low, carry, top):
            values = []
            for g in range(group):
                x = row * group + g
                above = top if top is not None and g == group - 1 else field[x + 1]
                flux_x = mob_x[x] * (above - here)
                flux_y = mob_y[x] * (above_y(here, halo_y[phase, 1, x]) - here)
                edge = low_my[x] * (here[0:1] - halo_y[phase, 0, x])
                flux_z = mob_z[x] * (above_z(here) - here)
                value = (
                    (flux_low - flux_x)
                    + (below_y(flux_y, edge) - flux_y)
                    + (below_z(flux_z) - flux_z)
                )
                values.append((here, value))
                here, flux_low = above, flux_x
            return here, flux_low, emit(row, values, carry)

        first = field[0]
        flux = low_mx[...] * (first - halo_x[phase, 0])
        state = (first, flux, zero_tile)
        state = lax.fori_loop(
            0, table_rows - 1, lambda row, s: group_step(row, *s, None), state
        )
        return jnp.sum(group_step(table_rows - 1, *state, halo_x[phase, 1])[2])

    def emit_local(n):
        def emit(row, values, total):
            parts = []
            for g, (here, value) in enumerate(values):
                total = total + fold_tiles(here * value)
                parts.append(fraction[row * group + g] * value)
            local_table[n, pl.ds(row, 1), :] = tile_sums(parts)
            return total

        return emit

    def emit_field(result):
        def emit(row, values, total):
            for g, (here, value) in enumerate(values):
                result[row * group + g] = value
            return total

        return emit

    def coarse_totals(phase):
        n = 2 * phase
        arrived(row_recv.at[n], row_recv_sem.at[n])
        return scatter_rows(row_recv.at[n], recv_ref, recv_hot, blocks)

    def sweep_first(phase, totals):
        sweep_one = block_products(totals, inverse_split)
        both = block_products(sweep_one, couplings_split)
        pushed = jnp.concatenate(
            [both[:, k * 128 : (k + 1) * 128] for k in range(couplings.shape[1])], axis=0
        )
        upper, lower = split_two(pushed)
        out_values = lax.dot_general(
            spread, upper.astype(BF16), NN, preferred_element_type=F32
        ) + lax.dot_general(spread, lower.astype(BF16), NN, preferred_element_type=F32)
        link_send[1 + phase] = out_values.reshape(devices, SLOT, 128)
        link_exchange(1 + phase)

    def sweep_second(phase, totals, gather_in):
        second = 2 * phase + 1
        arrived(link_recv.at[1 + phase], link_recv_sem.at[1 + phase])
        values = stack_two(link_recv[1 + phase].reshape(devices * SLOT, 128), axis=1)
        summed = lax.dot_general(gather_in, values, NN, preferred_element_type=F32)
        coupled = summed[:, :128] + summed[:, 128:]
        sweep_two = block_products(totals - coupled, inverse_split)
        gather_rows(sweep_two, recv_ref, recv_hot, row_send.at[second])
        row_exchange(second)

    def tile_values(phase):
        second = 2 * phase + 1
        arrived(row_recv.at[second], row_recv_sem.at[second])
        values_table[phase] = scatter_rows(
            row_recv.at[second], send_map, send_hot, table_rows
        )
        copies = table_copies(
            1 + phase, [(side, values_table.at[phase]) for side in range(4)]
        )
        start(copies)
        return copies

    def make_field(phase):
        field, plus = fields[2 * phase + 1], fields[2 * phase]

        def step(row, carry):
            stacked = jnp.broadcast_to(values_table[phase, pl.ds(row, 1), :], (128, 128)).T
            for g in range(group):
                x = row * group + g
                tiles = [
                    stacked[(k * group + g) * size_y : (k * group + g + 1) * size_y]
                    for k in range(tiles_z)
                ]
                value = fraction[x] * jnp.concatenate(tiles, axis=1) + plus[x]
                field[x] = value
                keep_edges(2 * phase + 1, x, value)
            return carry

        lax.fori_loop(0, table_rows, step, 0)
        copies = halo_copies(2 * phase + 1)
        start(copies)
        return copies

    def tile_operator(phase):
        table = values_table[phase]
        n = 1 + phase
        far_x, far_y = stencil_table[1], stencil_table[2]
        near_x = last_x(far_x, table_halo[0, 1])
        near_y = last_y(far_y, table_halo[0, 3])
        far_z = stencil_table[3]
        return (
            stencil_table[0] * table
            - (far_x * next_x(table, table_halo[n, 0]) + near_x * last_x(table, table_halo[n, 1]))
            - (far_y * next_y(table, table_halo[n, 2]) + near_y * last_y(table, table_halo[n, 3]))
            - (far_z * next_z(table) + last_z(far_z) * last_z(table))
        )

    place = iota((1, 128), 1)

    def start_sums(phase, values):
        row = jnp.zeros((1, 128), F32)
        for n, value in enumerate(values):
            row = jnp.where(place == n, value, row)
        sum_send[phase, 0] = row
        exchange(
            sum_send.at[phase],
            sum_recv.at[phase],
            sum_send_sem.at[phase],
            sum_recv_sem.at[phase],
            same=True,
        )

    def end_sums(phase, count):
        arrived(sum_recv.at[phase], sum_recv_sem.at[phase])
        totals = [sum_recv[phase, n] for n in range(4)]
        for n in range(4, devices):
            totals[n % 4] = totals[n % 4] + sum_recv[phase, n]
        total = (totals[0] + totals[1]) + (totals[2] + totals[3])
        return [
            jnp.sum(jnp.where(place == n, total, 0.0), axis=1, keepdims=True)
            for n in range(count)
        ]

    waits = [early]
    totals = coarse_totals(0)
    sweep_first(0, totals)

    loads[4].wait()
    came_in(early)
    lower, total = lax.fori_loop(
        0,
        table_rows - 1,
        lambda row, s: prepare(row, s[0], None, s[1]),
        (low_mx[...], zero_tile),
    )
    _, total = prepare(table_rows - 1, lower, high_fx[...], total)
    source_local = jnp.sum(total)
    waits.append(halo_copies(0))
    start(waits[-1])
    waits.append(table_copies(0, ((1, stencil_table.at[1]), (3, stencil_table.at[2]))))
    start(waits[-1])
    arrived(link_recv.at[0], link_recv_sem.at[0])
    names = link_recv[0].reshape(devices * SLOT, 128).T[:blocks]
    gather_in = jnp.where(
        names == iota((blocks, devices * SLOT), 0).astype(F32), 1.0, 0.0
    ).astype(BF16)

    sweep_second(0, totals, gather_in)

    came_in(waits[1])
    local_energy = apply_operator(0, emit_local(0))

    waits.append(tile_values(0))
    tables = waits[-1]
    waits.append(make_field(0))
    halos = waits[-1]
    came_in(waits[2])
    came_in(tables)
    values = values_table[0]
    operated = tile_operator(0)
    image_totals = operated + local_table[0]
    totals_table[1] = image_totals
    rz_part = jnp.sum(totals_table[0] * values) + source_local
    energy_part = jnp.sum(values * (image_totals + local_table[0])) + local_energy
    start_sums(0, (rz_part, energy_part))
    gather_rows(image_totals, send_map, send_hot, row_send.at[2])
    row_exchange(2)

    came_in(halos)
    apply_operator(1, emit_field(image))

    rz, energy = end_sums(0, 2)
    alpha = rz / energy
    totals = totals - alpha * coarse_totals(1)
    sweep_first(1, totals)

    def update(x, carry):
        own, cross = carry
        pushed = image[x]
        here = res[x] - alpha * pushed
        value = inv_diag[x] * here
        res[x] = here
        local_two[x] = value
        keep_edges(2, x, value)
        return own + fold_tiles(here * value), cross + fold_tiles(value * pushed)

    own, cross = lax.fori_loop(0, size_x, update, (zero_tile, zero_tile))
    residual_local, cross_local = jnp.sum(own), jnp.sum(cross)
    waits.append(halo_copies(2))
    start(waits[-1])

    sweep_second(1, totals, gather_in)

    came_in(waits[-1])
    local_energy = apply_operator(2, emit_local(1))

    waits.append(tile_values(1))
    tables = waits[-1]
    waits.append(make_field(1))
    halos = waits[-1]
    came_in(tables)
    values = values_table[1]
    operated = tile_operator(1)
    tile_totals = totals_table[0] - alpha * totals_table[1]
    next_part = jnp.sum(tile_totals * values) + residual_local
    own_part = jnp.sum(values * (operated + 2.0 * local_table[1])) + local_energy
    cross_part = jnp.sum(values * totals_table[1]) + cross_local
    start_sums(1, (next_part, own_part, cross_part))

    came_in(halos)
    apply_operator(3, emit_field(image_two))

    rz_next, own, cross = end_sums(1, 3)
    beta = rz_next / rz
    alpha_two = rz_next / (own + beta * (2.0 * cross + beta * energy))

    def finish(x, carry):
        first = direction[x]
        out_x[x] = alpha * first + alpha_two * (zed[x] + beta * first)
        out_r[x] = res[x] - alpha_two * (image_two[x] + beta * image[x])
        return carry

    lax.fori_loop(0, size_x, finish, 0)
    for copies in waits:
        for there, came, copy in copies:
            pl.when(there)(copy.wait_send)
    for n in range(4):
        arrived(row_send.at[n], row_send_sem.at[n])
    for n in range(3):
        arrived(link_send.at[n], link_send_sem.at[n])
    for n in range(2):
        arrived(sum_recv.at[n], sum_send_sem.at[n])


def body(
    source_term,
    mobility_x,
    mobility_y,
    mobility_z,
    bubble_fraction,
    tile_labels,
    send_tiles,
    recv_rows,
    block_inverse,
    couplings,
    neighbours,
):
    count_x, count_y = lax.axis_size("gx"), lax.axis_size("gy")
    devices = count_x * count_y
    size_x, size_y, depth = source_term.shape
    tiles = size_x * size_y * (depth // TZ)
    blocks, order = block_inverse.shape[:2]
    send, recv = send_tiles[0], recv_rows[0]
    pad = 128 - send.shape[1]
    assert order == 128 and pad >= 0
    if pad:
        send = jnp.pad(send, ((0, 0), (0, pad)), constant_values=tiles)
        recv = jnp.pad(recv, ((0, 0), (0, pad)), constant_values=blocks * order)
    table_rows = tiles // 128
    field = (size_x, size_y, depth)
    hbm = pl.BlockSpec(memory_space=pltpu.HBM)
    vmem = pl.BlockSpec(memory_space=pltpu.VMEM)
    dma = pltpu.SemaphoreType.DMA
    return pl.pallas_call(
        functools.partial(kernel, (count_x, count_y)),
        out_shape=(
            jax.ShapeDtypeStruct(field, F32),
            jax.ShapeDtypeStruct(field, F32),
        ),
        in_specs=[hbm] * 7 + [vmem] * 3,
        out_specs=(vmem, vmem),
        scratch_shapes=[
            *[pltpu.VMEM(field, F32)] * 5,
            pltpu.VMEM((blocks, order, order), F32),
            pltpu.VMEM(couplings.shape, F32),
            *[pltpu.VMEM(field, F32)] * 7,
            pltpu.VMEM((blocks, order, 2 * order), BF16),
            pltpu.VMEM((blocks, order * couplings.shape[1], 2 * order), BF16),
            pltpu.VMEM((devices // GROUP, 128, GROUP * 128), BF16),
            pltpu.VMEM((devices // GROUP, 128, GROUP * 128), BF16),
            pltpu.VMEM((devices, 128), jnp.int32),
            pltpu.VMEM((2, table_rows, 128), F32),
            pltpu.VMEM((2, table_rows, 128), F32),
            pltpu.VMEM((2, table_rows, 128), F32),
            pltpu.VMEM((4, table_rows, 128), F32),
            pltpu.VMEM((3, 4, table_rows, 128), F32),
            pltpu.VMEM((size_y, depth), F32),
            pltpu.VMEM((size_x, 1, depth), F32),
            pltpu.VMEM((size_x, 1, depth), F32),
            pltpu.VMEM((size_x, 1, depth), F32),
            pltpu.VMEM((size_y, depth), F32),
            pltpu.VMEM((size_x, 1, depth), F32),
            pltpu.VMEM((4, 2, size_x, 1, depth), F32),
            pltpu.VMEM((4, 2, size_y, depth), F32),
            pltpu.VMEM((4, 2, size_x, 1, depth), F32),
            pltpu.VMEM((4, devices, 1, 128), F32),
            pltpu.VMEM((4, devices, 1, 128), F32),
            pltpu.VMEM((3, devices, SLOT, 128), F32),
            pltpu.VMEM((3, devices, SLOT, 128), F32),
            pltpu.VMEM((2, 1, 1, 128), F32),
            pltpu.VMEM((2, devices, 1, 128), F32),
            dma((7,)),
            dma((4, 4)),
            dma((4, 4)),
            dma((4,)),
            dma((4,)),
            dma((3, 4)),
            dma((3, 4)),
            dma((4,)),
            dma((4,)),
            dma((3,)),
            dma((3,)),
            dma((2,)),
            dma((2,)),
        ],
        compiler_params=pltpu.CompilerParams(
            collective_id=0, has_side_effects=True, vmem_limit_bytes=63500000
        ),
    )(
        source_term,
        mobility_x,
        mobility_y,
        mobility_z,
        bubble_fraction,
        block_inverse,
        couplings,
        send,
        recv,
        neighbours.T,
    )


def solution(mesh):
    return jax.shard_map(
        body,
        mesh=mesh,
        in_specs=(
            P("gx", "gy", None),
            P("gx", "gy", None),
            P("gx", "gy", None),
            P("gx", "gy", None),
            P("gx", "gy", None),
            P("gx", "gy", None),
            P(("gx", "gy"), None, None),
            P(("gx", "gy"), None, None),
            P(("gx", "gy"), None, None),
            P(("gx", "gy"), None, None, None),
            P(("gx", "gy"), None),
        ),
        out_specs=(P("gx", "gy", None), P("gx", "gy", None)),
        check_vma=False,
    )
```

```python
import functools

import jax
import jax.numpy as jnp
from jax import lax
from jax.experimental import pallas as pl
from jax.experimental.pallas import tpu as pltpu
from jax.sharding import PartitionSpec as P

TZ = 128
LINK = 4
SLOT = 4
F32 = jnp.float32
BF16 = jnp.bfloat16
MESH = pl.DeviceIdType.MESH
NT = (((1,), (1,)), ((), ()))
NN = (((1,), (0,)), ((), ()))
GROUP = 8


def log2(value):
    assert value & (value - 1) == 0
    return value.bit_length() - 1


def iota(shape, axis):
    return lax.broadcasted_iota(jnp.int32, shape, axis)


def split_two(value):
    first = value.astype(BF16).astype(F32)
    return first, (value - first).astype(BF16).astype(F32)


def stack_two(value, axis=0):
    return jnp.concatenate(split_two(value), axis=axis).astype(BF16)


def fold_two(value):
    half = value.shape[0] // 2
    return value[:half] + value[half:]


def fold_tiles(value):
    tiles = [
        value[y : y + 8, z : z + 128]
        for y in range(0, value.shape[0], 8)
        for z in range(0, value.shape[1], 128)
    ]
    while len(tiles) > 1:
        tiles = [a + b for a, b in zip(tiles[::2], tiles[1::2])]
    return tiles[0]


def write_one_hots(index_ref, hot_ref):
    group = hot_ref.shape[2] // 128

    def step(block, carry):
        for sub in range(group):
            index = index_ref[pl.ds(block * group + sub, 1), :]
            hot = jnp.where(iota((128, 128), 0) == (index & 127), 1.0, 0.0)
            hot_ref[block, :, sub * 128 : (sub + 1) * 128] = hot.astype(BF16)
        return carry

    lax.fori_loop(0, hot_ref.shape[0], step, 0)


def in_chunks(count, step, carry):
    chunk = min(count, 4)

    def chunk_step(n, carry):
        for sub in range(chunk):
            carry = step(n * chunk + sub, carry)
        return carry

    if count == chunk:
        return chunk_step(0, carry)
    assert count % chunk == 0
    return lax.fori_loop(0, count // chunk, chunk_step, carry)


def gather_rows(table, index_ref, hot_ref, store):
    parts = stack_two(table)
    high_count = table.shape[0]
    group = hot_ref.shape[2] // 128

    def step(block, carry):
        picked = fold_two(
            lax.dot_general(parts, hot_ref[block], NN, preferred_element_type=F32)
        )
        for sub in range(group):
            row = block * group + sub
            hit = iota((high_count, 128), 0) == (index_ref[pl.ds(row, 1), :] >> 7)
            mine = picked[:, sub * 128 : (sub + 1) * 128]
            store(row, jnp.sum(jnp.where(hit, mine, 0.0), axis=0, keepdims=True))
        return carry

    in_chunks(hot_ref.shape[0], step, 0)


def scatter_rows(value_of, index_ref, hot_ref, high_count):
    group = hot_ref.shape[2] // 128

    def step(block, total):
        pieces = []
        for sub in range(group):
            row = block * group + sub
            hit = iota((high_count, 128), 0) == (index_ref[pl.ds(row, 1), :] >> 7)
            pieces.append(stack_two(jnp.where(hit, value_of(row), 0.0)))
        return total + lax.dot_general(
            jnp.concatenate(pieces, axis=1), hot_ref[block], NT, preferred_element_type=F32
        )

    start = jnp.zeros((2 * high_count, 128), F32)
    return fold_two(in_chunks(hot_ref.shape[0], step, start))


def block_vectors(vectors):
    first, second = split_two(vectors)
    out = []
    for q in range(vectors.shape[0]):
        mine = iota(vectors.shape, 0) == q
        top = jnp.where(mine, first, 0.0)
        low = jnp.where(mine, second, 0.0)
        upper = jnp.concatenate([top, top], axis=1)
        lower = jnp.concatenate([low, jnp.zeros_like(low)], axis=1)
        out.append(jnp.concatenate([upper, lower], axis=0).astype(BF16))
    return out


def block_products(vectors, split_ref):
    total = None
    for q, part in enumerate(block_vectors(vectors)):
        term = lax.dot_general(part, split_ref[q], NT, preferred_element_type=F32)
        total = term if total is None else total + term
    return fold_two(total)


def kernel(
    counts,
    source_hbm,
    mob_x_hbm,
    mob_y_hbm,
    mob_z_hbm,
    fraction_hbm,
    inverse_hbm,
    couplings_hbm,
    send_ref,
    recv_ref,
    near_ref,
    res,
    direction,
    zed,
    image,
    image_two,
    gain_ref,
    gain_two_ref,
    mix_ref,
    mob_x,
    mob_y,
    mob_z,
    fraction,
    inverse,
    couplings,
    inv_diag,
    local,
    local_two,
    inverse_split,
    couplings_split,
    send_hot,
    recv_hot,
    back_hot,
    side_hot,
    send_map,
    back_map,
    side_map,
    totals_table,
    values_table,
    local_table,
    stencil_table,
    code_table,
    beside_table,
    beside_row,
    table_halo,
    low_mx,
    low_my,
    edge_my,
    edge_f,
    halo_fx,
    halo_fy,
    edges,
    halo_x,
    halo_y,
    row_send,
    row_recv,
    side_send,
    side_recv,
    link_send,
    link_recv,
    sum_send,
    sum_recv,
    load_sem,
    side_send_sem,
    side_recv_sem,
    early_send_sem,
    early_recv_sem,
    table_send_sem,
    table_recv_sem,
    row_send_sem,
    row_recv_sem,
    spread_send_sem,
    spread_recv_sem,
    link_send_sem,
    link_recv_sem,
    sum_send_sem,
    sum_recv_sem,
):
    count_x, count_y = counts
    devices = count_x * count_y
    at_x, at_y = lax.axis_index("gx"), lax.axis_index("gy")
    me = at_x * count_y + at_y
    size_x, size_y, depth = res.shape
    tiles_z = depth // TZ
    group = 128 // (size_y * tiles_z)
    table_rows = size_x // group
    blocks = inverse.shape[0]
    push_count = near_ref.size

    loads = [
        pltpu.make_async_copy(src, dst, load_sem.at[n])
        for n, (src, dst) in enumerate(
            (
                (source_hbm, res),
                (fraction_hbm, fraction),
                (mob_y_hbm, mob_y),
                (mob_x_hbm, mob_x),
                (mob_z_hbm, mob_z),
                (inverse_hbm, inverse),
                (couplings_hbm, couplings),
            )
        )
    ]
    for load in loads:
        load.start()

    barrier = pltpu.get_barrier_semaphore()

    def peer(step):
        other = lax.rem(me + step, devices)
        return (other // count_y, lax.rem(other, count_y)), other

    def greet(step, carry):
        pl.semaphore_signal(barrier, inc=1, device_id=peer(step)[0], device_id_type=MESH)
        return carry

    for ref in (low_mx, low_my, halo_fx, halo_fy, halo_x, halo_y, side_send):
        ref[...] = jnp.zeros_like(ref)
    table_halo[0] = jnp.zeros_like(table_halo[0])
    table_halo[1] = jnp.full_like(table_halo[1], -1.0)
    lax.fori_loop(1, devices, greet, 0)

    def exchange(send, recv, send_sem, recv_sem, same=False):
        def one(step, carry):
            device, other = peer(step)
            pltpu.make_async_remote_copy(
                src_ref=send.at[0 if same else other],
                dst_ref=recv.at[me],
                send_sem=send_sem,
                recv_sem=recv_sem,
                device_id=device,
                device_id_type=MESH,
            ).start()
            return carry

        lax.fori_loop(1, devices, one, 0)
        recv[me] = send[0 if same else me]

    def arrived(recv, recv_sem):
        part = recv.at[pl.ds(0, devices - 1)]
        pltpu.make_async_copy(part, part, recv_sem).wait()

    tile = send_ref[...]
    low = tile & 127
    tile_k = low & (tiles_z - 1)
    tile_j = (low >> log2(tiles_z)) & (size_y - 1)
    tile_g = low >> log2(tiles_z * size_y)
    send_map[...] = (
        (tile - low) + tile_k * (group * size_y) + tile_g * size_y + tile_j
    )

    def tile_sums(planes):
        stacked = jnp.concatenate(
            [plane[:, k * TZ : (k + 1) * TZ] for k in range(tiles_z) for plane in planes],
            axis=0,
        )
        return jnp.sum(stacked.T, axis=0, keepdims=True)

    def row_exchange(n):
        exchange(row_send.at[n], row_recv.at[n], row_send_sem.at[n], row_recv_sem.at[n])

    write_one_hots(send_map, send_hot)
    loads[0].wait()
    loads[1].wait()

    def first_totals(row, carry):
        xs = [row * group + g for g in range(group)]
        totals_table[0, pl.ds(row, 1), :] = tile_sums([fraction[x] * res[x] for x in xs])
        return carry

    lax.fori_loop(0, table_rows, first_totals, 0)
    def to_owners(n):
        def store(row, value):
            row_send[n, row] = value

        return store

    gather_rows(totals_table[0], send_map, send_hot, to_owners(0))
    pl.semaphore_wait(barrier, devices - 1)
    row_exchange(0)

    def side_copy(src, dst, send_sem, recv_sem, shift_x, shift_y):
        return pltpu.make_async_remote_copy(
            src_ref=src,
            dst_ref=dst,
            send_sem=send_sem,
            recv_sem=recv_sem,
            device_id=(at_x + shift_x, at_y + shift_y),
            device_id_type=MESH,
        )

    has_low_x, has_high_x = at_x > 0, at_x < count_x - 1
    has_low_y, has_high_y = at_y > 0, at_y < count_y - 1
    sides = (
        (has_low_x, has_high_x, -1, 0),
        (has_high_x, has_low_x, 1, 0),
        (has_low_y, has_high_y, 0, -1),
        (has_high_y, has_low_y, 0, 1),
    )

    def side_group(parts, send_sem, recv_sem):
        out = []
        for n, (side, src, dst) in enumerate(parts):
            there, came, shift_x, shift_y = sides[side]
            copy = side_copy(src, dst, send_sem.at[n], recv_sem.at[n], shift_x, shift_y)
            out.append((there, came, copy))
        return out

    def start(copies):
        for there, came, copy in copies:
            pl.when(there)(copy.start)

    def came_in(copies):
        for there, came, copy in copies:
            pl.when(came)(copy.wait_recv)

    loads[2].wait()
    loads[3].wait()

    def take_edge(x, carry):
        edge_my[x] = mob_y[x, size_y - 1 : size_y, :]
        edge_f[0, x] = fraction[x, 0:1, :]
        edge_f[1, x] = fraction[x, size_y - 1 : size_y, :]
        return carry

    lax.fori_loop(0, size_x, take_edge, 0)
    early = side_group(
        (
            (1, mob_x.at[size_x - 1], low_mx),
            (3, edge_my, low_my),
            (0, fraction.at[0], halo_fx.at[1]),
            (1, fraction.at[size_x - 1], halo_fx.at[0]),
            (2, edge_f.at[0], halo_fy.at[1]),
            (3, edge_f.at[1], halo_fy.at[0]),
        ),
        early_send_sem,
        early_recv_sem,
    )
    start(early)

    near_row = jnp.concatenate([near_ref[k : k + 1] for k in range(near_ref.shape[0])], axis=1)
    target_row = near_row >> log2(blocks)
    down, across = iota((push_count, push_count), 0), iota((push_count, push_count), 1)
    target_col = jnp.sum(
        jnp.where(down == across, target_row.astype(F32), 0.0), axis=1, keepdims=True
    ).astype(jnp.int32)
    earlier = down < across
    same = jnp.where((target_row == target_col) & earlier, 1, 0)
    rank = jnp.sum(same, axis=0, keepdims=True)
    slot = target_row * SLOT + rank
    chosen = iota((devices * SLOT, push_count), 0) == slot
    local_block = (near_row & (blocks - 1)).astype(F32)
    identity = jnp.sum(jnp.where(chosen, local_block, 0.0), axis=1, keepdims=True)
    link_send[0] = jnp.broadcast_to(identity, (devices * SLOT, 128)).reshape(
        devices, SLOT, 128
    )
    spread = jnp.where(chosen, 1.0, 0.0).astype(BF16)

    def link_exchange(n):
        exchange(link_send.at[n], link_recv.at[n], link_send_sem.at[n], link_recv_sem.at[n])

    link_exchange(0)

    lane = iota((size_y, depth), 1)
    row_of = iota((size_y, depth), 0)

    def below_z(plane):
        return jnp.where(lane == 0, 0.0, pltpu.roll(plane, 1, 1))

    def above_z(plane):
        return jnp.where(lane == depth - 1, 0.0, pltpu.roll(plane, depth - 1, 1))

    def below_y(plane, edge):
        return jnp.where(row_of == 0, edge, pltpu.roll(plane, 1, 0))

    def above_y(plane, edge):
        return jnp.where(row_of == size_y - 1, edge, pltpu.roll(plane, size_y - 1, 0))

    wide = group * size_y
    slot_of = iota((table_rows, 128), 1)
    slot_y = slot_of & (size_y - 1)
    slot_g = (slot_of >> log2(size_y)) & (group - 1)
    slot_k = slot_of >> log2(wide)

    def turn(table, shift):
        return pltpu.roll(table, shift % 128, 1) if shift % 128 else table

    def next_x(table, high):
        inner = turn(table, -size_y)
        outer = turn(jnp.concatenate([table[1:], high], axis=0), (group - 1) * size_y)
        return jnp.where(slot_g < group - 1, inner, outer)

    def last_x(table, low):
        inner = turn(table, size_y)
        outer = turn(
            jnp.concatenate([low, table[: table_rows - 1]], axis=0), -(group - 1) * size_y
        )
        return jnp.where(slot_g > 0, inner, outer)

    def next_y(table, high):
        return jnp.where(slot_y < size_y - 1, turn(table, -1), high)

    def last_y(table, low):
        return jnp.where(slot_y > 0, turn(table, 1), low)

    def next_z(table):
        return jnp.where(slot_k < tiles_z - 1, turn(table, -wide), 0.0)

    def last_z(table):
        return jnp.where(slot_k > 0, turn(table, wide), 0.0)

    write_one_hots(recv_ref, recv_hot)
    loads[5].wait()

    def split_inverse(q, carry):
        inverse_split[q] = stack_two(inverse[q], axis=1)
        return carry

    lax.fori_loop(0, blocks, split_inverse, 0)
    loads[6].wait()

    def fold_couplings(q, carry):
        both = jnp.concatenate([couplings[q, k] for k in range(couplings.shape[1])], axis=0)
        upper, lower = split_two(both)
        top, rest = split_two(inverse[q])
        product = lax.dot_general(
            jnp.concatenate([upper, upper, lower], axis=1).astype(BF16),
            jnp.concatenate([top, rest, top], axis=0).astype(BF16),
            NN,
            preferred_element_type=F32,
        )
        couplings_split[q] = stack_two(product, axis=1)
        return carry

    lax.fori_loop(0, blocks, fold_couplings, 0)

    place = iota((1, 128), 1)
    codes = scatter_rows(
        lambda row: (row * 128 + place).astype(F32), send_map, send_hot, table_rows
    )
    code_table[...] = codes
    back_map[...] = codes.astype(jnp.int32)

    zero_tile = jnp.zeros((8, 128), F32)
    fields = (local, direction, local_two, zed)

    def keep_edges(phase, x, value):
        edges[phase, 0, x] = value[0:1]
        edges[phase, 1, x] = value[size_y - 1 : size_y]

    def halo_copies(phase):
        field = fields[2 * phase]
        return side_group(
            (
                (0, field.at[0], halo_x.at[2 * phase, 1]),
                (1, field.at[size_x - 1], halo_x.at[2 * phase, 0]),
                (2, edges.at[phase, 0], halo_y.at[2 * phase, 1]),
                (3, edges.at[phase, 1], halo_y.at[2 * phase, 0]),
            ),
            side_send_sem.at[phase],
            side_recv_sem.at[phase],
        )

    def prepare(row, lower, above, total):
        whole, across_x, across_y, across_z = [], [], [], []
        for g in range(group):
            x = row * group + g
            mob_a, mob_b, mob_c = mob_x[x], mob_y[x], mob_z[x]
            weight, source = fraction[x], res[x]
            diagonal = (
                (mob_a + lower) + (mob_b + below_y(mob_b, low_my[x])) + (mob_c + below_z(mob_c))
            )
            inverse_here = 1.0 / diagonal
            value = source * inverse_here
            inv_diag[x] = inverse_here
            local[x] = value
            keep_edges(0, x, value)
            total = total + fold_tiles(source * value)
            up = fraction[x + 1] if g < group - 1 or above is None else above
            whole.append(diagonal * (weight * weight))
            across_x.append(mob_a * weight * up)
            across_y.append(mob_b * weight * above_y(weight, halo_fy[1, x]))
            across_z.append(mob_c * weight * above_z(weight))
            lower = mob_a
        here = pl.ds(row, 1)
        stencil_table[1, here, :] = tile_sums(across_x)
        stencil_table[3, here, :] = tile_sums(across_y)
        turned = jnp.concatenate(
            [p[:, k * TZ : (k + 1) * TZ] for k in range(tiles_z) for p in across_z], axis=0
        ).T
        crossing = turned[TZ - 1 : TZ]
        inside = jnp.sum(turned, axis=0, keepdims=True) - crossing
        stencil_table[5, here, :] = crossing
        stencil_table[0, here, :] = tile_sums(whole) - 2.0 * inside
        return lower, total

    def table_copies(n, pairs):
        return side_group(
            [(side, src, table_halo.at[n, side]) for side, src in pairs],
            table_send_sem.at[n],
            table_recv_sem.at[n],
        )

    def apply_operator(phase, emit):
        field = fields[phase]

        def group_step(row, here, flux_low, carry, top):
            values = []
            for g in range(group):
                x = row * group + g
                above = top if top is not None and g == group - 1 else field[x + 1]
                flux_x = mob_x[x] * (above - here)
                flux_y = mob_y[x] * (above_y(here, halo_y[phase, 1, x]) - here)
                edge = low_my[x] * (here[0:1] - halo_y[phase, 0, x])
                flux_z = mob_z[x] * (above_z(here) - here)
                value = (
                    (flux_low - flux_x)
                    + (below_y(flux_y, edge) - flux_y)
                    + (below_z(flux_z) - flux_z)
                )
                values.append((here, value))
                here, flux_low = above, flux_x
            return here, flux_low, emit(row, values, carry)

        first = field[0]
        flux = low_mx[...] * (first - halo_x[phase, 0])
        state = (first, flux, zero_tile)
        state = lax.fori_loop(
            0, table_rows - 1, lambda row, s: group_step(row, *s, None), state
        )
        return jnp.sum(group_step(table_rows - 1, *state, halo_x[phase, 1])[2])

    def emit_local(n):
        def emit(row, values, total):
            parts = []
            for g, (here, value) in enumerate(values):
                total = total + fold_tiles(here * value)
                parts.append(fraction[row * group + g] * value)
            local_table[n, pl.ds(row, 1), :] = tile_sums(parts)
            return total

        return emit

    def emit_field(result):
        def emit(row, values, total):
            for g, (here, value) in enumerate(values):
                result[row * group + g] = value
            return total

        return emit

    def coarse_totals(phase):
        arrived(row_recv.at[phase], row_recv_sem.at[phase])
        return scatter_rows(lambda row: row_recv[phase, row], recv_ref, recv_hot, blocks)

    def sweep_first(phase, totals):
        both = block_products(totals, couplings_split)
        pushed = jnp.concatenate(
            [both[:, k * 128 : (k + 1) * 128] for k in range(couplings.shape[1])], axis=0
        )
        upper, lower = split_two(pushed)
        out_values = lax.dot_general(
            spread, upper.astype(BF16), NN, preferred_element_type=F32
        ) + lax.dot_general(spread, lower.astype(BF16), NN, preferred_element_type=F32)
        link_send[1 + phase] = out_values.reshape(devices, SLOT, 128)
        link_exchange(1 + phase)

    def sweep_second(phase, totals, gather_in):
        arrived(link_recv.at[1 + phase], link_recv_sem.at[1 + phase])
        values = stack_two(link_recv[1 + phase].reshape(devices * SLOT, 128), axis=1)
        summed = lax.dot_general(gather_in, values, NN, preferred_element_type=F32)
        coupled = summed[:, :128] + summed[:, 128:]
        sweep_two = block_products(totals - coupled, inverse_split)

        def store(row, value):
            side_send[phase, row + count_y, 0] = value
            side_send[phase, row, 1] = value
            side_send[phase, row + 2 * count_y, 2] = value
            side_send[phase, row + count_y - 1, 3] = value
            side_send[phase, row + count_y + 1, 4] = value

        gather_rows(sweep_two, recv_ref, recv_hot, store)

        def one(step, carry):
            device, other = peer(step)
            pltpu.make_async_remote_copy(
                src_ref=side_send.at[phase, other + count_y],
                dst_ref=side_recv.at[phase, :, me],
                send_sem=spread_send_sem.at[phase],
                recv_sem=spread_recv_sem.at[phase],
                device_id=device,
                device_id_type=MESH,
            ).start()
            return carry

        lax.fori_loop(1, devices, one, 0)
        side_recv[phase, :, me] = side_send[phase, me + count_y]

    def spread_done(phase, sem):
        part = side_recv.at[phase, :, pl.ds(0, devices - 1)]
        pltpu.make_async_copy(part, part, sem).wait()

    def tile_values(phase):
        spread_done(phase, spread_recv_sem.at[phase])

        def store(row, value):
            values_table[phase, pl.ds(row, 1), :] = value

        def rows_of(n):
            return side_recv[phase, n].reshape(devices, 128)

        gather_rows(rows_of(0), back_map, back_hot, store)
        beside = []
        gather_rows(
            jnp.concatenate([rows_of(1 + n) for n in range(4)], axis=0),
            side_map,
            side_hot,
            lambda row, value: beside.append(value),
        )
        packed = jnp.broadcast_to(beside[1], (table_rows, 128))
        high_y = pltpu.roll(packed, size_y - table_rows, 1, stride=1, stride_axis=0)
        low_y = pltpu.roll(packed, 1, 1, stride=1, stride_axis=0)
        beside_table[phase] = jnp.where(slot_y == 0, low_y, high_y)
        beside_row[phase] = beside[0]
        return beside[0], low_y, high_y

    def spread_tiles(row):
        return jnp.broadcast_to(row, (128, 128)).T

    def make_field(phase):
        n = 2 * phase + 1
        field, plus = fields[n], fields[2 * phase]

        def tile_part(stacked, g, first, count):
            return jnp.concatenate(
                [
                    stacked[
                        (k * group + g) * size_y + first : (k * group + g) * size_y + first + count
                    ]
                    for k in range(tiles_z)
                ],
                axis=1,
            )

        def step(row, carry):
            stacked = spread_tiles(values_table[phase, pl.ds(row, 1), :])
            beside = spread_tiles(beside_table[phase, pl.ds(row, 1), :])
            for g in range(group):
                x = row * group + g
                field[x] = fraction[x] * tile_part(stacked, g, 0, size_y) + plus[x]
                for side in range(2):
                    value = tile_part(beside, g, side * (size_y - 1), 1)
                    halo_y[n, side, x] = halo_fy[side, x] * value + halo_y[n - 1, side, x]
            return carry

        lax.fori_loop(0, table_rows, step, 0)
        stacked = spread_tiles(beside_row[phase])
        for side, g in ((0, group - 1), (1, 0)):
            value = tile_part(stacked, g, 0, size_y)
            halo_x[n, side] = halo_fx[side] * value + halo_x[n - 1, side]

    def tile_operator(phase, beside_x, low_y, high_y):
        table = values_table[phase]
        return (
            stencil_table[0] * table
            - (
                stencil_table[1] * next_x(table, beside_x)
                + stencil_table[2] * last_x(table, beside_x)
            )
            - (
                stencil_table[3] * next_y(table, high_y)
                + stencil_table[4] * last_y(table, low_y)
            )
            - (stencil_table[5] * next_z(table) + stencil_table[6] * last_z(table))
        )

    def start_sums(phase, values):
        row = jnp.zeros((1, 128), F32)
        for n, value in enumerate(values):
            row = jnp.where(place == n, value, row)
        sum_send[phase, 0] = row
        exchange(
            sum_send.at[phase],
            sum_recv.at[phase],
            sum_send_sem.at[phase],
            sum_recv_sem.at[phase],
            same=True,
        )

    def end_sums(phase, count):
        arrived(sum_recv.at[phase], sum_recv_sem.at[phase])
        totals = [sum_recv[phase, n] for n in range(4)]
        for n in range(4, devices):
            totals[n % 4] = totals[n % 4] + sum_recv[phase, n]
        total = (totals[0] + totals[1]) + (totals[2] + totals[3])
        return [
            jnp.sum(jnp.where(place == n, total, 0.0), axis=1, keepdims=True)
            for n in range(count)
        ]

    waits = [early, table_copies(1, [(side, code_table) for side in range(4)])]
    start(waits[1])
    totals = coarse_totals(0)
    sweep_first(0, totals)

    loads[4].wait()
    came_in(early)
    lower, total = lax.fori_loop(
        0,
        table_rows - 1,
        lambda row, s: prepare(row, s[0], None, s[1]),
        (low_mx[...], zero_tile),
    )
    _, total = prepare(table_rows - 1, lower, halo_fx[1], total)
    source_local = jnp.sum(total)
    waits.append(halo_copies(0))
    start(waits[2])
    waits.append(table_copies(0, ((1, stencil_table.at[1]), (3, stencil_table.at[3]))))
    start(waits[3])
    arrived(link_recv.at[0], link_recv_sem.at[0])
    names = link_recv[0].reshape(devices * SLOT, 128).T[:blocks]
    gather_in = jnp.where(
        names == iota((blocks, devices * SLOT), 0).astype(F32), 1.0, 0.0
    ).astype(BF16)

    sweep_second(0, totals, gather_in)

    write_one_hots(back_map, back_hot)
    came_in(waits[1])
    across_y, across_g = slot_y[:1], slot_g[:1]
    code_x = jnp.where(
        across_g == 0,
        table_halo[1, 0, 0:1],
        jnp.where(across_g == group - 1, table_halo[1, 1, table_rows - 1 :], -1.0),
    )
    code_y = jnp.full((1, 128), -1.0, F32)
    for r in range(table_rows):
        high = turn(table_halo[1, 2, r : r + 1], table_rows - 1 - r)
        low = turn(table_halo[1, 3, r : r + 1], -size_y - r)
        code_y = jnp.where(across_y == table_rows - 1 - r, high, code_y)
        code_y = jnp.where(across_y == size_y - 1 - r, low, code_y)
    span = devices * 128
    code_x, code_y = code_x.astype(jnp.int32), code_y.astype(jnp.int32)
    shift_x = jnp.where(across_g == 0, 0, span)
    shift_y = jnp.where(across_y < table_rows, 2 * span, 3 * span)
    side_map[0:1] = jnp.where(code_x < 0, -1, code_x + shift_x)
    side_map[1:2] = jnp.where(code_y < 0, -1, code_y + shift_y)
    write_one_hots(side_map, side_hot)
    came_in(waits[3])
    stencil_table[2] = last_x(stencil_table[1], table_halo[0, 1, table_rows - 1 :])
    stencil_table[4] = last_y(stencil_table[3], turn(table_halo[0, 3], 1 - size_y))
    stencil_table[6] = last_z(stencil_table[5])
    came_in(waits[2])
    local_energy = apply_operator(0, emit_local(0))

    beside = tile_values(0)
    operated = tile_operator(0, *beside)
    image_totals = operated + local_table[0]
    totals_table[1] = image_totals
    gather_rows(image_totals, send_map, send_hot, to_owners(1))
    row_exchange(1)
    values = values_table[0]
    rz_part = jnp.sum(totals_table[0] * values) + source_local
    energy_part = jnp.sum(values * (image_totals + local_table[0])) + local_energy
    start_sums(0, (rz_part, energy_part))

    make_field(0)

    rz, energy = end_sums(0, 2)
    alpha = rz / energy
    totals = totals - alpha * coarse_totals(1)
    sweep_first(1, totals)

    apply_operator(1, emit_field(image))

    def update(x, carry):
        own, cross = carry
        pushed = image[x]
        here = res[x] - alpha * pushed
        value = inv_diag[x] * here
        res[x] = here
        local_two[x] = value
        keep_edges(1, x, value)
        return own + fold_tiles(here * value), cross + fold_tiles(value * pushed)

    own, cross = lax.fori_loop(0, size_x, update, (zero_tile, zero_tile))
    residual_local, cross_local = jnp.sum(own), jnp.sum(cross)
    waits.append(halo_copies(1))
    start(waits[4])

    sweep_second(1, totals, gather_in)

    came_in(waits[4])
    local_energy = apply_operator(2, emit_local(1))

    beside = tile_values(1)
    operated = tile_operator(1, *beside)
    values = values_table[1]
    tile_totals = totals_table[0] - alpha * totals_table[1]
    next_part = jnp.sum(tile_totals * values) + residual_local
    own_part = jnp.sum(values * (operated + 2.0 * local_table[1])) + local_energy
    cross_part = jnp.sum(values * totals_table[1]) + cross_local
    start_sums(1, (next_part, own_part, cross_part))

    make_field(1)
    apply_operator(3, emit_field(image_two))

    rz_next, own, cross = end_sums(1, 3)
    beta = rz_next / rz
    alpha_two = rz_next / (own + beta * (2.0 * cross + beta * energy))

    for ref, value in ((gain_ref, alpha), (gain_two_ref, alpha_two), (mix_ref, beta)):
        ref[...] = jnp.broadcast_to(value, ref.shape)
    for copies in waits:
        for there, came, copy in copies:
            pl.when(there)(copy.wait_send)
    for n in range(2):
        arrived(row_send.at[n], row_send_sem.at[n])
        spread_done(n, spread_send_sem.at[n])
    for n in range(3):
        arrived(link_send.at[n], link_send_sem.at[n])
    for n in range(2):
        arrived(sum_recv.at[n], sum_send_sem.at[n])


def body(
    source_term,
    mobility_x,
    mobility_y,
    mobility_z,
    bubble_fraction,
    tile_labels,
    send_tiles,
    recv_rows,
    block_inverse,
    couplings,
    neighbours,
):
    count_x, count_y = lax.axis_size("gx"), lax.axis_size("gy")
    devices = count_x * count_y
    size_x, size_y, depth = source_term.shape
    tiles = size_x * size_y * (depth // TZ)
    blocks, order = block_inverse.shape[:2]
    send, recv = send_tiles[0], recv_rows[0]
    pad = 128 - send.shape[1]
    assert order == 128 and pad >= 0
    if pad:
        send = jnp.pad(send, ((0, 0), (0, pad)), constant_values=tiles)
        recv = jnp.pad(recv, ((0, 0), (0, pad)), constant_values=blocks * order)
    table_rows = tiles // 128
    field = (size_x, size_y, depth)
    hbm = pl.BlockSpec(memory_space=pltpu.HBM)
    vmem = pl.BlockSpec(memory_space=pltpu.VMEM)
    dma = pltpu.SemaphoreType.DMA
    res, direction, zed, image, image_two, *gains = pl.pallas_call(
        functools.partial(kernel, (count_x, count_y)),
        out_shape=(*[pltpu.VMEM(field, F32)] * 5, *[pltpu.VMEM((1, depth), F32)] * 3),
        in_specs=[hbm] * 7 + [vmem] * 3,
        out_specs=(vmem,) * 8,
        scratch_shapes=[
            *[pltpu.VMEM(field, F32)] * 4,
            pltpu.VMEM((blocks, order, order), F32),
            pltpu.VMEM(couplings.shape, F32),
            *[pltpu.VMEM(field, F32)] * 3,
            pltpu.VMEM((blocks, order, 2 * order), BF16),
            pltpu.VMEM((blocks, order * couplings.shape[1], 2 * order), BF16),
            pltpu.VMEM((devices // GROUP, 128, GROUP * 128), BF16),
            pltpu.VMEM((devices // GROUP, 128, GROUP * 128), BF16),
            pltpu.VMEM((table_rows // GROUP, 128, GROUP * 128), BF16),
            pltpu.VMEM((1, 128, 2 * 128), BF16),
            pltpu.VMEM((devices, 128), jnp.int32),
            pltpu.VMEM((table_rows, 128), jnp.int32),
            pltpu.VMEM((2, 128), jnp.int32),
            pltpu.VMEM((2, table_rows, 128), F32),
            pltpu.VMEM((2, table_rows, 128), F32),
            pltpu.VMEM((2, table_rows, 128), F32),
            pltpu.VMEM((7, table_rows, 128), F32),
            pltpu.VMEM((table_rows, 128), F32),
            pltpu.VMEM((2, table_rows, 128), F32),
            pltpu.VMEM((2, 1, 128), F32),
            pltpu.VMEM((2, 4, table_rows, 128), F32),
            pltpu.VMEM((size_y, depth), F32),
            pltpu.VMEM((size_x, 1, depth), F32),
            pltpu.VMEM((size_x, 1, depth), F32),
            pltpu.VMEM((2, size_x, 1, depth), F32),
            pltpu.VMEM((2, size_y, depth), F32),
            pltpu.VMEM((2, size_x, 1, depth), F32),
            pltpu.VMEM((2, 2, size_x, 1, depth), F32),
            pltpu.VMEM((4, 2, size_y, depth), F32),
            pltpu.VMEM((4, 2, size_x, 1, depth), F32),
            pltpu.VMEM((2, devices, 1, 128), F32),
            pltpu.VMEM((2, devices, 1, 128), F32),
            pltpu.VMEM((2, devices + 2 * count_y, 5, 1, 128), F32),
            pltpu.VMEM((2, 5, devices, 1, 128), F32),
            pltpu.VMEM((3, devices, SLOT, 128), F32),
            pltpu.VMEM((3, devices, SLOT, 128), F32),
            pltpu.VMEM((2, 1, 1, 128), F32),
            pltpu.VMEM((2, devices, 1, 128), F32),
            dma((7,)),
            dma((2, 4)),
            dma((2, 4)),
            dma((6,)),
            dma((6,)),
            dma((2, 4)),
            dma((2, 4)),
            dma((2,)),
            dma((2,)),
            dma((2,)),
            dma((2,)),
            dma((3,)),
            dma((3,)),
            dma((2,)),
            dma((2,)),
        ],
        compiler_params=pltpu.CompilerParams(
            collective_id=0, has_side_effects=True, vmem_limit_bytes=61000000
        ),
    )(
        source_term,
        mobility_x,
        mobility_y,
        mobility_z,
        bubble_fraction,
        block_inverse,
        couplings,
        send,
        recv,
        neighbours.T,
    )
    alpha, alpha_two, beta = [
        lax.broadcast_in_dim(g.reshape(depth), field, (2,)) for g in gains
    ]
    return (
        alpha * direction + alpha_two * (zed + beta * direction),
        res - alpha_two * (image_two + beta * image),
    )


def solution(mesh):
    return jax.shard_map(
        body,
        mesh=mesh,
        in_specs=(
            P("gx", "gy", None),
            P("gx", "gy", None),
            P("gx", "gy", None),
            P("gx", "gy", None),
            P("gx", "gy", None),
            P("gx", "gy", None),
            P(("gx", "gy"), None, None),
            P(("gx", "gy"), None, None),
            P(("gx", "gy"), None, None),
            P(("gx", "gy"), None, None, None),
            P(("gx", "gy"), None),
        ),
        out_specs=(P("gx", "gy", None), P("gx", "gy", None)),
        check_vma=False,
    )
```

```python
import functools

import jax
import jax.numpy as jnp
from jax import lax
from jax.experimental import pallas as pl
from jax.experimental.pallas import tpu as pltpu
from jax.sharding import PartitionSpec as P

TZ = 128
LINK = 4
SLOT = 4
F32 = jnp.float32
BF16 = jnp.bfloat16
MESH = pl.DeviceIdType.MESH
NT = (((1,), (1,)), ((), ()))
NN = (((1,), (0,)), ((), ()))
GROUP = 8


def log2(value):
    assert value & (value - 1) == 0
    return value.bit_length() - 1


def iota(shape, axis):
    return lax.broadcasted_iota(jnp.int32, shape, axis)


def split_two(value):
    first = value.astype(BF16).astype(F32)
    return first, (value - first).astype(BF16).astype(F32)


def stack_two(value, axis=0):
    return jnp.concatenate(split_two(value), axis=axis).astype(BF16)


def fold_two(value):
    half = value.shape[0] // 2
    return value[:half] + value[half:]


def fold_tiles(value):
    tiles = [
        value[y : y + 8, z : z + 128]
        for y in range(0, value.shape[0], 8)
        for z in range(0, value.shape[1], 128)
    ]
    while len(tiles) > 1:
        tiles = [a + b for a, b in zip(tiles[::2], tiles[1::2])]
    return tiles[0]


def write_one_hots(index_ref, hot_ref):
    group = hot_ref.shape[2] // 128

    def step(block, carry):
        for sub in range(group):
            index = index_ref[pl.ds(block * group + sub, 1), :]
            hot = jnp.where(iota((128, 128), 0) == (index & 127), 1.0, 0.0)
            hot_ref[block, :, sub * 128 : (sub + 1) * 128] = hot.astype(BF16)
        return carry

    lax.fori_loop(0, hot_ref.shape[0], step, 0)


def in_chunks(count, step, carry, chunk=4):
    chunk = max(c for c in range(1, chunk + 1) if count % c == 0)

    def chunk_step(n, carry):
        for sub in range(chunk):
            carry = step(n * chunk + sub, carry)
        return carry

    if count == chunk:
        return chunk_step(0, carry)
    return lax.fori_loop(0, count // chunk, chunk_step, carry)


def gather_rows(table, index_ref, hot_ref, store):
    parts = stack_two(table)
    high_count = table.shape[0]
    group = hot_ref.shape[2] // 128

    def step(block, carry):
        picked = fold_two(
            lax.dot_general(parts, hot_ref[block], NN, preferred_element_type=F32)
        )
        for sub in range(group):
            row = block * group + sub
            hit = iota((high_count, 128), 0) == (index_ref[pl.ds(row, 1), :] >> 7)
            mine = picked[:, sub * 128 : (sub + 1) * 128]
            store(row, jnp.sum(jnp.where(hit, mine, 0.0), axis=0, keepdims=True))
        return carry

    in_chunks(hot_ref.shape[0], step, 0)


def scatter_rows(value_of, index_ref, hot_ref, high_count):
    group = hot_ref.shape[2] // 128

    def step(block, total):
        pieces = []
        for sub in range(group):
            row = block * group + sub
            hit = iota((high_count, 128), 0) == (index_ref[pl.ds(row, 1), :] >> 7)
            pieces.append(
                jnp.concatenate(
                    [jnp.where(hit, part, 0.0) for part in split_two(value_of(row))], axis=0
                ).astype(BF16)
            )
        return total + lax.dot_general(
            jnp.concatenate(pieces, axis=1), hot_ref[block], NT, preferred_element_type=F32
        )

    start = jnp.zeros((2 * high_count, 128), F32)
    return fold_two(in_chunks(hot_ref.shape[0], step, start))


def block_vectors(vectors):
    first, second = split_two(vectors)
    out = []
    for q in range(vectors.shape[0]):
        mine = iota(vectors.shape, 0) == q
        top = jnp.where(mine, first, 0.0)
        low = jnp.where(mine, second, 0.0)
        upper = jnp.concatenate([top, top], axis=1)
        lower = jnp.concatenate([low, jnp.zeros_like(low)], axis=1)
        out.append(jnp.concatenate([upper, lower], axis=0).astype(BF16))
    return out


def block_products(vectors, split_ref):
    total = None
    for q, part in enumerate(block_vectors(vectors)):
        term = lax.dot_general(part, split_ref[q], NT, preferred_element_type=F32)
        total = term if total is None else total + term
    return fold_two(total)


def kernel(
    counts,
    source_hbm,
    mob_x_hbm,
    mob_y_hbm,
    mob_z_hbm,
    fraction_hbm,
    inverse_hbm,
    couplings_hbm,
    send_ref,
    recv_ref,
    near_ref,
    res,
    direction,
    zed,
    image,
    image_two,
    gain_ref,
    gain_two_ref,
    mix_ref,
    mob_x,
    mob_y,
    mob_z,
    fraction,
    inverse,
    couplings,
    inv_diag,
    local,
    local_two,
    inverse_split,
    couplings_split,
    send_hot,
    recv_hot,
    back_hot,
    side_hot,
    send_map,
    back_map,
    side_map,
    totals_table,
    values_table,
    local_table,
    stencil_table,
    code_table,
    beside_table,
    beside_row,
    table_halo,
    low_mx,
    low_my,
    edge_my,
    edge_f,
    halo_fx,
    halo_fy,
    edges,
    halo_x,
    halo_y,
    row_send,
    row_recv,
    side_send,
    side_recv,
    link_send,
    link_recv,
    sum_send,
    sum_recv,
    load_sem,
    side_send_sem,
    side_recv_sem,
    early_send_sem,
    early_recv_sem,
    table_send_sem,
    table_recv_sem,
    row_send_sem,
    row_recv_sem,
    spread_send_sem,
    spread_recv_sem,
    link_send_sem,
    link_recv_sem,
    sum_send_sem,
    sum_recv_sem,
):
    count_x, count_y = counts
    devices = count_x * count_y
    at_x, at_y = lax.axis_index("gx"), lax.axis_index("gy")
    me = at_x * count_y + at_y
    size_x, size_y, depth = res.shape
    tiles_z = depth // TZ
    group = 128 // (size_y * tiles_z)
    table_rows = size_x // group
    blocks = inverse.shape[0]
    push_count = near_ref.size

    loads = [
        pltpu.make_async_copy(src, dst, load_sem.at[n])
        for n, (src, dst) in enumerate(
            (
                (source_hbm, res),
                (fraction_hbm, fraction),
                (mob_y_hbm, mob_y),
                (mob_x_hbm, mob_x),
                (mob_z_hbm, mob_z),
                (inverse_hbm, inverse),
                (couplings_hbm, couplings),
            )
        )
    ]
    for load in loads:
        load.start()

    barrier = pltpu.get_barrier_semaphore()

    def peer(step):
        other = lax.rem(me + step, devices)
        return (other // count_y, lax.rem(other, count_y)), other

    def greet(step, carry):
        pl.semaphore_signal(barrier, inc=1, device_id=peer(step)[0], device_id_type=MESH)
        return carry

    for ref in (low_mx, low_my, halo_fx, halo_fy, halo_x, halo_y, side_send):
        ref[...] = jnp.zeros_like(ref)
    table_halo[0] = jnp.zeros_like(table_halo[0])
    table_halo[1] = jnp.full_like(table_halo[1], -1.0)
    lax.fori_loop(1, devices, greet, 0)

    def exchange(send, recv, send_sem, recv_sem, same=False):
        def one(step, carry):
            device, other = peer(step)
            pltpu.make_async_remote_copy(
                src_ref=send.at[0 if same else other],
                dst_ref=recv.at[me],
                send_sem=send_sem,
                recv_sem=recv_sem,
                device_id=device,
                device_id_type=MESH,
            ).start()
            return carry

        lax.fori_loop(1, devices, one, 0)
        recv[me] = send[0 if same else me]

    def arrived(recv, recv_sem):
        part = recv.at[pl.ds(0, devices - 1)]
        pltpu.make_async_copy(part, part, recv_sem).wait()

    tile = send_ref[...]
    low = tile & 127
    tile_k = low & (tiles_z - 1)
    tile_j = (low >> log2(tiles_z)) & (size_y - 1)
    tile_g = low >> log2(tiles_z * size_y)
    send_map[...] = (
        (tile - low) + tile_k * (group * size_y) + tile_g * size_y + tile_j
    )

    def tile_sums(planes):
        stacked = jnp.concatenate(
            [plane[:, k * TZ : (k + 1) * TZ] for k in range(tiles_z) for plane in planes],
            axis=0,
        )
        return jnp.sum(stacked.T, axis=0, keepdims=True)

    def row_exchange(n):
        exchange(row_send.at[n], row_recv.at[n], row_send_sem.at[n], row_recv_sem.at[n])

    write_one_hots(send_map, send_hot)
    loads[0].wait()
    loads[1].wait()

    def first_totals(row, carry):
        xs = [row * group + g for g in range(group)]
        totals_table[0, pl.ds(row, 1), :] = tile_sums([fraction[x] * res[x] for x in xs])
        return carry

    in_chunks(table_rows, first_totals, 0)
    def to_owners(n):
        def store(row, value):
            row_send[n, row] = value

        return store

    gather_rows(totals_table[0], send_map, send_hot, to_owners(0))
    pl.semaphore_wait(barrier, devices - 1)
    row_exchange(0)

    def side_copy(src, dst, send_sem, recv_sem, shift_x, shift_y):
        return pltpu.make_async_remote_copy(
            src_ref=src,
            dst_ref=dst,
            send_sem=send_sem,
            recv_sem=recv_sem,
            device_id=(at_x + shift_x, at_y + shift_y),
            device_id_type=MESH,
        )

    has_low_x, has_high_x = at_x > 0, at_x < count_x - 1
    has_low_y, has_high_y = at_y > 0, at_y < count_y - 1
    sides = (
        (has_low_x, has_high_x, -1, 0),
        (has_high_x, has_low_x, 1, 0),
        (has_low_y, has_high_y, 0, -1),
        (has_high_y, has_low_y, 0, 1),
    )

    def side_group(parts, send_sem, recv_sem):
        out = []
        for n, (side, src, dst) in enumerate(parts):
            there, came, shift_x, shift_y = sides[side]
            copy = side_copy(src, dst, send_sem.at[n], recv_sem.at[n], shift_x, shift_y)
            out.append((there, came, copy))
        return out

    def start(copies):
        for there, came, copy in copies:
            pl.when(there)(copy.start)

    def came_in(copies):
        for there, came, copy in copies:
            pl.when(came)(copy.wait_recv)

    loads[2].wait()
    loads[3].wait()

    def take_edge(x, carry):
        edge_my[x] = mob_y[x, size_y - 1 : size_y, :]
        edge_f[0, x] = fraction[x, 0:1, :]
        edge_f[1, x] = fraction[x, size_y - 1 : size_y, :]
        return carry

    lax.fori_loop(0, size_x, take_edge, 0)
    early = side_group(
        (
            (1, mob_x.at[size_x - 1], low_mx),
            (3, edge_my, low_my),
            (0, fraction.at[0], halo_fx.at[1]),
            (1, fraction.at[size_x - 1], halo_fx.at[0]),
            (2, edge_f.at[0], halo_fy.at[1]),
            (3, edge_f.at[1], halo_fy.at[0]),
        ),
        early_send_sem,
        early_recv_sem,
    )
    start(early)

    near_row = jnp.concatenate([near_ref[k : k + 1] for k in range(near_ref.shape[0])], axis=1)
    target_row = near_row >> log2(blocks)
    down, across = iota((push_count, push_count), 0), iota((push_count, push_count), 1)
    target_col = jnp.sum(
        jnp.where(down == across, target_row.astype(F32), 0.0), axis=1, keepdims=True
    ).astype(jnp.int32)
    earlier = down < across
    same = jnp.where((target_row == target_col) & earlier, 1, 0)
    rank = jnp.sum(same, axis=0, keepdims=True)
    slot = target_row * SLOT + rank
    chosen = iota((devices * SLOT, push_count), 0) == slot
    local_block = (near_row & (blocks - 1)).astype(F32)
    identity = jnp.sum(jnp.where(chosen, local_block, 0.0), axis=1, keepdims=True)
    link_send[0] = jnp.broadcast_to(identity, (devices * SLOT, 128)).reshape(
        devices, SLOT, 128
    )
    spread = jnp.where(chosen, 1.0, 0.0).astype(BF16)

    def link_exchange(n):
        exchange(link_send.at[n], link_recv.at[n], link_send_sem.at[n], link_recv_sem.at[n])

    link_exchange(0)

    lane = iota((size_y, depth), 1)
    row_of = iota((size_y, depth), 0)

    def below_z(plane):
        return jnp.where(lane == 0, 0.0, pltpu.roll(plane, 1, 1))

    def above_z(plane):
        return jnp.where(lane == depth - 1, 0.0, pltpu.roll(plane, depth - 1, 1))

    def below_y(plane, edge):
        return jnp.where(row_of == 0, edge, pltpu.roll(plane, 1, 0))

    def above_y(plane, edge):
        return jnp.where(row_of == size_y - 1, edge, pltpu.roll(plane, size_y - 1, 0))

    wide = group * size_y
    slot_of = iota((table_rows, 128), 1)
    slot_y = slot_of & (size_y - 1)
    slot_g = (slot_of >> log2(size_y)) & (group - 1)
    slot_k = slot_of >> log2(wide)

    def turn(table, shift):
        return pltpu.roll(table, shift % 128, 1) if shift % 128 else table

    def next_x(table, high):
        inner = turn(table, -size_y)
        outer = turn(jnp.concatenate([table[1:], high], axis=0), (group - 1) * size_y)
        return jnp.where(slot_g < group - 1, inner, outer)

    def last_x(table, low):
        inner = turn(table, size_y)
        outer = turn(
            jnp.concatenate([low, table[: table_rows - 1]], axis=0), -(group - 1) * size_y
        )
        return jnp.where(slot_g > 0, inner, outer)

    def next_y(table, high):
        return jnp.where(slot_y < size_y - 1, turn(table, -1), high)

    def last_y(table, low):
        return jnp.where(slot_y > 0, turn(table, 1), low)

    def next_z(table):
        return jnp.where(slot_k < tiles_z - 1, turn(table, -wide), 0.0)

    def last_z(table):
        return jnp.where(slot_k > 0, turn(table, wide), 0.0)

    write_one_hots(recv_ref, recv_hot)
    loads[5].wait()

    def split_inverse(q, carry):
        inverse_split[q] = stack_two(inverse[q], axis=1)
        return carry

    in_chunks(blocks, split_inverse, 0)
    loads[6].wait()

    def fold_couplings(q, carry):
        both = jnp.concatenate([couplings[q, k] for k in range(couplings.shape[1])], axis=0)
        upper, lower = split_two(both)
        top, rest = split_two(inverse[q])
        product = lax.dot_general(
            jnp.concatenate([upper, upper, lower], axis=1).astype(BF16),
            jnp.concatenate([top, rest, top], axis=0).astype(BF16),
            NN,
            preferred_element_type=F32,
        )
        couplings_split[q] = stack_two(product, axis=1)
        return carry

    in_chunks(blocks, fold_couplings, 0)

    place = iota((1, 128), 1)
    codes = scatter_rows(
        lambda row: (row * 128 + place).astype(F32), send_map, send_hot, table_rows
    )
    code_table[...] = codes
    back_map[...] = codes.astype(jnp.int32)

    zero_tile = jnp.zeros((8, 128), F32)
    fields = (local, direction, local_two, zed)

    def keep_edges(phase, x, value):
        edges[phase, 0, x] = value[0:1]
        edges[phase, 1, x] = value[size_y - 1 : size_y]

    def halo_copies(phase):
        field = fields[2 * phase]
        return side_group(
            (
                (0, field.at[0], halo_x.at[2 * phase, 1]),
                (1, field.at[size_x - 1], halo_x.at[2 * phase, 0]),
                (2, edges.at[phase, 0], halo_y.at[2 * phase, 1]),
                (3, edges.at[phase, 1], halo_y.at[2 * phase, 0]),
            ),
            side_send_sem.at[phase],
            side_recv_sem.at[phase],
        )

    def prepare(row, lower, above, total):
        whole, across_x, across_y, across_z = [], [], [], []
        for g in range(group):
            x = row * group + g
            mob_a, mob_b, mob_c = mob_x[x], mob_y[x], mob_z[x]
            weight, source = fraction[x], res[x]
            diagonal = (
                (mob_a + lower) + (mob_b + below_y(mob_b, low_my[x])) + (mob_c + below_z(mob_c))
            )
            inverse_here = 1.0 / diagonal
            value = source * inverse_here
            inv_diag[x] = inverse_here
            local[x] = value
            keep_edges(0, x, value)
            total = total + fold_tiles(source * value)
            up = fraction[x + 1] if g < group - 1 or above is None else above
            whole.append(diagonal * (weight * weight))
            across_x.append(mob_a * weight * up)
            across_y.append(mob_b * weight * above_y(weight, halo_fy[1, x]))
            across_z.append(mob_c * weight * above_z(weight))
            lower = mob_a
        here = pl.ds(row, 1)
        stencil_table[1, here, :] = tile_sums(across_x)
        stencil_table[3, here, :] = tile_sums(across_y)
        turned = jnp.concatenate(
            [p[:, k * TZ : (k + 1) * TZ] for k in range(tiles_z) for p in across_z], axis=0
        ).T
        crossing = turned[TZ - 1 : TZ]
        inside = jnp.sum(turned, axis=0, keepdims=True) - crossing
        stencil_table[5, here, :] = crossing
        stencil_table[0, here, :] = tile_sums(whole) - 2.0 * inside
        return lower, total

    def table_copies(n, pairs):
        return side_group(
            [(side, src, table_halo.at[n, side]) for side, src in pairs],
            table_send_sem.at[n],
            table_recv_sem.at[n],
        )

    def apply_operator(phase, emit):
        field = fields[phase]

        def group_step(row, here, flux_low, carry, top):
            values = []
            for g in range(group):
                x = row * group + g
                above = top if top is not None and g == group - 1 else field[x + 1]
                flux_x = mob_x[x] * (above - here)
                flux_y = mob_y[x] * (above_y(here, halo_y[phase, 1, x]) - here)
                edge = low_my[x] * (here[0:1] - halo_y[phase, 0, x])
                flux_z = mob_z[x] * (above_z(here) - here)
                value = (
                    (flux_low - flux_x)
                    + (below_y(flux_y, edge) - flux_y)
                    + (below_z(flux_z) - flux_z)
                )
                values.append((here, value))
                here, flux_low = above, flux_x
            return here, flux_low, emit(row, values, carry)

        first = field[0]
        flux = low_mx[...] * (first - halo_x[phase, 0])
        state = (first, flux, zero_tile)
        state = in_chunks(table_rows - 1, lambda row, s: group_step(row, *s, None), state, 3)
        return jnp.sum(group_step(table_rows - 1, *state, halo_x[phase, 1])[2])

    def emit_local(n):
        def emit(row, values, total):
            parts = []
            for g, (here, value) in enumerate(values):
                total = total + fold_tiles(here * value)
                parts.append(fraction[row * group + g] * value)
            local_table[n, pl.ds(row, 1), :] = tile_sums(parts)
            return total

        return emit

    def emit_field(result):
        def emit(row, values, total):
            for g, (here, value) in enumerate(values):
                result[row * group + g] = value
            return total

        return emit

    def coarse_totals(phase):
        arrived(row_recv.at[phase], row_recv_sem.at[phase])
        return scatter_rows(lambda row: row_recv[phase, row], recv_ref, recv_hot, blocks)

    def sweep_first(phase, totals):
        both = block_products(totals, couplings_split)
        pushed = jnp.concatenate(
            [both[:, k * 128 : (k + 1) * 128] for k in range(couplings.shape[1])], axis=0
        )
        upper, lower = split_two(pushed)
        out_values = lax.dot_general(
            spread, upper.astype(BF16), NN, preferred_element_type=F32
        ) + lax.dot_general(spread, lower.astype(BF16), NN, preferred_element_type=F32)
        link_send[1 + phase] = out_values.reshape(devices, SLOT, 128)
        link_exchange(1 + phase)

    def sweep_second(phase, totals, gather_in):
        arrived(link_recv.at[1 + phase], link_recv_sem.at[1 + phase])
        values = stack_two(link_recv[1 + phase].reshape(devices * SLOT, 128), axis=1)
        summed = lax.dot_general(gather_in, values, NN, preferred_element_type=F32)
        coupled = summed[:, :128] + summed[:, 128:]
        sweep_two = block_products(totals - coupled, inverse_split)

        def store(row, value):
            side_send[phase, row + count_y, 0] = value
            side_send[phase, row, 1] = value
            side_send[phase, row + 2 * count_y, 2] = value
            side_send[phase, row + count_y - 1, 3] = value
            side_send[phase, row + count_y + 1, 4] = value

        gather_rows(sweep_two, recv_ref, recv_hot, store)

        def one(step, carry):
            device, other = peer(step)
            pltpu.make_async_remote_copy(
                src_ref=side_send.at[phase, other + count_y],
                dst_ref=side_recv.at[phase, :, me],
                send_sem=spread_send_sem.at[phase],
                recv_sem=spread_recv_sem.at[phase],
                device_id=device,
                device_id_type=MESH,
            ).start()
            return carry

        lax.fori_loop(1, devices, one, 0)
        side_recv[phase, :, me] = side_send[phase, me + count_y]

    def spread_done(phase, sem):
        part = side_recv.at[phase, :, pl.ds(0, devices - 1)]
        pltpu.make_async_copy(part, part, sem).wait()

    def tile_values(phase):
        spread_done(phase, spread_recv_sem.at[phase])

        def store(row, value):
            values_table[phase, pl.ds(row, 1), :] = value

        def rows_of(n):
            return side_recv[phase, n].reshape(devices, 128)

        gather_rows(rows_of(0), back_map, back_hot, store)
        beside = []
        gather_rows(
            jnp.concatenate([rows_of(1 + n) for n in range(4)], axis=0),
            side_map,
            side_hot,
            lambda row, value: beside.append(value),
        )
        packed = jnp.broadcast_to(beside[1], (table_rows, 128))
        high_y = pltpu.roll(packed, size_y - table_rows, 1, stride=1, stride_axis=0)
        low_y = pltpu.roll(packed, 1, 1, stride=1, stride_axis=0)
        beside_table[phase] = jnp.where(slot_y == 0, low_y, high_y)
        beside_row[phase] = beside[0]
        return beside[0], low_y, high_y

    def spread_tiles(row):
        return jnp.broadcast_to(row, (128, 128)).T

    def make_field(phase):
        n = 2 * phase + 1
        field, plus = fields[n], fields[2 * phase]

        def tile_part(stacked, g, first, count):
            return jnp.concatenate(
                [
                    stacked[
                        (k * group + g) * size_y + first : (k * group + g) * size_y + first + count
                    ]
                    for k in range(tiles_z)
                ],
                axis=1,
            )

        def step(row, carry):
            stacked = spread_tiles(values_table[phase, pl.ds(row, 1), :])
            beside = spread_tiles(beside_table[phase, pl.ds(row, 1), :])
            for g in range(group):
                x = row * group + g
                field[x] = fraction[x] * tile_part(stacked, g, 0, size_y) + plus[x]
                for side in range(2):
                    value = tile_part(beside, g, side * (size_y - 1), 1)
                    halo_y[n, side, x] = halo_fy[side, x] * value + halo_y[n - 1, side, x]
            return carry

        in_chunks(table_rows, step, 0)
        stacked = spread_tiles(beside_row[phase])
        for side, g in ((0, group - 1), (1, 0)):
            value = tile_part(stacked, g, 0, size_y)
            halo_x[n, side] = halo_fx[side] * value + halo_x[n - 1, side]

    def tile_operator(phase, beside_x, low_y, high_y):
        table = values_table[phase]
        return (
            stencil_table[0] * table
            - (
                stencil_table[1] * next_x(table, beside_x)
                + stencil_table[2] * last_x(table, beside_x)
            )
            - (
                stencil_table[3] * next_y(table, high_y)
                + stencil_table[4] * last_y(table, low_y)
            )
            - (stencil_table[5] * next_z(table) + stencil_table[6] * last_z(table))
        )

    def start_sums(phase, values):
        row = jnp.zeros((1, 128), F32)
        for n, value in enumerate(values):
            row = jnp.where(place == n, value, row)
        sum_send[phase, 0] = row
        exchange(
            sum_send.at[phase],
            sum_recv.at[phase],
            sum_send_sem.at[phase],
            sum_recv_sem.at[phase],
            same=True,
        )

    def end_sums(phase, count):
        arrived(sum_recv.at[phase], sum_recv_sem.at[phase])
        totals = [sum_recv[phase, n] for n in range(4)]
        for n in range(4, devices):
            totals[n % 4] = totals[n % 4] + sum_recv[phase, n]
        total = (totals[0] + totals[1]) + (totals[2] + totals[3])
        return [
            jnp.sum(jnp.where(place == n, total, 0.0), axis=1, keepdims=True)
            for n in range(count)
        ]

    waits = [early, table_copies(1, [(side, code_table) for side in range(4)])]
    start(waits[1])
    totals = coarse_totals(0)
    sweep_first(0, totals)

    loads[4].wait()
    came_in(early)
    lower, total = in_chunks(
        table_rows - 1,
        lambda row, s: prepare(row, s[0], None, s[1]),
        (low_mx[...], zero_tile),
        3,
    )
    _, total = prepare(table_rows - 1, lower, halo_fx[1], total)
    source_local = jnp.sum(total)
    waits.append(halo_copies(0))
    start(waits[2])
    waits.append(table_copies(0, ((1, stencil_table.at[1]), (3, stencil_table.at[3]))))
    start(waits[3])
    arrived(link_recv.at[0], link_recv_sem.at[0])
    names = link_recv[0].reshape(devices * SLOT, 128).T[:blocks]
    gather_in = jnp.where(
        names == iota((blocks, devices * SLOT), 0).astype(F32), 1.0, 0.0
    ).astype(BF16)

    sweep_second(0, totals, gather_in)

    write_one_hots(back_map, back_hot)
    came_in(waits[1])
    across_y, across_g = slot_y[:1], slot_g[:1]
    code_x = jnp.where(
        across_g == 0,
        table_halo[1, 0, 0:1],
        jnp.where(across_g == group - 1, table_halo[1, 1, table_rows - 1 :], -1.0),
    )
    code_y = jnp.full((1, 128), -1.0, F32)
    for r in range(table_rows):
        high = turn(table_halo[1, 2, r : r + 1], table_rows - 1 - r)
        low = turn(table_halo[1, 3, r : r + 1], -size_y - r)
        code_y = jnp.where(across_y == table_rows - 1 - r, high, code_y)
        code_y = jnp.where(across_y == size_y - 1 - r, low, code_y)
    span = devices * 128
    code_x, code_y = code_x.astype(jnp.int32), code_y.astype(jnp.int32)
    shift_x = jnp.where(across_g == 0, 0, span)
    shift_y = jnp.where(across_y < table_rows, 2 * span, 3 * span)
    side_map[0:1] = jnp.where(code_x < 0, -1, code_x + shift_x)
    side_map[1:2] = jnp.where(code_y < 0, -1, code_y + shift_y)
    write_one_hots(side_map, side_hot)
    came_in(waits[3])
    stencil_table[2] = last_x(stencil_table[1], table_halo[0, 1, table_rows - 1 :])
    stencil_table[4] = last_y(stencil_table[3], turn(table_halo[0, 3], 1 - size_y))
    stencil_table[6] = last_z(stencil_table[5])
    came_in(waits[2])
    local_energy = apply_operator(0, emit_local(0))

    beside = tile_values(0)
    operated = tile_operator(0, *beside)
    image_totals = operated + local_table[0]
    totals_table[1] = image_totals
    gather_rows(image_totals, send_map, send_hot, to_owners(1))
    row_exchange(1)
    values = values_table[0]
    rz_part = jnp.sum(totals_table[0] * values) + source_local
    energy_part = jnp.sum(values * (image_totals + local_table[0])) + local_energy
    start_sums(0, (rz_part, energy_part))

    make_field(0)

    rz, energy = end_sums(0, 2)
    alpha = rz / energy
    totals = totals - alpha * coarse_totals(1)
    sweep_first(1, totals)

    apply_operator(1, emit_field(image))

    def update(x, carry):
        own, cross = carry
        pushed = image[x]
        here = res[x] - alpha * pushed
        value = inv_diag[x] * here
        res[x] = here
        local_two[x] = value
        keep_edges(1, x, value)
        return own + fold_tiles(here * value), cross + fold_tiles(value * pushed)

    own, cross = in_chunks(size_x, update, (zero_tile, zero_tile))
    residual_local, cross_local = jnp.sum(own), jnp.sum(cross)
    waits.append(halo_copies(1))
    start(waits[4])

    sweep_second(1, totals, gather_in)

    came_in(waits[4])
    local_energy = apply_operator(2, emit_local(1))

    beside = tile_values(1)
    operated = tile_operator(1, *beside)
    values = values_table[1]
    tile_totals = totals_table[0] - alpha * totals_table[1]
    next_part = jnp.sum(tile_totals * values) + residual_local
    own_part = jnp.sum(values * (operated + 2.0 * local_table[1])) + local_energy
    cross_part = jnp.sum(values * totals_table[1]) + cross_local
    start_sums(1, (next_part, own_part, cross_part))

    make_field(1)
    apply_operator(3, emit_field(image_two))

    rz_next, own, cross = end_sums(1, 3)
    beta = rz_next / rz
    alpha_two = rz_next / (own + beta * (2.0 * cross + beta * energy))

    for ref, value in ((gain_ref, alpha), (gain_two_ref, alpha_two), (mix_ref, beta)):
        ref[...] = jnp.broadcast_to(value, ref.shape)
    for copies in waits:
        for there, came, copy in copies:
            pl.when(there)(copy.wait_send)
    for n in range(2):
        arrived(row_send.at[n], row_send_sem.at[n])
        spread_done(n, spread_send_sem.at[n])
    for n in range(3):
        arrived(link_send.at[n], link_send_sem.at[n])
    for n in range(2):
        arrived(sum_recv.at[n], sum_send_sem.at[n])


def body(
    source_term,
    mobility_x,
    mobility_y,
    mobility_z,
    bubble_fraction,
    tile_labels,
    send_tiles,
    recv_rows,
    block_inverse,
    couplings,
    neighbours,
):
    count_x, count_y = lax.axis_size("gx"), lax.axis_size("gy")
    devices = count_x * count_y
    size_x, size_y, depth = source_term.shape
    tiles = size_x * size_y * (depth // TZ)
    blocks, order = block_inverse.shape[:2]
    send, recv = send_tiles[0], recv_rows[0]
    pad = 128 - send.shape[1]
    assert order == 128 and pad >= 0
    if pad:
        send = jnp.pad(send, ((0, 0), (0, pad)), constant_values=tiles)
        recv = jnp.pad(recv, ((0, 0), (0, pad)), constant_values=blocks * order)
    table_rows = tiles // 128
    field = (size_x, size_y, depth)
    hbm = pl.BlockSpec(memory_space=pltpu.HBM)
    vmem = pl.BlockSpec(memory_space=pltpu.VMEM)
    dma = pltpu.SemaphoreType.DMA
    res, direction, zed, image, image_two, *gains = pl.pallas_call(
        functools.partial(kernel, (count_x, count_y)),
        out_shape=(*[pltpu.VMEM(field, F32)] * 5, *[pltpu.VMEM((1, depth), F32)] * 3),
        in_specs=[hbm] * 7 + [vmem] * 3,
        out_specs=(vmem,) * 8,
        scratch_shapes=[
            *[pltpu.VMEM(field, F32)] * 4,
            pltpu.VMEM((blocks, order, order), F32),
            pltpu.VMEM(couplings.shape, F32),
            *[pltpu.VMEM(field, F32)] * 3,
            pltpu.VMEM((blocks, order, 2 * order), BF16),
            pltpu.VMEM((blocks, order * couplings.shape[1], 2 * order), BF16),
            pltpu.VMEM((devices // GROUP, 128, GROUP * 128), BF16),
            pltpu.VMEM((devices // GROUP, 128, GROUP * 128), BF16),
            pltpu.VMEM((table_rows // GROUP, 128, GROUP * 128), BF16),
            pltpu.VMEM((1, 128, 2 * 128), BF16),
            pltpu.VMEM((devices, 128), jnp.int32),
            pltpu.VMEM((table_rows, 128), jnp.int32),
            pltpu.VMEM((2, 128), jnp.int32),
            pltpu.VMEM((2, table_rows, 128), F32),
            pltpu.VMEM((2, table_rows, 128), F32),
            pltpu.VMEM((2, table_rows, 128), F32),
            pltpu.VMEM((7, table_rows, 128), F32),
            pltpu.VMEM((table_rows, 128), F32),
            pltpu.VMEM((2, table_rows, 128), F32),
            pltpu.VMEM((2, 1, 128), F32),
            pltpu.VMEM((2, 4, table_rows, 128), F32),
            pltpu.VMEM((size_y, depth), F32),
            pltpu.VMEM((size_x, 1, depth), F32),
            pltpu.VMEM((size_x, 1, depth), F32),
            pltpu.VMEM((2, size_x, 1, depth), F32),
            pltpu.VMEM((2, size_y, depth), F32),
            pltpu.VMEM((2, size_x, 1, depth), F32),
            pltpu.VMEM((2, 2, size_x, 1, depth), F32),
            pltpu.VMEM((4, 2, size_y, depth), F32),
            pltpu.VMEM((4, 2, size_x, 1, depth), F32),
            pltpu.VMEM((2, devices, 1, 128), F32),
            pltpu.VMEM((2, devices, 1, 128), F32),
            pltpu.VMEM((2, devices + 2 * count_y, 5, 1, 128), F32),
            pltpu.VMEM((2, 5, devices, 1, 128), F32),
            pltpu.VMEM((3, devices, SLOT, 128), F32),
            pltpu.VMEM((3, devices, SLOT, 128), F32),
            pltpu.VMEM((2, 1, 1, 128), F32),
            pltpu.VMEM((2, devices, 1, 128), F32),
            dma((7,)),
            dma((2, 4)),
            dma((2, 4)),
            dma((6,)),
            dma((6,)),
            dma((2, 4)),
            dma((2, 4)),
            dma((2,)),
            dma((2,)),
            dma((2,)),
            dma((2,)),
            dma((3,)),
            dma((3,)),
            dma((2,)),
            dma((2,)),
        ],
        compiler_params=pltpu.CompilerParams(
            collective_id=0, has_side_effects=True, vmem_limit_bytes=61000000
        ),
    )(
        source_term,
        mobility_x,
        mobility_y,
        mobility_z,
        bubble_fraction,
        block_inverse,
        couplings,
        send,
        recv,
        neighbours.T,
    )
    alpha, alpha_two, beta = [
        lax.broadcast_in_dim(g.reshape(depth), field, (2,)) for g in gains
    ]
    return (
        alpha * direction + alpha_two * (zed + beta * direction),
        res - alpha_two * (image_two + beta * image),
    )


def solution(mesh):
    return jax.shard_map(
        body,
        mesh=mesh,
        in_specs=(
            P("gx", "gy", None),
            P("gx", "gy", None),
            P("gx", "gy", None),
            P("gx", "gy", None),
            P("gx", "gy", None),
            P("gx", "gy", None),
            P(("gx", "gy"), None, None),
            P(("gx", "gy"), None, None),
            P(("gx", "gy"), None, None),
            P(("gx", "gy"), None, None, None),
            P(("gx", "gy"), None),
        ),
        out_specs=(P("gx", "gy", None), P("gx", "gy", None)),
        check_vma=False,
    )
```

```python
import functools

import jax
import jax.numpy as jnp
from jax import lax
from jax.experimental import pallas as pl
from jax.experimental.pallas import tpu as pltpu
from jax.sharding import PartitionSpec as P

TZ = 128
LINK = 4
SLOT = 4
F32 = jnp.float32
BF16 = jnp.bfloat16
MESH = pl.DeviceIdType.MESH
NT = (((1,), (1,)), ((), ()))
NN = (((1,), (0,)), ((), ()))
GROUP = 8
CHUNKS = 4


def log2(value):
    assert value & (value - 1) == 0
    return value.bit_length() - 1


def iota(shape, axis):
    return lax.broadcasted_iota(jnp.int32, shape, axis)


def split_two(value):
    first = value.astype(BF16).astype(F32)
    return first, (value - first).astype(BF16).astype(F32)


def stack_two(value, axis=0):
    return jnp.concatenate(split_two(value), axis=axis).astype(BF16)


def fold_two(value):
    half = value.shape[0] // 2
    return value[:half] + value[half:]


def fold_tiles(value):
    tiles = [
        value[y : y + 8, z : z + 128]
        for y in range(0, value.shape[0], 8)
        for z in range(0, value.shape[1], 128)
    ]
    while len(tiles) > 1:
        tiles = [a + b for a, b in zip(tiles[::2], tiles[1::2])]
    return tiles[0]


def write_one_hots(index_ref, hot_ref, turned_ref=None):
    group = hot_ref.shape[2] // 128

    def step(block, carry):
        for sub in range(group):
            index = index_ref[pl.ds(block * group + sub, 1), :]
            hot = jnp.where(iota((128, 128), 0) == (index & 127), 1.0, 0.0)
            hot_ref[block, :, sub * 128 : (sub + 1) * 128] = hot.astype(BF16)
            if turned_ref is not None:
                turned_ref[block, sub * 128 : (sub + 1) * 128, :] = hot.T.astype(BF16)
        return carry

    lax.fori_loop(0, hot_ref.shape[0], step, 0)


def in_chunks(count, step, carry, chunk=4):
    chunk = max(c for c in range(1, chunk + 1) if count % c == 0)

    def chunk_step(n, carry):
        for sub in range(chunk):
            carry = step(n * chunk + sub, carry)
        return carry

    if count == chunk:
        return chunk_step(0, carry)
    return lax.fori_loop(0, count // chunk, chunk_step, carry)


def gather_rows(table, index_ref, hot_ref, store):
    parts = stack_two(table)
    high_count = table.shape[0]
    group = hot_ref.shape[2] // 128

    def step(block, carry):
        picked = fold_two(
            lax.dot_general(parts, hot_ref[block], NN, preferred_element_type=F32)
        )
        for sub in range(group):
            row = block * group + sub
            hit = iota((high_count, 128), 0) == (index_ref[pl.ds(row, 1), :] >> 7)
            mine = picked[:, sub * 128 : (sub + 1) * 128]
            store(row, jnp.sum(jnp.where(hit, mine, 0.0), axis=0, keepdims=True))
        return carry

    in_chunks(hot_ref.shape[0], step, 0)


def scatter_rows(value_of, index_ref, hot_ref, high_count, dims=NT):
    group = max(hot_ref.shape[1:]) // 128

    def step(block, total):
        pieces = []
        for sub in range(group):
            row = block * group + sub
            hit = iota((high_count, 128), 0) == (index_ref[pl.ds(row, 1), :] >> 7)
            pieces.append(
                jnp.concatenate(
                    [jnp.where(hit, part, 0.0) for part in split_two(value_of(row))], axis=0
                ).astype(BF16)
            )
        return total + lax.dot_general(
            jnp.concatenate(pieces, axis=1), hot_ref[block], dims, preferred_element_type=F32
        )

    start = jnp.zeros((2 * high_count, 128), F32)
    return fold_two(in_chunks(hot_ref.shape[0], step, start))


def block_vectors(vectors):
    first, second = split_two(vectors)
    out = []
    for q in range(vectors.shape[0]):
        mine = iota(vectors.shape, 0) == q
        top = jnp.where(mine, first, 0.0)
        low = jnp.where(mine, second, 0.0)
        upper = jnp.concatenate([top, top], axis=1)
        lower = jnp.concatenate([low, jnp.zeros_like(low)], axis=1)
        out.append(jnp.concatenate([upper, lower], axis=0).astype(BF16))
    return out


def block_products(vectors, split_ref):
    total = None
    for q, part in enumerate(block_vectors(vectors)):
        term = lax.dot_general(part, split_ref[q], NN, preferred_element_type=F32)
        total = term if total is None else total + term
    return fold_two(total)


def kernel(
    counts,
    source_hbm,
    mob_x_hbm,
    mob_y_hbm,
    mob_z_hbm,
    fraction_hbm,
    inverse_hbm,
    couplings_hbm,
    send_ref,
    recv_ref,
    near_ref,
    res,
    direction,
    zed,
    image,
    image_two,
    gain_ref,
    gain_two_ref,
    mix_ref,
    mob_x,
    mob_y,
    mob_z,
    fraction,
    inverse,
    couplings,
    inv_diag,
    local,
    local_two,
    inverse_split,
    couplings_split,
    send_hot,
    recv_hot,
    recv_turned,
    back_hot,
    side_hot,
    send_map,
    back_map,
    side_map,
    totals_table,
    values_table,
    local_table,
    stencil_table,
    code_table,
    beside_table,
    beside_row,
    table_halo,
    low_mx,
    low_my,
    edge_my,
    edge_f,
    halo_fx,
    halo_fy,
    edges,
    halo_x,
    halo_y,
    row_send,
    row_recv,
    side_send,
    side_recv,
    link_send,
    link_recv,
    sum_send,
    sum_recv,
    load_sem,
    side_send_sem,
    side_recv_sem,
    early_send_sem,
    early_recv_sem,
    table_send_sem,
    table_recv_sem,
    row_send_sem,
    row_recv_sem,
    spread_send_sem,
    spread_recv_sem,
    link_send_sem,
    link_recv_sem,
    sum_send_sem,
    sum_recv_sem,
):
    count_x, count_y = counts
    devices = count_x * count_y
    at_x, at_y = lax.axis_index("gx"), lax.axis_index("gy")
    me = at_x * count_y + at_y
    size_x, size_y, depth = res.shape
    tiles_z = depth // TZ
    group = 128 // (size_y * tiles_z)
    table_rows = size_x // group
    blocks = inverse.shape[0]
    push_count = near_ref.size

    loads = [
        pltpu.make_async_copy(src, dst, load_sem.at[n])
        for n, (src, dst) in enumerate(
            (
                (source_hbm, res),
                (fraction_hbm, fraction),
                (mob_y_hbm, mob_y),
                (mob_x_hbm, mob_x),
                (mob_z_hbm, mob_z),
                (inverse_hbm, inverse),
                (couplings_hbm, couplings),
            )
        )
    ]
    for load in loads:
        load.start()

    barrier = pltpu.get_barrier_semaphore()

    def peer(step):
        other = lax.rem(me + step, devices)
        return (other // count_y, lax.rem(other, count_y)), other

    def greet(step, carry):
        pl.semaphore_signal(barrier, inc=1, device_id=peer(step)[0], device_id_type=MESH)
        return carry

    for ref in (low_mx, low_my, halo_fx, halo_fy, halo_x, halo_y, side_send):
        ref[...] = jnp.zeros_like(ref)
    table_halo[0] = jnp.zeros_like(table_halo[0])
    table_halo[1] = jnp.full_like(table_halo[1], -1.0)
    lax.fori_loop(1, devices, greet, 0)

    def exchange(send, recv, send_sem, recv_sem, same=False):
        def one(step, carry):
            device, other = peer(step)
            pltpu.make_async_remote_copy(
                src_ref=send.at[0 if same else other],
                dst_ref=recv.at[me],
                send_sem=send_sem,
                recv_sem=recv_sem,
                device_id=device,
                device_id_type=MESH,
            ).start()
            return carry

        lax.fori_loop(1, devices, one, 0)
        recv[me] = send[0 if same else me]

    def arrived(recv, recv_sem):
        part = recv.at[pl.ds(0, devices - 1)]
        pltpu.make_async_copy(part, part, recv_sem).wait()

    tile = send_ref[...]
    low = tile & 127
    tile_k = low & (tiles_z - 1)
    tile_j = (low >> log2(tiles_z)) & (size_y - 1)
    tile_g = low >> log2(tiles_z * size_y)
    send_map[...] = (
        (tile - low) + tile_k * (group * size_y) + tile_g * size_y + tile_j
    )

    def tile_sums(planes):
        stacked = jnp.concatenate(
            [plane[:, k * TZ : (k + 1) * TZ] for k in range(tiles_z) for plane in planes],
            axis=0,
        )
        return jnp.sum(stacked.T, axis=0, keepdims=True)

    def row_exchange(n):
        exchange(row_send.at[n], row_recv.at[n], row_send_sem.at[n], row_recv_sem.at[n])

    write_one_hots(send_map, send_hot)
    loads[0].wait()
    loads[1].wait()

    def first_totals(row, carry):
        xs = [row * group + g for g in range(group)]
        totals_table[0, pl.ds(row, 1), :] = tile_sums([fraction[x] * res[x] for x in xs])
        return carry

    in_chunks(table_rows, first_totals, 0)
    def to_owners(n):
        def store(row, value):
            row_send[n, row] = value

        return store

    gather_rows(totals_table[0], send_map, send_hot, to_owners(0))
    pl.semaphore_wait(barrier, devices - 1)
    row_exchange(0)

    def side_copy(src, dst, send_sem, recv_sem, shift_x, shift_y):
        return pltpu.make_async_remote_copy(
            src_ref=src,
            dst_ref=dst,
            send_sem=send_sem,
            recv_sem=recv_sem,
            device_id=(at_x + shift_x, at_y + shift_y),
            device_id_type=MESH,
        )

    has_low_x, has_high_x = at_x > 0, at_x < count_x - 1
    has_low_y, has_high_y = at_y > 0, at_y < count_y - 1
    sides = (
        (has_low_x, has_high_x, -1, 0),
        (has_high_x, has_low_x, 1, 0),
        (has_low_y, has_high_y, 0, -1),
        (has_high_y, has_low_y, 0, 1),
    )

    def side_group(parts, send_sem, recv_sem):
        out = []
        for n, (side, src, dst) in enumerate(parts):
            there, came, shift_x, shift_y = sides[side]
            copy = side_copy(src, dst, send_sem.at[n], recv_sem.at[n], shift_x, shift_y)
            out.append((there, came, copy))
        return out

    def start(copies):
        for there, came, copy in copies:
            pl.when(there)(copy.start)

    def came_in(copies):
        for there, came, copy in copies:
            pl.when(came)(copy.wait_recv)

    loads[2].wait()
    loads[3].wait()

    def take_edge(x, carry):
        edge_my[x] = mob_y[x, size_y - 1 : size_y, :]
        edge_f[0, x] = fraction[x, 0:1, :]
        edge_f[1, x] = fraction[x, size_y - 1 : size_y, :]
        return carry

    lax.fori_loop(0, size_x, take_edge, 0)
    early = side_group(
        (
            (1, mob_x.at[size_x - 1], low_mx),
            (3, edge_my, low_my),
            (0, fraction.at[0], halo_fx.at[1]),
            (1, fraction.at[size_x - 1], halo_fx.at[0]),
            (2, edge_f.at[0], halo_fy.at[1]),
            (3, edge_f.at[1], halo_fy.at[0]),
        ),
        early_send_sem,
        early_recv_sem,
    )
    start(early)

    near_row = jnp.concatenate([near_ref[k : k + 1] for k in range(near_ref.shape[0])], axis=1)
    target_row = near_row >> log2(blocks)
    down, across = iota((push_count, push_count), 0), iota((push_count, push_count), 1)
    target_col = jnp.sum(
        jnp.where(down == across, target_row.astype(F32), 0.0), axis=1, keepdims=True
    ).astype(jnp.int32)
    earlier = down < across
    same = jnp.where((target_row == target_col) & earlier, 1, 0)
    rank = jnp.sum(same, axis=0, keepdims=True)
    slot = target_row * SLOT + rank
    chosen = iota((devices * SLOT, push_count), 0) == slot
    local_block = (near_row & (blocks - 1)).astype(F32)
    identity = jnp.sum(jnp.where(chosen, local_block, 0.0), axis=1, keepdims=True)
    link_send[0] = jnp.broadcast_to(identity, (devices * SLOT, 128)).reshape(
        devices, SLOT, 128
    )
    spread = jnp.where(chosen, 1.0, 0.0).astype(BF16)

    def link_exchange(n):
        exchange(link_send.at[n], link_recv.at[n], link_send_sem.at[n], link_recv_sem.at[n])

    link_exchange(0)

    lane = iota((size_y, depth), 1)
    row_of = iota((size_y, depth), 0)

    def below_z(plane):
        return jnp.where(lane == 0, 0.0, pltpu.roll(plane, 1, 1))

    def above_z(plane):
        return jnp.where(lane == depth - 1, 0.0, pltpu.roll(plane, depth - 1, 1))

    def below_y(plane, edge):
        return jnp.where(row_of == 0, edge, pltpu.roll(plane, 1, 0))

    def above_y(plane, edge):
        return jnp.where(row_of == size_y - 1, edge, pltpu.roll(plane, size_y - 1, 0))

    wide = group * size_y
    slot_of = iota((table_rows, 128), 1)
    slot_y = slot_of & (size_y - 1)
    slot_g = (slot_of >> log2(size_y)) & (group - 1)
    slot_k = slot_of >> log2(wide)

    def turn(table, shift):
        return pltpu.roll(table, shift % 128, 1) if shift % 128 else table

    def next_x(table, high):
        inner = turn(table, -size_y)
        outer = turn(jnp.concatenate([table[1:], high], axis=0), (group - 1) * size_y)
        return jnp.where(slot_g < group - 1, inner, outer)

    def last_x(table, low):
        inner = turn(table, size_y)
        outer = turn(
            jnp.concatenate([low, table[: table_rows - 1]], axis=0), -(group - 1) * size_y
        )
        return jnp.where(slot_g > 0, inner, outer)

    def next_y(table, high):
        return jnp.where(slot_y < size_y - 1, turn(table, -1), high)

    def last_y(table, low):
        return jnp.where(slot_y > 0, turn(table, 1), low)

    def next_z(table):
        return jnp.where(slot_k < tiles_z - 1, turn(table, -wide), 0.0)

    def last_z(table):
        return jnp.where(slot_k > 0, turn(table, wide), 0.0)

    write_one_hots(recv_ref, recv_hot, recv_turned)
    loads[5].wait()

    def split_inverse(q, carry):
        inverse_split[q] = stack_two(inverse[q].T)
        return carry

    in_chunks(blocks, split_inverse, 0)
    loads[6].wait()

    def fold_couplings(q, carry):
        both = jnp.concatenate([couplings[q, k] for k in range(couplings.shape[1])], axis=0)
        upper, lower = split_two(both)
        top, rest = inverse_split[q, : inverse.shape[1]], inverse_split[q, inverse.shape[1] :]
        product = lax.dot_general(
            jnp.concatenate([top, rest, top], axis=1),
            jnp.concatenate([upper, upper, lower], axis=1).astype(BF16),
            NT,
            preferred_element_type=F32,
        )
        couplings_split[q] = stack_two(product)
        return carry

    in_chunks(blocks, fold_couplings, 0)

    place = iota((1, 128), 1)
    codes = scatter_rows(
        lambda row: (row * 128 + place).astype(F32), send_map, send_hot, table_rows
    )
    code_table[...] = codes
    back_map[...] = codes.astype(jnp.int32)

    zero_tile = jnp.zeros((8, 128), F32)
    fields = (local, direction, local_two, zed)

    def keep_edges(phase, x, value):
        edges[phase, 0, x] = value[0:1]
        edges[phase, 1, x] = value[size_y - 1 : size_y]

    def halo_copies(phase):
        field = fields[2 * phase]
        return side_group(
            (
                (0, field.at[0], halo_x.at[2 * phase, 1]),
                (1, field.at[size_x - 1], halo_x.at[2 * phase, 0]),
                (2, edges.at[phase, 0], halo_y.at[2 * phase, 1]),
                (3, edges.at[phase, 1], halo_y.at[2 * phase, 0]),
            ),
            side_send_sem.at[phase],
            side_recv_sem.at[phase],
        )

    def prepare(row, lower, above, total):
        whole, across_x, across_y, across_z = [], [], [], []
        for g in range(group):
            x = row * group + g
            mob_a, mob_b, mob_c = mob_x[x], mob_y[x], mob_z[x]
            weight, source = fraction[x], res[x]
            diagonal = (
                (mob_a + lower) + (mob_b + below_y(mob_b, low_my[x])) + (mob_c + below_z(mob_c))
            )
            inverse_here = 1.0 / diagonal
            value = source * inverse_here
            inv_diag[x] = inverse_here
            local[x] = value
            keep_edges(0, x, value)
            total = total + fold_tiles(source * value)
            up = fraction[x + 1] if g < group - 1 or above is None else above
            whole.append(diagonal * (weight * weight))
            across_x.append(mob_a * weight * up)
            across_y.append(mob_b * weight * above_y(weight, halo_fy[1, x]))
            across_z.append(mob_c * weight * above_z(weight))
            lower = mob_a
        here = pl.ds(row, 1)
        stencil_table[1, here, :] = tile_sums(across_x)
        stencil_table[3, here, :] = tile_sums(across_y)
        turned = jnp.concatenate(
            [p[:, k * TZ : (k + 1) * TZ] for k in range(tiles_z) for p in across_z], axis=0
        ).T
        crossing = turned[TZ - 1 : TZ]
        inside = jnp.sum(turned, axis=0, keepdims=True) - crossing
        stencil_table[5, here, :] = crossing
        stencil_table[0, here, :] = tile_sums(whole) - 2.0 * inside
        return lower, total

    def table_copies(n, pairs):
        return side_group(
            [(side, src, table_halo.at[n, side]) for side, src in pairs],
            table_send_sem.at[n],
            table_recv_sem.at[n],
        )

    def apply_operator(phase, emit):
        field = fields[phase]

        def group_step(row, here, flux_low, carry, top):
            values = []
            for g in range(group):
                x = row * group + g
                above = top if top is not None and g == group - 1 else field[x + 1]
                flux_x = mob_x[x] * (above - here)
                flux_y = mob_y[x] * (above_y(here, halo_y[phase, 1, x]) - here)
                edge = low_my[x] * (here[0:1] - halo_y[phase, 0, x])
                flux_z = mob_z[x] * (above_z(here) - here)
                value = (
                    (flux_low - flux_x)
                    + (below_y(flux_y, edge) - flux_y)
                    + (below_z(flux_z) - flux_z)
                )
                values.append((here, value))
                here, flux_low = above, flux_x
            return here, flux_low, emit(row, values, carry)

        first = field[0]
        flux = low_mx[...] * (first - halo_x[phase, 0])
        state = (first, flux, zero_tile)
        state = in_chunks(table_rows - 1, lambda row, s: group_step(row, *s, None), state, 3)
        return jnp.sum(group_step(table_rows - 1, *state, halo_x[phase, 1])[2])

    def emit_local(n):
        def emit(row, values, total):
            parts = []
            for g, (here, value) in enumerate(values):
                total = total + fold_tiles(here * value)
                parts.append(fraction[row * group + g] * value)
            local_table[n, pl.ds(row, 1), :] = tile_sums(parts)
            return total

        return emit

    def emit_field(result):
        def emit(row, values, total):
            for g, (here, value) in enumerate(values):
                result[row * group + g] = value
            return total

        return emit

    def coarse_totals(phase):
        arrived(row_recv.at[phase], row_recv_sem.at[phase])
        return scatter_rows(
            lambda row: row_recv[phase, row], recv_ref, recv_turned, blocks, NN
        )

    def sweep_first(phase, totals):
        both = block_products(totals, couplings_split)
        pushed = jnp.concatenate(
            [both[:, k * 128 : (k + 1) * 128] for k in range(couplings.shape[1])], axis=0
        )
        upper, lower = split_two(pushed)
        out_values = lax.dot_general(
            spread, upper.astype(BF16), NN, preferred_element_type=F32
        ) + lax.dot_general(spread, lower.astype(BF16), NN, preferred_element_type=F32)
        link_send[1 + phase] = out_values.reshape(devices, SLOT, 128)
        link_exchange(1 + phase)

    def sweep_second(phase, totals, gather_in):
        arrived(link_recv.at[1 + phase], link_recv_sem.at[1 + phase])
        values = stack_two(link_recv[1 + phase].reshape(devices * SLOT, 128), axis=1)
        summed = lax.dot_general(gather_in, values, NN, preferred_element_type=F32)
        coupled = summed[:, :128] + summed[:, 128:]
        sweep_two = block_products(totals - coupled, inverse_split)

        def store(row, value):
            side_send[phase, row + count_y, 0] = value
            side_send[phase, row, 1] = value
            side_send[phase, row + 2 * count_y, 2] = value
            side_send[phase, row + count_y - 1, 3] = value
            side_send[phase, row + count_y + 1, 4] = value

        gather_rows(sweep_two, recv_ref, recv_hot, store)

        def one(step, carry):
            device, other = peer(step)
            pltpu.make_async_remote_copy(
                src_ref=side_send.at[phase, other + count_y],
                dst_ref=side_recv.at[phase, :, me],
                send_sem=spread_send_sem.at[phase],
                recv_sem=spread_recv_sem.at[phase],
                device_id=device,
                device_id_type=MESH,
            ).start()
            return carry

        lax.fori_loop(1, devices, one, 0)
        side_recv[phase, :, me] = side_send[phase, me + count_y]

    def spread_done(phase, sem):
        part = side_recv.at[phase, :, pl.ds(0, devices - 1)]
        pltpu.make_async_copy(part, part, sem).wait()

    def tile_values(phase):
        spread_done(phase, spread_recv_sem.at[phase])

        def store(row, value):
            values_table[phase, pl.ds(row, 1), :] = value

        def rows_of(n):
            return side_recv[phase, n].reshape(devices, 128)

        gather_rows(rows_of(0), back_map, back_hot, store)
        beside = []
        gather_rows(
            jnp.concatenate([rows_of(1 + n) for n in range(4)], axis=0),
            side_map,
            side_hot,
            lambda row, value: beside.append(value),
        )
        packed = jnp.broadcast_to(beside[1], (table_rows, 128))
        high_y = pltpu.roll(packed, size_y - table_rows, 1, stride=1, stride_axis=0)
        low_y = pltpu.roll(packed, 1, 1, stride=1, stride_axis=0)
        beside_table[phase] = jnp.where(slot_y == 0, low_y, high_y)
        beside_row[phase] = beside[0]
        return beside[0], low_y, high_y

    def spread_tiles(row):
        return jnp.broadcast_to(row, (128, 128)).T

    def make_field(phase):
        n = 2 * phase + 1
        field, plus = fields[n], fields[2 * phase]

        def tile_part(stacked, g, first, count):
            return jnp.concatenate(
                [
                    stacked[
                        (k * group + g) * size_y + first : (k * group + g) * size_y + first + count
                    ]
                    for k in range(tiles_z)
                ],
                axis=1,
            )

        def step(row, carry):
            stacked = spread_tiles(values_table[phase, pl.ds(row, 1), :])
            beside = spread_tiles(beside_table[phase, pl.ds(row, 1), :])
            for g in range(group):
                x = row * group + g
                field[x] = fraction[x] * tile_part(stacked, g, 0, size_y) + plus[x]
                for side in range(2):
                    value = tile_part(beside, g, side * (size_y - 1), 1)
                    halo_y[n, side, x] = halo_fy[side, x] * value + halo_y[n - 1, side, x]
            return carry

        in_chunks(table_rows, step, 0)
        stacked = spread_tiles(beside_row[phase])
        for side, g in ((0, group - 1), (1, 0)):
            value = tile_part(stacked, g, 0, size_y)
            halo_x[n, side] = halo_fx[side] * value + halo_x[n - 1, side]

    def tile_operator(phase, beside_x, low_y, high_y):
        table = values_table[phase]
        return (
            stencil_table[0] * table
            - (
                stencil_table[1] * next_x(table, beside_x)
                + stencil_table[2] * last_x(table, beside_x)
            )
            - (
                stencil_table[3] * next_y(table, high_y)
                + stencil_table[4] * last_y(table, low_y)
            )
            - (stencil_table[5] * next_z(table) + stencil_table[6] * last_z(table))
        )

    def start_sums(phase, values):
        row = jnp.zeros((1, 128), F32)
        for n, value in enumerate(values):
            row = jnp.where(place == n, value, row)
        sum_send[phase, 0] = row
        exchange(
            sum_send.at[phase],
            sum_recv.at[phase],
            sum_send_sem.at[phase],
            sum_recv_sem.at[phase],
            same=True,
        )

    def end_sums(phase, count):
        arrived(sum_recv.at[phase], sum_recv_sem.at[phase])
        totals = [sum_recv[phase, n] for n in range(4)]
        for n in range(4, devices):
            totals[n % 4] = totals[n % 4] + sum_recv[phase, n]
        total = (totals[0] + totals[1]) + (totals[2] + totals[3])
        return [
            jnp.sum(jnp.where(place == n, total, 0.0), axis=1, keepdims=True)
            for n in range(count)
        ]

    waits = [early, table_copies(1, [(side, code_table) for side in range(4)])]
    start(waits[1])
    totals = coarse_totals(0)
    sweep_first(0, totals)

    loads[4].wait()
    came_in(early)
    lower, total = in_chunks(
        table_rows - 1,
        lambda row, s: prepare(row, s[0], None, s[1]),
        (low_mx[...], zero_tile),
        3,
    )
    _, total = prepare(table_rows - 1, lower, halo_fx[1], total)
    source_local = jnp.sum(total)
    waits.append(halo_copies(0))
    start(waits[2])
    waits.append(table_copies(0, ((1, stencil_table.at[1]), (3, stencil_table.at[3]))))
    start(waits[3])
    arrived(link_recv.at[0], link_recv_sem.at[0])
    names = link_recv[0].reshape(devices * SLOT, 128).T[:blocks]
    gather_in = jnp.where(
        names == iota((blocks, devices * SLOT), 0).astype(F32), 1.0, 0.0
    ).astype(BF16)

    sweep_second(0, totals, gather_in)

    write_one_hots(back_map, back_hot)
    came_in(waits[1])
    across_y, across_g = slot_y[:1], slot_g[:1]
    code_x = jnp.where(
        across_g == 0,
        table_halo[1, 0, 0:1],
        jnp.where(across_g == group - 1, table_halo[1, 1, table_rows - 1 :], -1.0),
    )
    code_y = jnp.full((1, 128), -1.0, F32)
    for r in range(table_rows):
        high = turn(table_halo[1, 2, r : r + 1], table_rows - 1 - r)
        low = turn(table_halo[1, 3, r : r + 1], -size_y - r)
        code_y = jnp.where(across_y == table_rows - 1 - r, high, code_y)
        code_y = jnp.where(across_y == size_y - 1 - r, low, code_y)
    span = devices * 128
    code_x, code_y = code_x.astype(jnp.int32), code_y.astype(jnp.int32)
    shift_x = jnp.where(across_g == 0, 0, span)
    shift_y = jnp.where(across_y < table_rows, 2 * span, 3 * span)
    side_map[0:1] = jnp.where(code_x < 0, -1, code_x + shift_x)
    side_map[1:2] = jnp.where(code_y < 0, -1, code_y + shift_y)
    write_one_hots(side_map, side_hot)
    came_in(waits[3])
    stencil_table[2] = last_x(stencil_table[1], table_halo[0, 1, table_rows - 1 :])
    stencil_table[4] = last_y(stencil_table[3], turn(table_halo[0, 3], 1 - size_y))
    stencil_table[6] = last_z(stencil_table[5])
    came_in(waits[2])
    local_energy = apply_operator(0, emit_local(0))

    beside = tile_values(0)
    operated = tile_operator(0, *beside)
    image_totals = operated + local_table[0]
    totals_table[1] = image_totals
    gather_rows(image_totals, send_map, send_hot, to_owners(1))
    row_exchange(1)
    values = values_table[0]
    rz_part = jnp.sum(totals_table[0] * values) + source_local
    energy_part = jnp.sum(values * (image_totals + local_table[0])) + local_energy
    start_sums(0, (rz_part, energy_part))

    make_field(0)

    rz, energy = end_sums(0, 2)
    alpha = rz / energy
    totals = totals - alpha * coarse_totals(1)
    sweep_first(1, totals)

    apply_operator(1, emit_field(image))

    def update(x, carry):
        own, cross = carry
        pushed = image[x]
        here = res[x] - alpha * pushed
        value = inv_diag[x] * here
        res[x] = here
        local_two[x] = value
        keep_edges(1, x, value)
        return own + fold_tiles(here * value), cross + fold_tiles(value * pushed)

    own, cross = in_chunks(size_x, update, (zero_tile, zero_tile))
    residual_local, cross_local = jnp.sum(own), jnp.sum(cross)
    waits.append(halo_copies(1))
    start(waits[4])

    sweep_second(1, totals, gather_in)

    came_in(waits[4])
    local_energy = apply_operator(2, emit_local(1))

    beside = tile_values(1)
    operated = tile_operator(1, *beside)
    values = values_table[1]
    tile_totals = totals_table[0] - alpha * totals_table[1]
    next_part = jnp.sum(tile_totals * values) + residual_local
    own_part = jnp.sum(values * (operated + 2.0 * local_table[1])) + local_energy
    cross_part = jnp.sum(values * totals_table[1]) + cross_local
    start_sums(1, (next_part, own_part, cross_part))

    make_field(1)
    apply_operator(3, emit_field(image_two))

    rz_next, own, cross = end_sums(1, 3)
    beta = rz_next / rz
    alpha_two = rz_next / (own + beta * (2.0 * cross + beta * energy))

    for ref, value in ((gain_ref, alpha), (gain_two_ref, alpha_two), (mix_ref, beta)):
        ref[...] = jnp.broadcast_to(value, ref.shape)
    for copies in waits:
        for there, came, copy in copies:
            pl.when(there)(copy.wait_send)
    for n in range(2):
        arrived(row_send.at[n], row_send_sem.at[n])
        spread_done(n, spread_send_sem.at[n])
    for n in range(3):
        arrived(link_send.at[n], link_send_sem.at[n])
    for n in range(2):
        arrived(sum_recv.at[n], sum_send_sem.at[n])


def finish(
    direction, zed, res, image_two, image, gain_ref, gain_two_ref, mix_ref, x_hbm, r_hbm, x, r, sem
):
    alpha, alpha_two, beta = gain_ref[...], gain_two_ref[...], mix_ref[...]
    planes = x.shape[0] // CHUNKS
    copies = []
    for n in range(CHUNKS):
        for p in range(n * planes, (n + 1) * planes):
            first = direction[p]
            x[p] = alpha * first + alpha_two * (zed[p] + beta * first)
            r[p] = res[p] - alpha_two * (image_two[p] + beta * image[p])
        part = pl.ds(n * planes, planes)
        for k, (src, dst) in enumerate(((x, x_hbm), (r, r_hbm))):
            copies.append(pltpu.make_async_copy(src.at[part], dst.at[part], sem.at[k, n]))
            copies[-1].start()
    for copy in copies:
        copy.wait()


def body(
    source_term,
    mobility_x,
    mobility_y,
    mobility_z,
    bubble_fraction,
    tile_labels,
    send_tiles,
    recv_rows,
    block_inverse,
    couplings,
    neighbours,
):
    count_x, count_y = lax.axis_size("gx"), lax.axis_size("gy")
    devices = count_x * count_y
    size_x, size_y, depth = source_term.shape
    tiles = size_x * size_y * (depth // TZ)
    blocks, order = block_inverse.shape[:2]
    send, recv = send_tiles[0], recv_rows[0]
    pad = 128 - send.shape[1]
    assert order == 128 and pad >= 0
    if pad:
        send = jnp.pad(send, ((0, 0), (0, pad)), constant_values=tiles)
        recv = jnp.pad(recv, ((0, 0), (0, pad)), constant_values=blocks * order)
    table_rows = tiles // 128
    field = (size_x, size_y, depth)
    hbm = pl.BlockSpec(memory_space=pltpu.HBM)
    vmem = pl.BlockSpec(memory_space=pltpu.VMEM)
    dma = pltpu.SemaphoreType.DMA
    res, direction, zed, image, image_two, *gains = pl.pallas_call(
        functools.partial(kernel, (count_x, count_y)),
        out_shape=(*[pltpu.VMEM(field, F32)] * 5, *[pltpu.VMEM((1, depth), F32)] * 3),
        in_specs=[hbm] * 7 + [vmem] * 3,
        out_specs=(vmem,) * 8,
        scratch_shapes=[
            *[pltpu.VMEM(field, F32)] * 4,
            pltpu.VMEM((blocks, order, order), F32),
            pltpu.VMEM(couplings.shape, F32),
            *[pltpu.VMEM(field, F32)] * 3,
            pltpu.VMEM((blocks, 2 * order, order), BF16),
            pltpu.VMEM((blocks, 2 * order, order * couplings.shape[1]), BF16),
            pltpu.VMEM((devices // GROUP, 128, GROUP * 128), BF16),
            pltpu.VMEM((devices // GROUP, 128, GROUP * 128), BF16),
            pltpu.VMEM((devices // GROUP, GROUP * 128, 128), BF16),
            pltpu.VMEM((table_rows // GROUP, 128, GROUP * 128), BF16),
            pltpu.VMEM((1, 128, 2 * 128), BF16),
            pltpu.VMEM((devices, 128), jnp.int32),
            pltpu.VMEM((table_rows, 128), jnp.int32),
            pltpu.VMEM((2, 128), jnp.int32),
            pltpu.VMEM((2, table_rows, 128), F32),
            pltpu.VMEM((2, table_rows, 128), F32),
            pltpu.VMEM((2, table_rows, 128), F32),
            pltpu.VMEM((7, table_rows, 128), F32),
            pltpu.VMEM((table_rows, 128), F32),
            pltpu.VMEM((2, table_rows, 128), F32),
            pltpu.VMEM((2, 1, 128), F32),
            pltpu.VMEM((2, 4, table_rows, 128), F32),
            pltpu.VMEM((size_y, depth), F32),
            pltpu.VMEM((size_x, 1, depth), F32),
            pltpu.VMEM((size_x, 1, depth), F32),
            pltpu.VMEM((2, size_x, 1, depth), F32),
            pltpu.VMEM((2, size_y, depth), F32),
            pltpu.VMEM((2, size_x, 1, depth), F32),
            pltpu.VMEM((2, 2, size_x, 1, depth), F32),
            pltpu.VMEM((4, 2, size_y, depth), F32),
            pltpu.VMEM((4, 2, size_x, 1, depth), F32),
            pltpu.VMEM((2, devices, 1, 128), F32),
            pltpu.VMEM((2, devices, 1, 128), F32),
            pltpu.VMEM((2, devices + 2 * count_y, 5, 1, 128), F32),
            pltpu.VMEM((2, 5, devices, 1, 128), F32),
            pltpu.VMEM((3, devices, SLOT, 128), F32),
            pltpu.VMEM((3, devices, SLOT, 128), F32),
            pltpu.VMEM((2, 1, 1, 128), F32),
            pltpu.VMEM((2, devices, 1, 128), F32),
            dma((7,)),
            dma((2, 4)),
            dma((2, 4)),
            dma((6,)),
            dma((6,)),
            dma((2, 4)),
            dma((2, 4)),
            dma((2,)),
            dma((2,)),
            dma((2,)),
            dma((2,)),
            dma((3,)),
            dma((3,)),
            dma((2,)),
            dma((2,)),
        ],
        compiler_params=pltpu.CompilerParams(
            collective_id=0, has_side_effects=True, vmem_limit_bytes=61000000
        ),
    )(
        source_term,
        mobility_x,
        mobility_y,
        mobility_z,
        bubble_fraction,
        block_inverse,
        couplings,
        send,
        recv,
        neighbours.T,
    )
    return tuple(
        pl.pallas_call(
            finish,
            out_shape=(jax.ShapeDtypeStruct(field, F32), jax.ShapeDtypeStruct(field, F32)),
            in_specs=[vmem] * 8,
            out_specs=(hbm, hbm),
            scratch_shapes=[
                pltpu.VMEM(field, F32),
                pltpu.VMEM(field, F32),
                dma((2, CHUNKS)),
            ],
            compiler_params=pltpu.CompilerParams(vmem_limit_bytes=50000000),
        )(direction, zed, res, image_two, image, *gains)
    )


def solution(mesh):
    return jax.shard_map(
        body,
        mesh=mesh,
        in_specs=(
            P("gx", "gy", None),
            P("gx", "gy", None),
            P("gx", "gy", None),
            P("gx", "gy", None),
            P("gx", "gy", None),
            P("gx", "gy", None),
            P(("gx", "gy"), None, None),
            P(("gx", "gy"), None, None),
            P(("gx", "gy"), None, None),
            P(("gx", "gy"), None, None, None),
            P(("gx", "gy"), None),
        ),
        out_specs=(P("gx", "gy", None), P("gx", "gy", None)),
        check_vma=False,
    )
```

```python
import functools

import jax
import jax.numpy as jnp
from jax import lax
from jax.experimental import pallas as pl
from jax.experimental.pallas import tpu as pltpu
from jax.sharding import PartitionSpec as P

TZ = 128
LINK = 4
SLOT = 4
F32 = jnp.float32
BF16 = jnp.bfloat16
MESH = pl.DeviceIdType.MESH
NT = (((1,), (1,)), ((), ()))
NN = (((1,), (0,)), ((), ()))
GROUP = 8
CHUNKS = 4


def log2(value):
    assert value & (value - 1) == 0
    return value.bit_length() - 1


def iota(shape, axis):
    return lax.broadcasted_iota(jnp.int32, shape, axis)


def split_two(value):
    first = value.astype(BF16).astype(F32)
    return first, (value - first).astype(BF16).astype(F32)


def stack_two(value, axis=0):
    return jnp.concatenate(split_two(value), axis=axis).astype(BF16)


def fold_two(value):
    half = value.shape[0] // 2
    return value[:half] + value[half:]


def fold_tiles(value):
    tiles = [
        value[y : y + 8, z : z + 128]
        for y in range(0, value.shape[0], 8)
        for z in range(0, value.shape[1], 128)
    ]
    while len(tiles) > 1:
        tiles = [a + b for a, b in zip(tiles[::2], tiles[1::2])]
    return tiles[0]


def write_one_hots(index_ref, hot_ref, turned_ref=None):
    group = hot_ref.shape[2] // 128

    def step(block, carry):
        for sub in range(group):
            index = index_ref[pl.ds(block * group + sub, 1), :]
            hot = jnp.where(iota((128, 128), 0) == (index & 127), 1.0, 0.0)
            hot_ref[block, :, sub * 128 : (sub + 1) * 128] = hot.astype(BF16)
            if turned_ref is not None:
                turned_ref[block, sub * 128 : (sub + 1) * 128, :] = hot.T.astype(BF16)
        return carry

    lax.fori_loop(0, hot_ref.shape[0], step, 0)


def in_chunks(count, step, carry, chunk=4):
    chunk = max(c for c in range(1, chunk + 1) if count % c == 0)

    def chunk_step(n, carry):
        for sub in range(chunk):
            carry = step(n * chunk + sub, carry)
        return carry

    if count == chunk:
        return chunk_step(0, carry)
    return lax.fori_loop(0, count // chunk, chunk_step, carry)


def gather_rows(table, index_ref, hot_ref, store):
    parts = stack_two(table)
    high_count = table.shape[0]
    group = hot_ref.shape[2] // 128

    def step(block, carry):
        picked = fold_two(
            lax.dot_general(parts, hot_ref[block], NN, preferred_element_type=F32)
        )
        for sub in range(group):
            row = block * group + sub
            hit = iota((high_count, 128), 0) == (index_ref[pl.ds(row, 1), :] >> 7)
            mine = picked[:, sub * 128 : (sub + 1) * 128]
            store(row, jnp.sum(jnp.where(hit, mine, 0.0), axis=0, keepdims=True))
        return carry

    in_chunks(hot_ref.shape[0], step, 0)


def scatter_rows(value_of, index_ref, hot_ref, high_count, dims=NT):
    group = max(hot_ref.shape[1:]) // 128

    def step(block, total):
        pieces = []
        for sub in range(group):
            row = block * group + sub
            hit = iota((high_count, 128), 0) == (index_ref[pl.ds(row, 1), :] >> 7)
            pieces.append(
                jnp.concatenate(
                    [jnp.where(hit, part, 0.0) for part in split_two(value_of(row))], axis=0
                ).astype(BF16)
            )
        return total + lax.dot_general(
            jnp.concatenate(pieces, axis=1), hot_ref[block], dims, preferred_element_type=F32
        )

    start = jnp.zeros((2 * high_count, 128), F32)
    return fold_two(in_chunks(hot_ref.shape[0], step, start))


def block_vectors(vectors):
    first, second = split_two(vectors)
    out = []
    for q in range(vectors.shape[0]):
        mine = iota(vectors.shape, 0) == q
        top = jnp.where(mine, first, 0.0)
        low = jnp.where(mine, second, 0.0)
        upper = jnp.concatenate([top, top], axis=1)
        lower = jnp.concatenate([low, jnp.zeros_like(low)], axis=1)
        out.append(jnp.concatenate([upper, lower], axis=0).astype(BF16))
    return out


def block_products(vectors, split_ref):
    total = None
    for q, part in enumerate(block_vectors(vectors)):
        term = lax.dot_general(part, split_ref[q], NN, preferred_element_type=F32)
        total = term if total is None else total + term
    return fold_two(total)


def kernel(
    counts,
    source_hbm,
    mob_x_hbm,
    mob_y_hbm,
    mob_z_hbm,
    fraction_hbm,
    inverse_hbm,
    couplings_hbm,
    send_ref,
    recv_ref,
    near_ref,
    res,
    direction,
    zed,
    image,
    image_two,
    gain_ref,
    gain_two_ref,
    mix_ref,
    mob_x,
    mob_y,
    mob_z,
    fraction,
    inverse,
    couplings,
    inv_diag,
    local,
    local_two,
    inverse_split,
    couplings_split,
    send_hot,
    recv_hot,
    recv_turned,
    back_hot,
    side_hot,
    send_map,
    back_map,
    side_map,
    totals_table,
    values_table,
    local_table,
    stencil_table,
    code_table,
    beside_table,
    beside_row,
    table_halo,
    low_mx,
    low_my,
    edge_my,
    edge_f,
    halo_fx,
    halo_fy,
    edges,
    halo_x,
    halo_y,
    row_send,
    row_recv,
    side_send,
    side_recv,
    link_send,
    link_recv,
    sum_send,
    sum_recv,
    load_sem,
    side_send_sem,
    side_recv_sem,
    early_send_sem,
    early_recv_sem,
    table_send_sem,
    table_recv_sem,
    row_send_sem,
    row_recv_sem,
    spread_send_sem,
    spread_recv_sem,
    link_send_sem,
    link_recv_sem,
    sum_send_sem,
    sum_recv_sem,
):
    count_x, count_y = counts
    devices = count_x * count_y
    assert devices & (devices - 1) == 0
    at_x, at_y = lax.axis_index("gx"), lax.axis_index("gy")
    me = at_x * count_y + at_y
    size_x, size_y, depth = res.shape
    tiles_z = depth // TZ
    group = 128 // (size_y * tiles_z)
    table_rows = size_x // group
    blocks = inverse.shape[0]
    push_count = near_ref.size

    loads = [
        pltpu.make_async_copy(src, dst, load_sem.at[n])
        for n, (src, dst) in enumerate(
            (
                (source_hbm, res),
                (fraction_hbm, fraction),
                (mob_y_hbm, mob_y),
                (mob_x_hbm, mob_x),
                (mob_z_hbm, mob_z),
                (inverse_hbm, inverse),
                (couplings_hbm, couplings),
            )
        )
    ]
    for load in loads:
        load.start()

    barrier = pltpu.get_barrier_semaphore()

    def peer(step):
        other = me ^ (devices - step)
        return (other // count_y, lax.rem(other, count_y)), other

    def greet(step, carry):
        pl.semaphore_signal(barrier, inc=1, device_id=peer(step)[0], device_id_type=MESH)
        return carry

    for ref in (low_mx, low_my, halo_fx, halo_fy, halo_x, halo_y, side_send):
        ref[...] = jnp.zeros_like(ref)
    table_halo[0] = jnp.zeros_like(table_halo[0])
    table_halo[1] = jnp.full_like(table_halo[1], -1.0)
    lax.fori_loop(1, devices, greet, 0)

    def exchange(send, recv, send_sem, recv_sem, same=False):
        def one(step, carry):
            device, other = peer(step)
            pltpu.make_async_remote_copy(
                src_ref=send.at[0 if same else other],
                dst_ref=recv.at[me],
                send_sem=send_sem,
                recv_sem=recv_sem,
                device_id=device,
                device_id_type=MESH,
            ).start()
            return carry

        lax.fori_loop(1, devices, one, 0)
        recv[me] = send[0 if same else me]

    def arrived(recv, recv_sem):
        part = recv.at[pl.ds(0, devices - 1)]
        pltpu.make_async_copy(part, part, recv_sem).wait()

    tile = send_ref[...]
    low = tile & 127
    tile_k = low & (tiles_z - 1)
    tile_j = (low >> log2(tiles_z)) & (size_y - 1)
    tile_g = low >> log2(tiles_z * size_y)
    send_map[...] = (
        (tile - low) + tile_k * (group * size_y) + tile_g * size_y + tile_j
    )

    def tile_sums(planes):
        stacked = jnp.concatenate(
            [plane[:, k * TZ : (k + 1) * TZ] for k in range(tiles_z) for plane in planes],
            axis=0,
        )
        return jnp.sum(stacked.T, axis=0, keepdims=True)

    def row_exchange(n):
        exchange(row_send.at[n], row_recv.at[n], row_send_sem.at[n], row_recv_sem.at[n])

    write_one_hots(send_map, send_hot)
    loads[0].wait()
    loads[1].wait()

    def first_totals(row, carry):
        xs = [row * group + g for g in range(group)]
        totals_table[0, pl.ds(row, 1), :] = tile_sums([fraction[x] * res[x] for x in xs])
        return carry

    in_chunks(table_rows, first_totals, 0)
    def to_owners(n):
        def store(row, value):
            row_send[n, row] = value

        return store

    gather_rows(totals_table[0], send_map, send_hot, to_owners(0))
    pl.semaphore_wait(barrier, devices - 1)
    row_exchange(0)

    def side_copy(src, dst, send_sem, recv_sem, shift_x, shift_y):
        return pltpu.make_async_remote_copy(
            src_ref=src,
            dst_ref=dst,
            send_sem=send_sem,
            recv_sem=recv_sem,
            device_id=(at_x + shift_x, at_y + shift_y),
            device_id_type=MESH,
        )

    has_low_x, has_high_x = at_x > 0, at_x < count_x - 1
    has_low_y, has_high_y = at_y > 0, at_y < count_y - 1
    sides = (
        (has_low_x, has_high_x, -1, 0),
        (has_high_x, has_low_x, 1, 0),
        (has_low_y, has_high_y, 0, -1),
        (has_high_y, has_low_y, 0, 1),
    )

    def side_group(parts, send_sem, recv_sem):
        out = []
        for n, (side, src, dst) in enumerate(parts):
            there, came, shift_x, shift_y = sides[side]
            copy = side_copy(src, dst, send_sem.at[n], recv_sem.at[n], shift_x, shift_y)
            out.append((there, came, copy))
        return out

    def start(copies):
        for there, came, copy in copies:
            pl.when(there)(copy.start)

    def came_in(copies):
        for there, came, copy in copies:
            pl.when(came)(copy.wait_recv)

    loads[2].wait()
    loads[3].wait()

    def take_edge(x, carry):
        edge_my[x] = mob_y[x, size_y - 1 : size_y, :]
        edge_f[0, x] = fraction[x, 0:1, :]
        edge_f[1, x] = fraction[x, size_y - 1 : size_y, :]
        return carry

    lax.fori_loop(0, size_x, take_edge, 0)
    early = side_group(
        (
            (1, mob_x.at[size_x - 1], low_mx),
            (3, edge_my, low_my),
            (0, fraction.at[0], halo_fx.at[1]),
            (1, fraction.at[size_x - 1], halo_fx.at[0]),
            (2, edge_f.at[0], halo_fy.at[1]),
            (3, edge_f.at[1], halo_fy.at[0]),
        ),
        early_send_sem,
        early_recv_sem,
    )
    start(early)

    near_row = jnp.concatenate([near_ref[k : k + 1] for k in range(near_ref.shape[0])], axis=1)
    target_row = near_row >> log2(blocks)
    down, across = iota((push_count, push_count), 0), iota((push_count, push_count), 1)
    target_col = jnp.sum(
        jnp.where(down == across, target_row.astype(F32), 0.0), axis=1, keepdims=True
    ).astype(jnp.int32)
    earlier = down < across
    same = jnp.where((target_row == target_col) & earlier, 1, 0)
    rank = jnp.sum(same, axis=0, keepdims=True)
    slot = target_row * SLOT + rank
    chosen = iota((devices * SLOT, push_count), 0) == slot
    local_block = (near_row & (blocks - 1)).astype(F32)
    identity = jnp.sum(jnp.where(chosen, local_block, 0.0), axis=1, keepdims=True)
    link_send[0] = jnp.broadcast_to(identity, (devices * SLOT, 128)).reshape(
        devices, SLOT, 128
    )
    spread = jnp.where(chosen, 1.0, 0.0).astype(BF16)

    def link_exchange(n):
        exchange(link_send.at[n], link_recv.at[n], link_send_sem.at[n], link_recv_sem.at[n])

    link_exchange(0)

    lane = iota((size_y, depth), 1)
    row_of = iota((size_y, depth), 0)

    def below_z(plane):
        return jnp.where(lane == 0, 0.0, pltpu.roll(plane, 1, 1))

    def above_z(plane):
        return jnp.where(lane == depth - 1, 0.0, pltpu.roll(plane, depth - 1, 1))

    def below_y(plane, edge):
        return jnp.where(row_of == 0, edge, pltpu.roll(plane, 1, 0))

    def above_y(plane, edge):
        return jnp.where(row_of == size_y - 1, edge, pltpu.roll(plane, size_y - 1, 0))

    wide = group * size_y
    slot_of = iota((table_rows, 128), 1)
    slot_y = slot_of & (size_y - 1)
    slot_g = (slot_of >> log2(size_y)) & (group - 1)
    slot_k = slot_of >> log2(wide)

    def turn(table, shift):
        return pltpu.roll(table, shift % 128, 1) if shift % 128 else table

    def next_x(table, high):
        inner = turn(table, -size_y)
        outer = turn(jnp.concatenate([table[1:], high], axis=0), (group - 1) * size_y)
        return jnp.where(slot_g < group - 1, inner, outer)

    def last_x(table, low):
        inner = turn(table, size_y)
        outer = turn(
            jnp.concatenate([low, table[: table_rows - 1]], axis=0), -(group - 1) * size_y
        )
        return jnp.where(slot_g > 0, inner, outer)

    def next_y(table, high):
        return jnp.where(slot_y < size_y - 1, turn(table, -1), high)

    def last_y(table, low):
        return jnp.where(slot_y > 0, turn(table, 1), low)

    def next_z(table):
        return jnp.where(slot_k < tiles_z - 1, turn(table, -wide), 0.0)

    def last_z(table):
        return jnp.where(slot_k > 0, turn(table, wide), 0.0)

    write_one_hots(recv_ref, recv_hot, recv_turned)
    loads[5].wait()

    def split_inverse(q, carry):
        inverse_split[q] = stack_two(inverse[q].T)
        return carry

    in_chunks(blocks, split_inverse, 0)
    loads[6].wait()

    def fold_couplings(q, carry):
        both = jnp.concatenate([couplings[q, k] for k in range(couplings.shape[1])], axis=0)
        upper, lower = split_two(both)
        top, rest = inverse_split[q, : inverse.shape[1]], inverse_split[q, inverse.shape[1] :]
        product = lax.dot_general(
            jnp.concatenate([top, rest, top], axis=1),
            jnp.concatenate([upper, upper, lower], axis=1).astype(BF16),
            NT,
            preferred_element_type=F32,
        )
        couplings_split[q] = stack_two(product)
        return carry

    in_chunks(blocks, fold_couplings, 0)

    place = iota((1, 128), 1)

    zero_tile = jnp.zeros((8, 128), F32)
    fields = (local, direction, local_two, zed)

    def keep_edges(phase, x, value):
        edges[phase, 0, x] = value[0:1]
        edges[phase, 1, x] = value[size_y - 1 : size_y]

    def halo_copies(phase):
        field = fields[2 * phase]
        return side_group(
            (
                (0, field.at[0], halo_x.at[2 * phase, 1]),
                (1, field.at[size_x - 1], halo_x.at[2 * phase, 0]),
                (2, edges.at[phase, 0], halo_y.at[2 * phase, 1]),
                (3, edges.at[phase, 1], halo_y.at[2 * phase, 0]),
            ),
            side_send_sem.at[phase],
            side_recv_sem.at[phase],
        )

    def prepare(row, lower, above, total):
        whole, across_x, across_y, across_z = [], [], [], []
        for g in range(group):
            x = row * group + g
            mob_a, mob_b, mob_c = mob_x[x], mob_y[x], mob_z[x]
            weight, source = fraction[x], res[x]
            diagonal = (
                (mob_a + lower) + (mob_b + below_y(mob_b, low_my[x])) + (mob_c + below_z(mob_c))
            )
            inverse_here = 1.0 / diagonal
            value = source * inverse_here
            inv_diag[x] = inverse_here
            local[x] = value
            keep_edges(0, x, value)
            total = total + fold_tiles(source * value)
            up = fraction[x + 1] if g < group - 1 or above is None else above
            whole.append(diagonal * (weight * weight))
            across_x.append(mob_a * weight * up)
            across_y.append(mob_b * weight * above_y(weight, halo_fy[1, x]))
            across_z.append(mob_c * weight * above_z(weight))
            lower = mob_a
        here = pl.ds(row, 1)
        stencil_table[1, here, :] = tile_sums(across_x)
        stencil_table[3, here, :] = tile_sums(across_y)
        turned = jnp.concatenate(
            [p[:, k * TZ : (k + 1) * TZ] for k in range(tiles_z) for p in across_z], axis=0
        ).T
        crossing = turned[TZ - 1 : TZ]
        inside = jnp.sum(turned, axis=0, keepdims=True) - crossing
        stencil_table[5, here, :] = crossing
        stencil_table[0, here, :] = tile_sums(whole) - 2.0 * inside
        return lower, total

    def table_copies(n, pairs):
        return side_group(
            [(side, src, table_halo.at[n, side]) for side, src in pairs],
            table_send_sem.at[n],
            table_recv_sem.at[n],
        )

    def apply_operator(phase, emit):
        field = fields[phase]

        def group_step(row, here, flux_low, carry, top):
            values = []
            for g in range(group):
                x = row * group + g
                above = top if top is not None and g == group - 1 else field[x + 1]
                flux_x = mob_x[x] * (above - here)
                flux_y = mob_y[x] * (above_y(here, halo_y[phase, 1, x]) - here)
                edge = low_my[x] * (here[0:1] - halo_y[phase, 0, x])
                flux_z = mob_z[x] * (above_z(here) - here)
                value = (
                    (flux_low - flux_x)
                    + (below_y(flux_y, edge) - flux_y)
                    + (below_z(flux_z) - flux_z)
                )
                values.append((here, value))
                here, flux_low = above, flux_x
            return here, flux_low, emit(row, values, carry)

        first = field[0]
        flux = low_mx[...] * (first - halo_x[phase, 0])
        state = (first, flux, zero_tile)
        state = in_chunks(table_rows - 1, lambda row, s: group_step(row, *s, None), state, 3)
        return jnp.sum(group_step(table_rows - 1, *state, halo_x[phase, 1])[2])

    def emit_local(n):
        def emit(row, values, total):
            parts = []
            for g, (here, value) in enumerate(values):
                total = total + fold_tiles(here * value)
                parts.append(fraction[row * group + g] * value)
            local_table[n, pl.ds(row, 1), :] = tile_sums(parts)
            return total

        return emit

    def emit_field(result):
        def emit(row, values, total):
            for g, (here, value) in enumerate(values):
                result[row * group + g] = value
            return total

        return emit

    def coarse_totals(phase):
        arrived(row_recv.at[phase], row_recv_sem.at[phase])
        return scatter_rows(
            lambda row: row_recv[phase, row], recv_ref, recv_turned, blocks, NN
        )

    def sweep_first(phase, totals):
        both = block_products(totals, couplings_split)
        pushed = jnp.concatenate(
            [both[:, k * 128 : (k + 1) * 128] for k in range(couplings.shape[1])], axis=0
        )
        upper, lower = split_two(pushed)
        out_values = lax.dot_general(
            spread, upper.astype(BF16), NN, preferred_element_type=F32
        ) + lax.dot_general(spread, lower.astype(BF16), NN, preferred_element_type=F32)
        link_send[1 + phase] = out_values.reshape(devices, SLOT, 128)
        link_exchange(1 + phase)

    def sweep_second(phase, totals, gather_in):
        arrived(link_recv.at[1 + phase], link_recv_sem.at[1 + phase])
        values = stack_two(link_recv[1 + phase].reshape(devices * SLOT, 128), axis=1)
        summed = lax.dot_general(gather_in, values, NN, preferred_element_type=F32)
        coupled = summed[:, :128] + summed[:, 128:]
        sweep_two = block_products(totals - coupled, inverse_split)

        def store(row, value):
            side_send[phase, row + count_y, 0] = value
            side_send[phase, row, 1] = value
            side_send[phase, row + 2 * count_y, 2] = value
            side_send[phase, row + count_y - 1, 3] = value
            side_send[phase, row + count_y + 1, 4] = value

        gather_rows(sweep_two, recv_ref, recv_hot, store)

        def one(step, carry):
            device, other = peer(step)
            pltpu.make_async_remote_copy(
                src_ref=side_send.at[phase, other + count_y],
                dst_ref=side_recv.at[phase, :, me],
                send_sem=spread_send_sem.at[phase],
                recv_sem=spread_recv_sem.at[phase],
                device_id=device,
                device_id_type=MESH,
            ).start()
            return carry

        lax.fori_loop(1, devices, one, 0)
        side_recv[phase, :, me] = side_send[phase, me + count_y]

    def spread_done(phase, sem):
        part = side_recv.at[phase, :, pl.ds(0, devices - 1)]
        pltpu.make_async_copy(part, part, sem).wait()

    def tile_values(phase):
        spread_done(phase, spread_recv_sem.at[phase])

        def store(row, value):
            values_table[phase, pl.ds(row, 1), :] = value

        def rows_of(n):
            return side_recv[phase, n].reshape(devices, 128)

        gather_rows(rows_of(0), back_map, back_hot, store)
        beside = []
        gather_rows(
            jnp.concatenate([rows_of(1 + n) for n in range(4)], axis=0),
            side_map,
            side_hot,
            lambda row, value: beside.append(value),
        )
        packed = jnp.broadcast_to(beside[1], (table_rows, 128))
        high_y = pltpu.roll(packed, size_y - table_rows, 1, stride=1, stride_axis=0)
        low_y = pltpu.roll(packed, 1, 1, stride=1, stride_axis=0)
        beside_table[phase] = jnp.where(slot_y == 0, low_y, high_y)
        beside_row[phase] = beside[0]
        return beside[0], low_y, high_y

    def spread_tiles(row):
        return jnp.broadcast_to(row, (128, 128)).T

    def make_field(phase):
        n = 2 * phase + 1
        field, plus = fields[n], fields[2 * phase]

        def tile_part(stacked, g, first, count):
            return jnp.concatenate(
                [
                    stacked[
                        (k * group + g) * size_y + first : (k * group + g) * size_y + first + count
                    ]
                    for k in range(tiles_z)
                ],
                axis=1,
            )

        def step(row, carry):
            stacked = spread_tiles(values_table[phase, pl.ds(row, 1), :])
            beside = spread_tiles(beside_table[phase, pl.ds(row, 1), :])
            for g in range(group):
                x = row * group + g
                field[x] = fraction[x] * tile_part(stacked, g, 0, size_y) + plus[x]
                for side in range(2):
                    value = tile_part(beside, g, side * (size_y - 1), 1)
                    halo_y[n, side, x] = halo_fy[side, x] * value + halo_y[n - 1, side, x]
            return carry

        in_chunks(table_rows, step, 0)
        stacked = spread_tiles(beside_row[phase])
        for side, g in ((0, group - 1), (1, 0)):
            value = tile_part(stacked, g, 0, size_y)
            halo_x[n, side] = halo_fx[side] * value + halo_x[n - 1, side]

    def tile_operator(phase, beside_x, low_y, high_y):
        table = values_table[phase]
        return (
            stencil_table[0] * table
            - (
                stencil_table[1] * next_x(table, beside_x)
                + stencil_table[2] * last_x(table, beside_x)
            )
            - (
                stencil_table[3] * next_y(table, high_y)
                + stencil_table[4] * last_y(table, low_y)
            )
            - (stencil_table[5] * next_z(table) + stencil_table[6] * last_z(table))
        )

    def start_sums(phase, values):
        row = jnp.zeros((1, 128), F32)
        for n, value in enumerate(values):
            row = jnp.where(place == n, value, row)
        sum_send[phase, 0] = row
        exchange(
            sum_send.at[phase],
            sum_recv.at[phase],
            sum_send_sem.at[phase],
            sum_recv_sem.at[phase],
            same=True,
        )

    def end_sums(phase, count):
        arrived(sum_recv.at[phase], sum_recv_sem.at[phase])
        totals = [sum_recv[phase, n] for n in range(4)]
        for n in range(4, devices):
            totals[n % 4] = totals[n % 4] + sum_recv[phase, n]
        total = (totals[0] + totals[1]) + (totals[2] + totals[3])
        return [
            jnp.sum(jnp.where(place == n, total, 0.0), axis=1, keepdims=True)
            for n in range(count)
        ]

    totals = coarse_totals(0)
    sweep_first(0, totals)

    codes = scatter_rows(
        lambda row: (row * 128 + place).astype(F32), send_map, send_hot, table_rows
    )
    code_table[...] = codes
    back_map[...] = codes.astype(jnp.int32)
    waits = [early, table_copies(1, [(side, code_table) for side in range(4)])]
    start(waits[1])
    loads[4].wait()
    came_in(early)
    lower, total = in_chunks(
        table_rows - 1,
        lambda row, s: prepare(row, s[0], None, s[1]),
        (low_mx[...], zero_tile),
        3,
    )
    _, total = prepare(table_rows - 1, lower, halo_fx[1], total)
    source_local = jnp.sum(total)
    waits.append(halo_copies(0))
    start(waits[2])
    waits.append(table_copies(0, ((1, stencil_table.at[1]), (3, stencil_table.at[3]))))
    start(waits[3])
    arrived(link_recv.at[0], link_recv_sem.at[0])
    names = link_recv[0].reshape(devices * SLOT, 128).T[:blocks]
    gather_in = jnp.where(
        names == iota((blocks, devices * SLOT), 0).astype(F32), 1.0, 0.0
    ).astype(BF16)

    sweep_second(0, totals, gather_in)

    write_one_hots(back_map, back_hot)
    came_in(waits[1])
    across_y, across_g = slot_y[:1], slot_g[:1]
    code_x = jnp.where(
        across_g == 0,
        table_halo[1, 0, 0:1],
        jnp.where(across_g == group - 1, table_halo[1, 1, table_rows - 1 :], -1.0),
    )
    code_y = jnp.full((1, 128), -1.0, F32)
    for r in range(table_rows):
        high = turn(table_halo[1, 2, r : r + 1], table_rows - 1 - r)
        low = turn(table_halo[1, 3, r : r + 1], -size_y - r)
        code_y = jnp.where(across_y == table_rows - 1 - r, high, code_y)
        code_y = jnp.where(across_y == size_y - 1 - r, low, code_y)
    span = devices * 128
    code_x, code_y = code_x.astype(jnp.int32), code_y.astype(jnp.int32)
    shift_x = jnp.where(across_g == 0, 0, span)
    shift_y = jnp.where(across_y < table_rows, 2 * span, 3 * span)
    side_map[0:1] = jnp.where(code_x < 0, -1, code_x + shift_x)
    side_map[1:2] = jnp.where(code_y < 0, -1, code_y + shift_y)
    write_one_hots(side_map, side_hot)
    came_in(waits[3])
    stencil_table[2] = last_x(stencil_table[1], table_halo[0, 1, table_rows - 1 :])
    stencil_table[4] = last_y(stencil_table[3], turn(table_halo[0, 3], 1 - size_y))
    stencil_table[6] = last_z(stencil_table[5])
    came_in(waits[2])
    local_energy = apply_operator(0, emit_local(0))

    beside = tile_values(0)
    operated = tile_operator(0, *beside)
    image_totals = operated + local_table[0]
    totals_table[1] = image_totals
    gather_rows(image_totals, send_map, send_hot, to_owners(1))
    row_exchange(1)
    values = values_table[0]
    rz_part = jnp.sum(totals_table[0] * values) + source_local
    energy_part = jnp.sum(values * (image_totals + local_table[0])) + local_energy
    start_sums(0, (rz_part, energy_part))

    make_field(0)

    rz, energy = end_sums(0, 2)
    alpha = rz / energy
    totals = totals - alpha * coarse_totals(1)
    sweep_first(1, totals)

    apply_operator(1, emit_field(image))

    def update(x, carry):
        own, cross = carry
        pushed = image[x]
        here = res[x] - alpha * pushed
        value = inv_diag[x] * here
        res[x] = here
        local_two[x] = value
        keep_edges(1, x, value)
        return own + fold_tiles(here * value), cross + fold_tiles(value * pushed)

    own, cross = in_chunks(size_x, update, (zero_tile, zero_tile))
    residual_local, cross_local = jnp.sum(own), jnp.sum(cross)
    waits.append(halo_copies(1))
    start(waits[4])

    sweep_second(1, totals, gather_in)

    came_in(waits[4])
    local_energy = apply_operator(2, emit_local(1))

    beside = tile_values(1)
    operated = tile_operator(1, *beside)
    values = values_table[1]
    tile_totals = totals_table[0] - alpha * totals_table[1]
    next_part = jnp.sum(tile_totals * values) + residual_local
    own_part = jnp.sum(values * (operated + 2.0 * local_table[1])) + local_energy
    cross_part = jnp.sum(values * totals_table[1]) + cross_local
    start_sums(1, (next_part, own_part, cross_part))

    make_field(1)
    apply_operator(3, emit_field(image_two))

    rz_next, own, cross = end_sums(1, 3)
    beta = rz_next / rz
    alpha_two = rz_next / (own + beta * (2.0 * cross + beta * energy))

    for ref, value in ((gain_ref, alpha), (gain_two_ref, alpha_two), (mix_ref, beta)):
        ref[...] = jnp.broadcast_to(value, ref.shape)
    for copies in waits:
        for there, came, copy in copies:
            pl.when(there)(copy.wait_send)
    for n in range(2):
        arrived(row_send.at[n], row_send_sem.at[n])
        spread_done(n, spread_send_sem.at[n])
    for n in range(3):
        arrived(link_send.at[n], link_send_sem.at[n])
    for n in range(2):
        arrived(sum_recv.at[n], sum_send_sem.at[n])


def finish(
    direction, zed, res, image_two, image, gain_ref, gain_two_ref, mix_ref, x_hbm, r_hbm, x, r, sem
):
    alpha, alpha_two, beta = gain_ref[...], gain_two_ref[...], mix_ref[...]
    planes = x.shape[0] // CHUNKS
    copies = []
    for n in range(CHUNKS):
        for p in range(n * planes, (n + 1) * planes):
            first = direction[p]
            x[p] = alpha * first + alpha_two * (zed[p] + beta * first)
            r[p] = res[p] - alpha_two * (image_two[p] + beta * image[p])
        part = pl.ds(n * planes, planes)
        for k, (src, dst) in enumerate(((x, x_hbm), (r, r_hbm))):
            copies.append(pltpu.make_async_copy(src.at[part], dst.at[part], sem.at[k, n]))
            copies[-1].start()
    for copy in copies:
        copy.wait()


def body(
    source_term,
    mobility_x,
    mobility_y,
    mobility_z,
    bubble_fraction,
    tile_labels,
    send_tiles,
    recv_rows,
    block_inverse,
    couplings,
    neighbours,
):
    count_x, count_y = lax.axis_size("gx"), lax.axis_size("gy")
    devices = count_x * count_y
    size_x, size_y, depth = source_term.shape
    tiles = size_x * size_y * (depth // TZ)
    blocks, order = block_inverse.shape[:2]
    send, recv = send_tiles[0], recv_rows[0]
    pad = 128 - send.shape[1]
    assert order == 128 and pad >= 0
    if pad:
        send = jnp.pad(send, ((0, 0), (0, pad)), constant_values=tiles)
        recv = jnp.pad(recv, ((0, 0), (0, pad)), constant_values=blocks * order)
    table_rows = tiles // 128
    field = (size_x, size_y, depth)
    hbm = pl.BlockSpec(memory_space=pltpu.HBM)
    vmem = pl.BlockSpec(memory_space=pltpu.VMEM)
    dma = pltpu.SemaphoreType.DMA
    res, direction, zed, image, image_two, *gains = pl.pallas_call(
        functools.partial(kernel, (count_x, count_y)),
        out_shape=(*[pltpu.VMEM(field, F32)] * 5, *[pltpu.VMEM((1, depth), F32)] * 3),
        in_specs=[hbm] * 7 + [vmem] * 3,
        out_specs=(vmem,) * 8,
        scratch_shapes=[
            *[pltpu.VMEM(field, F32)] * 4,
            pltpu.VMEM((blocks, order, order), F32),
            pltpu.VMEM(couplings.shape, F32),
            *[pltpu.VMEM(field, F32)] * 3,
            pltpu.VMEM((blocks, 2 * order, order), BF16),
            pltpu.VMEM((blocks, 2 * order, order * couplings.shape[1]), BF16),
            pltpu.VMEM((devices // GROUP, 128, GROUP * 128), BF16),
            pltpu.VMEM((devices // GROUP, 128, GROUP * 128), BF16),
            pltpu.VMEM((devices // GROUP, GROUP * 128, 128), BF16),
            pltpu.VMEM((table_rows // GROUP, 128, GROUP * 128), BF16),
            pltpu.VMEM((1, 128, 2 * 128), BF16),
            pltpu.VMEM((devices, 128), jnp.int32),
            pltpu.VMEM((table_rows, 128), jnp.int32),
            pltpu.VMEM((2, 128), jnp.int32),
            pltpu.VMEM((2, table_rows, 128), F32),
            pltpu.VMEM((2, table_rows, 128), F32),
            pltpu.VMEM((2, table_rows, 128), F32),
            pltpu.VMEM((7, table_rows, 128), F32),
            pltpu.VMEM((table_rows, 128), F32),
            pltpu.VMEM((2, table_rows, 128), F32),
            pltpu.VMEM((2, 1, 128), F32),
            pltpu.VMEM((2, 4, table_rows, 128), F32),
            pltpu.VMEM((size_y, depth), F32),
            pltpu.VMEM((size_x, 1, depth), F32),
            pltpu.VMEM((size_x, 1, depth), F32),
            pltpu.VMEM((2, size_x, 1, depth), F32),
            pltpu.VMEM((2, size_y, depth), F32),
            pltpu.VMEM((2, size_x, 1, depth), F32),
            pltpu.VMEM((2, 2, size_x, 1, depth), F32),
            pltpu.VMEM((4, 2, size_y, depth), F32),
            pltpu.VMEM((4, 2, size_x, 1, depth), F32),
            pltpu.VMEM((2, devices, 1, 128), F32),
            pltpu.VMEM((2, devices, 1, 128), F32),
            pltpu.VMEM((2, devices + 2 * count_y, 5, 1, 128), F32),
            pltpu.VMEM((2, 5, devices, 1, 128), F32),
            pltpu.VMEM((3, devices, SLOT, 128), F32),
            pltpu.VMEM((3, devices, SLOT, 128), F32),
            pltpu.VMEM((2, 1, 1, 128), F32),
            pltpu.VMEM((2, devices, 1, 128), F32),
            dma((7,)),
            dma((2, 4)),
            dma((2, 4)),
            dma((6,)),
            dma((6,)),
            dma((2, 4)),
            dma((2, 4)),
            dma((2,)),
            dma((2,)),
            dma((2,)),
            dma((2,)),
            dma((3,)),
            dma((3,)),
            dma((2,)),
            dma((2,)),
        ],
        compiler_params=pltpu.CompilerParams(
            collective_id=0, has_side_effects=True, vmem_limit_bytes=61000000
        ),
    )(
        source_term,
        mobility_x,
        mobility_y,
        mobility_z,
        bubble_fraction,
        block_inverse,
        couplings,
        send,
        recv,
        neighbours.T,
    )
    return tuple(
        pl.pallas_call(
            finish,
            out_shape=(jax.ShapeDtypeStruct(field, F32), jax.ShapeDtypeStruct(field, F32)),
            in_specs=[vmem] * 8,
            out_specs=(hbm, hbm),
            scratch_shapes=[
                pltpu.VMEM(field, F32),
                pltpu.VMEM(field, F32),
                dma((2, CHUNKS)),
            ],
            compiler_params=pltpu.CompilerParams(vmem_limit_bytes=50000000),
        )(direction, zed, res, image_two, image, *gains)
    )


def solution(mesh):
    return jax.shard_map(
        body,
        mesh=mesh,
        in_specs=(
            P("gx", "gy", None),
            P("gx", "gy", None),
            P("gx", "gy", None),
            P("gx", "gy", None),
            P("gx", "gy", None),
            P("gx", "gy", None),
            P(("gx", "gy"), None, None),
            P(("gx", "gy"), None, None),
            P(("gx", "gy"), None, None),
            P(("gx", "gy"), None, None, None),
            P(("gx", "gy"), None),
        ),
        out_specs=(P("gx", "gy", None), P("gx", "gy", None)),
        check_vma=False,
    )
```

```python
import functools

import jax
import jax.numpy as jnp
from jax import lax
from jax.experimental import pallas as pl
from jax.experimental.pallas import tpu as pltpu
from jax.sharding import PartitionSpec as P

TZ = 128
LINK = 4
SLOT = 4
F32 = jnp.float32
BF16 = jnp.bfloat16
MESH = pl.DeviceIdType.MESH
NT = (((1,), (1,)), ((), ()))
NN = (((1,), (0,)), ((), ()))
GROUP = 8
CHUNKS = 4


def log2(value):
    assert value & (value - 1) == 0
    return value.bit_length() - 1


def iota(shape, axis):
    return lax.broadcasted_iota(jnp.int32, shape, axis)


def split_two(value):
    first = value.astype(BF16).astype(F32)
    return first, (value - first).astype(BF16).astype(F32)


def stack_two(value, axis=0):
    return jnp.concatenate(split_two(value), axis=axis).astype(BF16)


def fold_two(value):
    half = value.shape[0] // 2
    return value[:half] + value[half:]


def fold_tiles(value):
    tiles = [
        value[y : y + 8, z : z + 128]
        for y in range(0, value.shape[0], 8)
        for z in range(0, value.shape[1], 128)
    ]
    while len(tiles) > 1:
        tiles = [a + b for a, b in zip(tiles[::2], tiles[1::2])]
    return tiles[0]


def write_one_hots(index_ref, hot_ref, turned_ref=None):
    group = hot_ref.shape[2] // 128

    def step(block, carry):
        for sub in range(group):
            index = index_ref[pl.ds(block * group + sub, 1), :]
            hot = jnp.where(iota((128, 128), 0) == (index & 127), 1.0, 0.0)
            hot_ref[block, :, sub * 128 : (sub + 1) * 128] = hot.astype(BF16)
            if turned_ref is not None:
                turned_ref[block, sub * 128 : (sub + 1) * 128, :] = hot.T.astype(BF16)
        return carry

    lax.fori_loop(0, hot_ref.shape[0], step, 0)


def in_chunks(count, step, carry, chunk=4):
    chunk = max(c for c in range(1, chunk + 1) if count % c == 0)

    def chunk_step(n, carry):
        for sub in range(chunk):
            carry = step(n * chunk + sub, carry)
        return carry

    if count == chunk:
        return chunk_step(0, carry)
    return lax.fori_loop(0, count // chunk, chunk_step, carry)


def gather_rows(table, index_ref, hot_ref, store):
    parts = stack_two(table)
    high_count = table.shape[0]
    group = hot_ref.shape[2] // 128

    def step(block, carry):
        picked = fold_two(
            lax.dot_general(parts, hot_ref[block], NN, preferred_element_type=F32)
        )
        for sub in range(group):
            row = block * group + sub
            hit = iota((high_count, 128), 0) == (index_ref[pl.ds(row, 1), :] >> 7)
            mine = picked[:, sub * 128 : (sub + 1) * 128]
            store(row, jnp.sum(jnp.where(hit, mine, 0.0), axis=0, keepdims=True))
        return carry

    in_chunks(hot_ref.shape[0], step, 0)


def scatter_rows(value_of, index_ref, hot_ref, high_count, dims=NT):
    group = max(hot_ref.shape[1:]) // 128

    def step(block, total):
        pieces = []
        for sub in range(group):
            row = block * group + sub
            hit = iota((high_count, 128), 0) == (index_ref[pl.ds(row, 1), :] >> 7)
            pieces.append(
                jnp.concatenate(
                    [jnp.where(hit, part, 0.0) for part in split_two(value_of(row))], axis=0
                ).astype(BF16)
            )
        return total + lax.dot_general(
            jnp.concatenate(pieces, axis=1), hot_ref[block], dims, preferred_element_type=F32
        )

    start = jnp.zeros((2 * high_count, 128), F32)
    return fold_two(in_chunks(hot_ref.shape[0], step, start))


def block_vectors(vectors):
    first, second = split_two(vectors)
    out = []
    for q in range(vectors.shape[0]):
        mine = iota(vectors.shape, 0) == q
        top = jnp.where(mine, first, 0.0)
        low = jnp.where(mine, second, 0.0)
        upper = jnp.concatenate([top, top], axis=1)
        lower = jnp.concatenate([low, jnp.zeros_like(low)], axis=1)
        out.append(jnp.concatenate([upper, lower], axis=0).astype(BF16))
    return out


def block_products(vectors, split_ref):
    total = None
    for q, part in enumerate(block_vectors(vectors)):
        term = lax.dot_general(part, split_ref[q], NN, preferred_element_type=F32)
        total = term if total is None else total + term
    return fold_two(total)


def kernel(
    counts,
    source_hbm,
    mob_x_hbm,
    mob_y_hbm,
    mob_z_hbm,
    fraction_hbm,
    inverse_hbm,
    couplings_hbm,
    send_ref,
    recv_ref,
    near_ref,
    res,
    direction,
    zed,
    image,
    image_two,
    gain_ref,
    gain_two_ref,
    mix_ref,
    mob_x,
    mob_y,
    mob_z,
    fraction,
    inverse,
    couplings,
    inv_diag,
    local,
    local_two,
    inverse_split,
    couplings_split,
    send_hot,
    recv_hot,
    recv_turned,
    back_hot,
    side_hot,
    send_map,
    back_map,
    side_map,
    totals_table,
    values_table,
    local_table,
    stencil_table,
    code_table,
    beside_table,
    beside_row,
    table_halo,
    low_mx,
    low_my,
    edge_my,
    edge_f,
    halo_fx,
    halo_fy,
    edges,
    halo_x,
    halo_y,
    row_send,
    row_recv,
    side_send,
    side_recv,
    link_send,
    link_recv,
    sum_send,
    sum_recv,
    load_sem,
    side_send_sem,
    side_recv_sem,
    early_send_sem,
    early_recv_sem,
    table_send_sem,
    table_recv_sem,
    row_send_sem,
    row_recv_sem,
    spread_send_sem,
    spread_recv_sem,
    link_send_sem,
    link_recv_sem,
    sum_send_sem,
    sum_recv_sem,
):
    count_x, count_y = counts
    devices = count_x * count_y
    assert devices & (devices - 1) == 0
    at_x, at_y = lax.axis_index("gx"), lax.axis_index("gy")
    me = at_x * count_y + at_y
    size_x, size_y, depth = res.shape
    tiles_z = depth // TZ
    group = 128 // (size_y * tiles_z)
    table_rows = size_x // group
    blocks = inverse.shape[0]
    push_count = near_ref.size

    loads = [
        pltpu.make_async_copy(src, dst, load_sem.at[n])
        for n, (src, dst) in enumerate(
            (
                (source_hbm, res),
                (fraction_hbm, fraction),
                (mob_y_hbm, mob_y),
                (mob_x_hbm, mob_x),
                (mob_z_hbm, mob_z),
                (inverse_hbm, inverse),
                (couplings_hbm, couplings),
            )
        )
    ]
    for load in loads:
        load.start()

    barrier = pltpu.get_barrier_semaphore()

    def peer(step):
        other = me ^ (devices - step)
        return (other // count_y, lax.rem(other, count_y)), other

    def greet(step, carry):
        pl.semaphore_signal(barrier, inc=1, device_id=peer(step)[0], device_id_type=MESH)
        return carry

    for ref in (low_mx, low_my, halo_fx, halo_fy):
        ref[...] = jnp.zeros_like(ref)
    for ref in (halo_x, halo_y):
        for phase in (0, 2):
            ref[phase] = jnp.zeros_like(ref[phase])
    table_halo[0] = jnp.zeros_like(table_halo[0])
    table_halo[1] = jnp.full_like(table_halo[1], -1.0)
    lax.fori_loop(1, devices, greet, 0)
    side_send[...] = jnp.zeros_like(side_send)

    def exchange(send, recv, send_sem, recv_sem, same=False):
        def one(step, carry):
            device, other = peer(step)
            pltpu.make_async_remote_copy(
                src_ref=send.at[0 if same else other],
                dst_ref=recv.at[me],
                send_sem=send_sem,
                recv_sem=recv_sem,
                device_id=device,
                device_id_type=MESH,
            ).start()
            return carry

        lax.fori_loop(1, devices, one, 0)
        recv[me] = send[0 if same else me]

    def arrived(recv, recv_sem):
        part = recv.at[pl.ds(0, devices - 1)]
        pltpu.make_async_copy(part, part, recv_sem).wait()

    tile = send_ref[...]
    low = tile & 127
    tile_k = low & (tiles_z - 1)
    tile_j = (low >> log2(tiles_z)) & (size_y - 1)
    tile_g = low >> log2(tiles_z * size_y)
    send_map[...] = (
        (tile - low) + tile_k * (group * size_y) + tile_g * size_y + tile_j
    )

    def tile_sums(planes):
        stacked = jnp.concatenate(
            [plane[:, k * TZ : (k + 1) * TZ] for k in range(tiles_z) for plane in planes],
            axis=0,
        )
        return jnp.sum(stacked.T, axis=0, keepdims=True)

    def row_exchange(n):
        exchange(row_send.at[n], row_recv.at[n], row_send_sem.at[n], row_recv_sem.at[n])

    write_one_hots(send_map, send_hot)
    loads[0].wait()
    loads[1].wait()

    def first_totals(row, carry):
        xs = [row * group + g for g in range(group)]
        totals_table[0, pl.ds(row, 1), :] = tile_sums([fraction[x] * res[x] for x in xs])
        return carry

    in_chunks(table_rows, first_totals, 0)
    def to_owners(n):
        def store(row, value):
            row_send[n, row] = value

        return store

    gather_rows(totals_table[0], send_map, send_hot, to_owners(0))
    pl.semaphore_wait(barrier, devices - 1)
    row_exchange(0)

    def side_copy(src, dst, send_sem, recv_sem, shift_x, shift_y):
        return pltpu.make_async_remote_copy(
            src_ref=src,
            dst_ref=dst,
            send_sem=send_sem,
            recv_sem=recv_sem,
            device_id=(at_x + shift_x, at_y + shift_y),
            device_id_type=MESH,
        )

    has_low_x, has_high_x = at_x > 0, at_x < count_x - 1
    has_low_y, has_high_y = at_y > 0, at_y < count_y - 1
    sides = (
        (has_low_x, has_high_x, -1, 0),
        (has_high_x, has_low_x, 1, 0),
        (has_low_y, has_high_y, 0, -1),
        (has_high_y, has_low_y, 0, 1),
    )

    def side_group(parts, send_sem, recv_sem):
        out = []
        for n, (side, src, dst) in enumerate(parts):
            there, came, shift_x, shift_y = sides[side]
            copy = side_copy(src, dst, send_sem.at[n], recv_sem.at[n], shift_x, shift_y)
            out.append((there, came, copy))
        return out

    def start(copies):
        for there, came, copy in copies:
            pl.when(there)(copy.start)

    def came_in(copies):
        for there, came, copy in copies:
            pl.when(came)(copy.wait_recv)

    loads[2].wait()
    loads[3].wait()

    def take_edge(x, carry):
        edge_my[x] = mob_y[x, size_y - 1 : size_y, :]
        edge_f[0, x] = fraction[x, 0:1, :]
        edge_f[1, x] = fraction[x, size_y - 1 : size_y, :]
        return carry

    lax.fori_loop(0, size_x, take_edge, 0)
    early = side_group(
        (
            (1, mob_x.at[size_x - 1], low_mx),
            (3, edge_my, low_my),
            (0, fraction.at[0], halo_fx.at[1]),
            (1, fraction.at[size_x - 1], halo_fx.at[0]),
            (2, edge_f.at[0], halo_fy.at[1]),
            (3, edge_f.at[1], halo_fy.at[0]),
        ),
        early_send_sem,
        early_recv_sem,
    )
    start(early)

    near_row = jnp.concatenate([near_ref[k : k + 1] for k in range(near_ref.shape[0])], axis=1)
    target_row = near_row >> log2(blocks)
    down, across = iota((push_count, push_count), 0), iota((push_count, push_count), 1)
    target_col = jnp.sum(
        jnp.where(down == across, target_row.astype(F32), 0.0), axis=1, keepdims=True
    ).astype(jnp.int32)
    earlier = down < across
    same = jnp.where((target_row == target_col) & earlier, 1, 0)
    rank = jnp.sum(same, axis=0, keepdims=True)
    slot = target_row * SLOT + rank
    chosen = iota((devices * SLOT, push_count), 0) == slot
    local_block = (near_row & (blocks - 1)).astype(F32)
    identity = jnp.sum(jnp.where(chosen, local_block, 0.0), axis=1, keepdims=True)
    link_send[0] = jnp.broadcast_to(identity, (devices * SLOT, 128)).reshape(
        devices, SLOT, 128
    )
    spread = jnp.where(chosen, 1.0, 0.0).astype(BF16)

    def link_exchange(n):
        exchange(link_send.at[n], link_recv.at[n], link_send_sem.at[n], link_recv_sem.at[n])

    link_exchange(0)

    lane = iota((size_y, depth), 1)
    row_of = iota((size_y, depth), 0)

    def below_z(plane):
        return jnp.where(lane == 0, 0.0, pltpu.roll(plane, 1, 1))

    def above_z(plane):
        return jnp.where(lane == depth - 1, 0.0, pltpu.roll(plane, depth - 1, 1))

    def below_y(plane, edge):
        return jnp.where(row_of == 0, edge, pltpu.roll(plane, 1, 0))

    def above_y(plane, edge):
        return jnp.where(row_of == size_y - 1, edge, pltpu.roll(plane, size_y - 1, 0))

    wide = group * size_y
    slot_of = iota((table_rows, 128), 1)
    slot_y = slot_of & (size_y - 1)
    slot_g = (slot_of >> log2(size_y)) & (group - 1)
    slot_k = slot_of >> log2(wide)

    def turn(table, shift):
        return pltpu.roll(table, shift % 128, 1) if shift % 128 else table

    def next_x(table, high):
        inner = turn(table, -size_y)
        outer = turn(jnp.concatenate([table[1:], high], axis=0), (group - 1) * size_y)
        return jnp.where(slot_g < group - 1, inner, outer)

    def last_x(table, low):
        inner = turn(table, size_y)
        outer = turn(
            jnp.concatenate([low, table[: table_rows - 1]], axis=0), -(group - 1) * size_y
        )
        return jnp.where(slot_g > 0, inner, outer)

    def next_y(table, high):
        return jnp.where(slot_y < size_y - 1, turn(table, -1), high)

    def last_y(table, low):
        return jnp.where(slot_y > 0, turn(table, 1), low)

    def next_z(table):
        return jnp.where(slot_k < tiles_z - 1, turn(table, -wide), 0.0)

    def last_z(table):
        return jnp.where(slot_k > 0, turn(table, wide), 0.0)

    write_one_hots(recv_ref, recv_hot, recv_turned)
    loads[5].wait()

    def split_inverse(q, carry):
        inverse_split[q] = stack_two(inverse[q].T)
        return carry

    in_chunks(blocks, split_inverse, 0)
    loads[6].wait()

    def fold_couplings(q, carry):
        both = jnp.concatenate([couplings[q, k] for k in range(couplings.shape[1])], axis=0)
        upper, lower = split_two(both)
        top, rest = inverse_split[q, : inverse.shape[1]], inverse_split[q, inverse.shape[1] :]
        product = lax.dot_general(
            jnp.concatenate([top, rest, top], axis=1),
            jnp.concatenate([upper, upper, lower], axis=1).astype(BF16),
            NT,
            preferred_element_type=F32,
        )
        couplings_split[q] = stack_two(product)
        return carry

    in_chunks(blocks, fold_couplings, 0)

    place = iota((1, 128), 1)

    zero_tile = jnp.zeros((8, 128), F32)
    fields = (local, direction, local_two, zed)

    def keep_edges(phase, x, value):
        edges[phase, 0, x] = value[0:1]
        edges[phase, 1, x] = value[size_y - 1 : size_y]

    def halo_copies(phase):
        field = fields[2 * phase]
        return side_group(
            (
                (0, field.at[0], halo_x.at[2 * phase, 1]),
                (1, field.at[size_x - 1], halo_x.at[2 * phase, 0]),
                (2, edges.at[phase, 0], halo_y.at[2 * phase, 1]),
                (3, edges.at[phase, 1], halo_y.at[2 * phase, 0]),
            ),
            side_send_sem.at[phase],
            side_recv_sem.at[phase],
        )

    def prepare(row, lower, above, total):
        whole, across_x, across_y, across_z = [], [], [], []
        for g in range(group):
            x = row * group + g
            mob_a, mob_b, mob_c = mob_x[x], mob_y[x], mob_z[x]
            weight, source = fraction[x], res[x]
            diagonal = (
                (mob_a + lower) + (mob_b + below_y(mob_b, low_my[x])) + (mob_c + below_z(mob_c))
            )
            inverse_here = 1.0 / diagonal
            value = source * inverse_here
            inv_diag[x] = inverse_here
            local[x] = value
            keep_edges(0, x, value)
            total = total + fold_tiles(source * value)
            up = fraction[x + 1] if g < group - 1 or above is None else above
            whole.append(diagonal * (weight * weight))
            across_x.append(mob_a * weight * up)
            across_y.append(mob_b * weight * above_y(weight, halo_fy[1, x]))
            across_z.append(mob_c * weight * above_z(weight))
            lower = mob_a
        here = pl.ds(row, 1)
        stencil_table[1, here, :] = tile_sums(across_x)
        stencil_table[3, here, :] = tile_sums(across_y)
        turned = jnp.concatenate(
            [p[:, k * TZ : (k + 1) * TZ] for k in range(tiles_z) for p in across_z], axis=0
        ).T
        crossing = turned[TZ - 1 : TZ]
        inside = jnp.sum(turned, axis=0, keepdims=True) - crossing
        stencil_table[5, here, :] = crossing
        stencil_table[0, here, :] = tile_sums(whole) - 2.0 * inside
        return lower, total

    def table_copies(n, pairs):
        return side_group(
            [(side, src, table_halo.at[n, side]) for side, src in pairs],
            table_send_sem.at[n],
            table_recv_sem.at[n],
        )

    def apply_operator(phase, emit):
        field = fields[phase]

        def group_step(row, here, flux_low, carry, top):
            values = []
            for g in range(group):
                x = row * group + g
                above = top if top is not None and g == group - 1 else field[x + 1]
                flux_x = mob_x[x] * (above - here)
                flux_y = mob_y[x] * (above_y(here, halo_y[phase, 1, x]) - here)
                edge = low_my[x] * (here[0:1] - halo_y[phase, 0, x])
                flux_z = mob_z[x] * (above_z(here) - here)
                value = (
                    (flux_low - flux_x)
                    + (below_y(flux_y, edge) - flux_y)
                    + (below_z(flux_z) - flux_z)
                )
                values.append((here, value))
                here, flux_low = above, flux_x
            return here, flux_low, emit(row, values, carry)

        first = field[0]
        flux = low_mx[...] * (first - halo_x[phase, 0])
        state = (first, flux, zero_tile)
        state = in_chunks(table_rows - 1, lambda row, s: group_step(row, *s, None), state, 3)
        return jnp.sum(group_step(table_rows - 1, *state, halo_x[phase, 1])[2])

    def emit_local(n):
        def emit(row, values, total):
            parts = []
            for g, (here, value) in enumerate(values):
                total = total + fold_tiles(here * value)
                parts.append(fraction[row * group + g] * value)
            local_table[n, pl.ds(row, 1), :] = tile_sums(parts)
            return total

        return emit

    def emit_field(result):
        def emit(row, values, total):
            for g, (here, value) in enumerate(values):
                result[row * group + g] = value
            return total

        return emit

    def coarse_totals(phase):
        arrived(row_recv.at[phase], row_recv_sem.at[phase])
        return scatter_rows(
            lambda row: row_recv[phase, row], recv_ref, recv_turned, blocks, NN
        )

    def sweep_first(phase, totals):
        both = block_products(totals, couplings_split)
        pushed = jnp.concatenate(
            [both[:, k * 128 : (k + 1) * 128] for k in range(couplings.shape[1])], axis=0
        )
        upper, lower = split_two(pushed)
        out_values = lax.dot_general(
            spread, upper.astype(BF16), NN, preferred_element_type=F32
        ) + lax.dot_general(spread, lower.astype(BF16), NN, preferred_element_type=F32)
        link_send[1 + phase] = out_values.reshape(devices, SLOT, 128)
        link_exchange(1 + phase)

    def sweep_second(phase, totals, gather_in):
        arrived(link_recv.at[1 + phase], link_recv_sem.at[1 + phase])
        values = stack_two(link_recv[1 + phase].reshape(devices * SLOT, 128), axis=1)
        summed = lax.dot_general(gather_in, values, NN, preferred_element_type=F32)
        coupled = summed[:, :128] + summed[:, 128:]
        sweep_two = block_products(totals - coupled, inverse_split)

        def store(row, value):
            side_send[phase, row + count_y, 0] = value
            side_send[phase, row, 1] = value
            side_send[phase, row + 2 * count_y, 2] = value
            side_send[phase, row + count_y - 1, 3] = value
            side_send[phase, row + count_y + 1, 4] = value

        gather_rows(sweep_two, recv_ref, recv_hot, store)

        def one(step, carry):
            device, other = peer(step)
            pltpu.make_async_remote_copy(
                src_ref=side_send.at[phase, other + count_y],
                dst_ref=side_recv.at[phase, :, me],
                send_sem=spread_send_sem.at[phase],
                recv_sem=spread_recv_sem.at[phase],
                device_id=device,
                device_id_type=MESH,
            ).start()
            return carry

        lax.fori_loop(1, devices, one, 0)
        side_recv[phase, :, me] = side_send[phase, me + count_y]

    def spread_done(phase, sem):
        part = side_recv.at[phase, :, pl.ds(0, devices - 1)]
        pltpu.make_async_copy(part, part, sem).wait()

    def tile_values(phase):
        spread_done(phase, spread_recv_sem.at[phase])

        def store(row, value):
            values_table[phase, pl.ds(row, 1), :] = value

        def rows_of(n):
            return side_recv[phase, n].reshape(devices, 128)

        gather_rows(rows_of(0), back_map, back_hot, store)
        beside = []
        gather_rows(
            jnp.concatenate([rows_of(1 + n) for n in range(4)], axis=0),
            side_map,
            side_hot,
            lambda row, value: beside.append(value),
        )
        packed = jnp.broadcast_to(beside[1], (table_rows, 128))
        high_y = pltpu.roll(packed, size_y - table_rows, 1, stride=1, stride_axis=0)
        low_y = pltpu.roll(packed, 1, 1, stride=1, stride_axis=0)
        beside_table[phase] = jnp.where(slot_y == 0, low_y, high_y)
        beside_row[phase] = beside[0]
        return beside[0], low_y, high_y

    def spread_tiles(row):
        return jnp.broadcast_to(row, (128, 128)).T

    def make_field(phase):
        n = 2 * phase + 1
        field, plus = fields[n], fields[2 * phase]

        def tile_part(stacked, g, first, count):
            return jnp.concatenate(
                [
                    stacked[
                        (k * group + g) * size_y + first : (k * group + g) * size_y + first + count
                    ]
                    for k in range(tiles_z)
                ],
                axis=1,
            )

        def step(row, carry):
            stacked = spread_tiles(values_table[phase, pl.ds(row, 1), :])
            beside = spread_tiles(beside_table[phase, pl.ds(row, 1), :])
            for g in range(group):
                x = row * group + g
                field[x] = fraction[x] * tile_part(stacked, g, 0, size_y) + plus[x]
                for side in range(2):
                    value = tile_part(beside, g, side * (size_y - 1), 1)
                    halo_y[n, side, x] = halo_fy[side, x] * value + halo_y[n - 1, side, x]
            return carry

        in_chunks(table_rows, step, 0)
        stacked = spread_tiles(beside_row[phase])
        for side, g in ((0, group - 1), (1, 0)):
            value = tile_part(stacked, g, 0, size_y)
            halo_x[n, side] = halo_fx[side] * value + halo_x[n - 1, side]

    def tile_operator(phase, beside_x, low_y, high_y):
        table = values_table[phase]
        return (
            stencil_table[0] * table
            - (
                stencil_table[1] * next_x(table, beside_x)
                + stencil_table[2] * last_x(table, beside_x)
            )
            - (
                stencil_table[3] * next_y(table, high_y)
                + stencil_table[4] * last_y(table, low_y)
            )
            - (stencil_table[5] * next_z(table) + stencil_table[6] * last_z(table))
        )

    def start_sums(phase, values):
        row = jnp.zeros((1, 128), F32)
        for n, value in enumerate(values):
            row = jnp.where(place == n, value, row)
        sum_send[phase, 0] = row
        exchange(
            sum_send.at[phase],
            sum_recv.at[phase],
            sum_send_sem.at[phase],
            sum_recv_sem.at[phase],
            same=True,
        )

    def end_sums(phase, count):
        arrived(sum_recv.at[phase], sum_recv_sem.at[phase])
        totals = [sum_recv[phase, n] for n in range(4)]
        for n in range(4, devices):
            totals[n % 4] = totals[n % 4] + sum_recv[phase, n]
        total = (totals[0] + totals[1]) + (totals[2] + totals[3])
        return [
            jnp.sum(jnp.where(place == n, total, 0.0), axis=1, keepdims=True)
            for n in range(count)
        ]

    totals = coarse_totals(0)
    sweep_first(0, totals)

    codes = scatter_rows(
        lambda row: (row * 128 + place).astype(F32), send_map, send_hot, table_rows
    )
    code_table[...] = codes
    back_map[...] = codes.astype(jnp.int32)
    waits = [early, table_copies(1, [(side, code_table) for side in range(4)])]
    start(waits[1])
    loads[4].wait()
    came_in(early)
    lower, total = in_chunks(
        table_rows - 1,
        lambda row, s: prepare(row, s[0], None, s[1]),
        (low_mx[...], zero_tile),
        3,
    )
    _, total = prepare(table_rows - 1, lower, halo_fx[1], total)
    source_local = jnp.sum(total)
    waits.append(halo_copies(0))
    start(waits[2])
    waits.append(table_copies(0, ((1, stencil_table.at[1]), (3, stencil_table.at[3]))))
    start(waits[3])
    arrived(link_recv.at[0], link_recv_sem.at[0])
    names = link_recv[0].reshape(devices * SLOT, 128).T[:blocks]
    gather_in = jnp.where(
        names == iota((blocks, devices * SLOT), 0).astype(F32), 1.0, 0.0
    ).astype(BF16)

    sweep_second(0, totals, gather_in)

    write_one_hots(back_map, back_hot)
    came_in(waits[1])
    across_y, across_g = slot_y[:1], slot_g[:1]
    code_x = jnp.where(
        across_g == 0,
        table_halo[1, 0, 0:1],
        jnp.where(across_g == group - 1, table_halo[1, 1, table_rows - 1 :], -1.0),
    )
    code_y = jnp.full((1, 128), -1.0, F32)
    for r in range(table_rows):
        high = turn(table_halo[1, 2, r : r + 1], table_rows - 1 - r)
        low = turn(table_halo[1, 3, r : r + 1], -size_y - r)
        code_y = jnp.where(across_y == table_rows - 1 - r, high, code_y)
        code_y = jnp.where(across_y == size_y - 1 - r, low, code_y)
    span = devices * 128
    code_x, code_y = code_x.astype(jnp.int32), code_y.astype(jnp.int32)
    shift_x = jnp.where(across_g == 0, 0, span)
    shift_y = jnp.where(across_y < table_rows, 2 * span, 3 * span)
    side_map[0:1] = jnp.where(code_x < 0, -1, code_x + shift_x)
    side_map[1:2] = jnp.where(code_y < 0, -1, code_y + shift_y)
    write_one_hots(side_map, side_hot)
    came_in(waits[3])
    stencil_table[2] = last_x(stencil_table[1], table_halo[0, 1, table_rows - 1 :])
    stencil_table[4] = last_y(stencil_table[3], turn(table_halo[0, 3], 1 - size_y))
    stencil_table[6] = last_z(stencil_table[5])
    came_in(waits[2])
    local_energy = apply_operator(0, emit_local(0))

    beside = tile_values(0)
    operated = tile_operator(0, *beside)
    image_totals = operated + local_table[0]
    totals_table[1] = image_totals
    gather_rows(image_totals, send_map, send_hot, to_owners(1))
    row_exchange(1)
    values = values_table[0]
    rz_part = jnp.sum(totals_table[0] * values) + source_local
    energy_part = jnp.sum(values * (image_totals + local_table[0])) + local_energy
    start_sums(0, (rz_part, energy_part))

    make_field(0)

    rz, energy = end_sums(0, 2)
    alpha = rz / energy
    totals = totals - alpha * coarse_totals(1)
    sweep_first(1, totals)

    apply_operator(1, emit_field(image))

    def update(x, carry):
        own, cross = carry
        pushed = image[x]
        here = res[x] - alpha * pushed
        value = inv_diag[x] * here
        res[x] = here
        local_two[x] = value
        keep_edges(1, x, value)
        return own + fold_tiles(here * value), cross + fold_tiles(value * pushed)

    own, cross = in_chunks(size_x, update, (zero_tile, zero_tile))
    residual_local, cross_local = jnp.sum(own), jnp.sum(cross)
    waits.append(halo_copies(1))
    start(waits[4])

    sweep_second(1, totals, gather_in)

    came_in(waits[4])
    local_energy = apply_operator(2, emit_local(1))

    beside = tile_values(1)
    operated = tile_operator(1, *beside)
    values = values_table[1]
    tile_totals = totals_table[0] - alpha * totals_table[1]
    next_part = jnp.sum(tile_totals * values) + residual_local
    own_part = jnp.sum(values * (operated + 2.0 * local_table[1])) + local_energy
    cross_part = jnp.sum(values * totals_table[1]) + cross_local
    start_sums(1, (next_part, own_part, cross_part))

    make_field(1)
    apply_operator(3, emit_field(image_two))

    rz_next, own, cross = end_sums(1, 3)
    beta = rz_next / rz
    alpha_two = rz_next / (own + beta * (2.0 * cross + beta * energy))

    for ref, value in ((gain_ref, alpha), (gain_two_ref, alpha_two), (mix_ref, beta)):
        ref[...] = jnp.broadcast_to(value, ref.shape)
    for copies in waits:
        for there, came, copy in copies:
            pl.when(there)(copy.wait_send)
    for n in range(2):
        arrived(row_send.at[n], row_send_sem.at[n])
        spread_done(n, spread_send_sem.at[n])
    for n in range(3):
        arrived(link_send.at[n], link_send_sem.at[n])
    for n in range(2):
        arrived(sum_recv.at[n], sum_send_sem.at[n])


def finish(
    direction, zed, res, image_two, image, gain_ref, gain_two_ref, mix_ref, x_hbm, r_hbm, x, r, sem
):
    alpha, alpha_two, beta = gain_ref[...], gain_two_ref[...], mix_ref[...]
    planes = x.shape[0] // CHUNKS
    copies = []
    for n in range(CHUNKS):
        for p in range(n * planes, (n + 1) * planes):
            first = direction[p]
            x[p] = alpha * first + alpha_two * (zed[p] + beta * first)
            r[p] = res[p] - alpha_two * (image_two[p] + beta * image[p])
        part = pl.ds(n * planes, planes)
        for k, (src, dst) in enumerate(((x, x_hbm), (r, r_hbm))):
            copies.append(pltpu.make_async_copy(src.at[part], dst.at[part], sem.at[k, n]))
            copies[-1].start()
    for copy in copies:
        copy.wait()


def body(
    source_term,
    mobility_x,
    mobility_y,
    mobility_z,
    bubble_fraction,
    tile_labels,
    send_tiles,
    recv_rows,
    block_inverse,
    couplings,
    neighbours,
):
    count_x, count_y = lax.axis_size("gx"), lax.axis_size("gy")
    devices = count_x * count_y
    size_x, size_y, depth = source_term.shape
    tiles = size_x * size_y * (depth // TZ)
    blocks, order = block_inverse.shape[:2]
    send, recv = send_tiles[0], recv_rows[0]
    pad = 128 - send.shape[1]
    assert order == 128 and pad >= 0
    if pad:
        send = jnp.pad(send, ((0, 0), (0, pad)), constant_values=tiles)
        recv = jnp.pad(recv, ((0, 0), (0, pad)), constant_values=blocks * order)
    table_rows = tiles // 128
    field = (size_x, size_y, depth)
    hbm = pl.BlockSpec(memory_space=pltpu.HBM)
    vmem = pl.BlockSpec(memory_space=pltpu.VMEM)
    dma = pltpu.SemaphoreType.DMA
    res, direction, zed, image, image_two, *gains = pl.pallas_call(
        functools.partial(kernel, (count_x, count_y)),
        out_shape=(*[pltpu.VMEM(field, F32)] * 5, *[pltpu.VMEM((1, depth), F32)] * 3),
        in_specs=[hbm] * 7 + [vmem] * 3,
        out_specs=(vmem,) * 8,
        scratch_shapes=[
            *[pltpu.VMEM(field, F32)] * 4,
            pltpu.VMEM((blocks, order, order), F32),
            pltpu.VMEM(couplings.shape, F32),
            *[pltpu.VMEM(field, F32)] * 3,
            pltpu.VMEM((blocks, 2 * order, order), BF16),
            pltpu.VMEM((blocks, 2 * order, order * couplings.shape[1]), BF16),
            pltpu.VMEM((devices // GROUP, 128, GROUP * 128), BF16),
            pltpu.VMEM((devices // GROUP, 128, GROUP * 128), BF16),
            pltpu.VMEM((devices // GROUP, GROUP * 128, 128), BF16),
            pltpu.VMEM((table_rows // GROUP, 128, GROUP * 128), BF16),
            pltpu.VMEM((1, 128, 2 * 128), BF16),
            pltpu.VMEM((devices, 128), jnp.int32),
            pltpu.VMEM((table_rows, 128), jnp.int32),
            pltpu.VMEM((2, 128), jnp.int32),
            pltpu.VMEM((2, table_rows, 128), F32),
            pltpu.VMEM((2, table_rows, 128), F32),
            pltpu.VMEM((2, table_rows, 128), F32),
            pltpu.VMEM((7, table_rows, 128), F32),
            pltpu.VMEM((table_rows, 128), F32),
            pltpu.VMEM((2, table_rows, 128), F32),
            pltpu.VMEM((2, 1, 128), F32),
            pltpu.VMEM((2, 4, table_rows, 128), F32),
            pltpu.VMEM((size_y, depth), F32),
            pltpu.VMEM((size_x, 1, depth), F32),
            pltpu.VMEM((size_x, 1, depth), F32),
            pltpu.VMEM((2, size_x, 1, depth), F32),
            pltpu.VMEM((2, size_y, depth), F32),
            pltpu.VMEM((2, size_x, 1, depth), F32),
            pltpu.VMEM((2, 2, size_x, 1, depth), F32),
            pltpu.VMEM((4, 2, size_y, depth), F32),
            pltpu.VMEM((4, 2, size_x, 1, depth), F32),
            pltpu.VMEM((2, devices, 1, 128), F32),
            pltpu.VMEM((2, devices, 1, 128), F32),
            pltpu.VMEM((2, devices + 2 * count_y, 5, 1, 128), F32),
            pltpu.VMEM((2, 5, devices, 1, 128), F32),
            pltpu.VMEM((3, devices, SLOT, 128), F32),
            pltpu.VMEM((3, devices, SLOT, 128), F32),
            pltpu.VMEM((2, 1, 1, 128), F32),
            pltpu.VMEM((2, devices, 1, 128), F32),
            dma((7,)),
            dma((2, 4)),
            dma((2, 4)),
            dma((6,)),
            dma((6,)),
            dma((2, 4)),
            dma((2, 4)),
            dma((2,)),
            dma((2,)),
            dma((2,)),
            dma((2,)),
            dma((3,)),
            dma((3,)),
            dma((2,)),
            dma((2,)),
        ],
        compiler_params=pltpu.CompilerParams(
            collective_id=0, has_side_effects=True, vmem_limit_bytes=61000000
        ),
    )(
        source_term,
        mobility_x,
        mobility_y,
        mobility_z,
        bubble_fraction,
        block_inverse,
        couplings,
        send,
        recv,
        neighbours.T,
    )
    return tuple(
        pl.pallas_call(
            finish,
            out_shape=(jax.ShapeDtypeStruct(field, F32), jax.ShapeDtypeStruct(field, F32)),
            in_specs=[vmem] * 8,
            out_specs=(hbm, hbm),
            scratch_shapes=[
                pltpu.VMEM(field, F32),
                pltpu.VMEM(field, F32),
                dma((2, CHUNKS)),
            ],
            compiler_params=pltpu.CompilerParams(vmem_limit_bytes=50000000),
        )(direction, zed, res, image_two, image, *gains)
    )


def solution(mesh):
    return jax.shard_map(
        body,
        mesh=mesh,
        in_specs=(
            P("gx", "gy", None),
            P("gx", "gy", None),
            P("gx", "gy", None),
            P("gx", "gy", None),
            P("gx", "gy", None),
            P("gx", "gy", None),
            P(("gx", "gy"), None, None),
            P(("gx", "gy"), None, None),
            P(("gx", "gy"), None, None),
            P(("gx", "gy"), None, None, None),
            P(("gx", "gy"), None),
        ),
        out_specs=(P("gx", "gy", None), P("gx", "gy", None)),
        check_vma=False,
    )
```
